32 devices in a mesh: row: 4 (over y, core), col: 8 (over z, x).
Axes of the slice: x: 2, y: 2, z: 4, core: 2. Of those that a mesh axis runs over, the one named last changes fastest.
Arguments:
- hidden_in: float32 [1280, 8192], P('col', 'row'), may hold values from -6 to 6
- lengths: int32 [8], replicated, may hold values from 256 to 1024, as said below
- ln1_gain: float32 [1280], P('col'), may hold values from 0.25 to 1.75
- ln1_shift: float32 [1280], P('col'), may hold values from -1.5 to 1.5
- qkv_weight: bfloat16 [3, 1280, 1280], P(None, 'row', 'col'), may hold values from -0.21875 to 0.21875
- qv_bias: float32 [2, 1280], P(None, 'col'), may hold values from -2.5 to 2.5
- out_weight: bfloat16 [1280, 1280], P('col', 'row'), may hold values from -1.25 to 1.25
- out_bias: float32 [1280], P('col'), may hold values from -1.5 to 1.5
- ln2_gain: float32 [1280], P('col'), may hold values from 0.25 to 1.75
- ln2_shift: float32 [1280], P('col'), may hold values from -1.5 to 1.5
- in_weight: bfloat16 [1280, 5120], P('row', 'col'), may hold values from -0.15625 to 0.15625
- in_bias: float32 [5120], P('col'), may hold values from -2.5 to 2.5
- down_weight: bfloat16 [5120, 1280], P('col', 'row'), may hold values from -0.078125 to 0.078125
- down_bias: float32 [1280], P('col'), may hold values from -1.5 to 1.5
- cotangent: float32 [1280, 8192], P('col', 'row'), may hold values from -6 to 6
Outputs:
- hidden_out: float32 [1280, 8192], P('col', 'row')
- hidden_grad: float32 [1280, 8192], P('col', 'row')
- ln1_gain_grad: float32 [1280], P('col')
- ln1_shift_grad: float32 [1280], P('col')
- qkv_weight_grad: float32 [3, 1280, 1280], P(None, 'row', 'col')
- qv_bias_grad: float32 [2, 1280], P(None, 'col')
- out_weight_grad: float32 [1280, 1280], P('col', 'row')
- out_bias_grad: float32 [1280], P('col')
- ln2_gain_grad: float32 [1280], P('col')
- ln2_shift_grad: float32 [1280], P('col')
- in_weight_grad: float32 [1280, 5120], P('row', 'col')
- in_bias_grad: float32 [5120], P('col')
- down_weight_grad: float32 [5120, 1280], P('col', 'row')
- down_bias_grad: float32 [1280], P('col')
The draws below stay inside these ranges and needn't reach their ends.
Inputs may be any that keep to these rules, and one draw needn't show every extreme that they name: lengths[c] is the number of valid tokens at the start of clip c; later positions of the clip are padding.
All inputs are finite; a program needn't handle non-finite values.
Results may differ from the reference program's by a relative error of at most 0.012.
The reference program's roundings to bfloat16 on the way count: a program that leaves them out, or rounds other values in their place, can miss the bound.
Values may be sent and summed in bfloat16 or wider, within the bound.
No kernel may reach another device: no remote copies, remote signals or barrier semaphores. Data moves between devices by JAX's collectives and lax.ppermute only.
A program may use at most 320 MiB of HBM per device.

```python
import jax
import jax.numpy as jnp
from jax import lax

HEADS = 16
HEAD_DIM = 80
D = 1280
FF = 5120
CLIP = 1024
CLIPS = 8
TOKENS = 8192


def draw_lengths(key, part):
    base_key = jax.random.fold_in(key, 11)
    long_key = jax.random.fold_in(key, 12)
    short_key = jax.random.fold_in(key, 13)
    drawn_len = jax.random.randint(base_key, (CLIPS,), CLIP // 4, CLIP + 1, dtype=jnp.int32)
    long_spot = jax.random.randint(long_key, (), 0, CLIPS, dtype=jnp.int32)
    short_spot = (long_spot + 1 + jax.random.randint(short_key, (), 0, CLIPS - 1, dtype=jnp.int32)) % CLIPS
    clip_ids = jnp.arange(CLIPS, dtype=jnp.int32)
    drawn_len = jnp.where(clip_ids == long_spot, CLIP, drawn_len)
    drawn_len = jnp.where(clip_ids == short_spot, CLIP // 4, drawn_len)
    return drawn_len.astype(jnp.int32)


def block_levels(stream_key, extent, cuts, low, largest):
    loudness = 1.0
    for axis_at, blocks in cuts:
        steps = jax.random.uniform(jax.random.fold_in(jax.random.fold_in(stream_key, 6), axis_at), (blocks,), jnp.float32, low / len(cuts), largest / len(cuts))
        loudness = loudness * jnp.repeat(jnp.exp(steps), extent[axis_at] // blocks).reshape((-1,) + (1,) * (len(extent) - 1 - axis_at))
    return loudness


def centred(stream_key, dims, scale, bound, shards=(), kind=jnp.bfloat16):
    array = scale * jax.random.normal(stream_key, dims, jnp.float32)
    if shards:
        array = array * block_levels(stream_key, dims, shards, -0.22, 0.18)
    return jnp.clip(array, -bound, bound).astype(kind)


def setup_inputs(seed: int = 0) -> dict:
    key_of = jax.random.split(jax.random.key(seed), 16)
    return {
        "hidden_in": centred(key_of[0], (D, TOKENS), 1.0, 6.0, ((0, 8), (1, 4)), jnp.float32),
        "lengths": draw_lengths(jax.random.fold_in(key_of[15], 71), 0),
        "ln1_gain": jnp.clip(1.0 + 0.15 * jax.random.normal(key_of[2], (D,), jnp.float32), 0.25, 1.75),
        "ln1_shift": centred(key_of[3], (D,), 0.3, 1.5, ((0, 8),), jnp.float32),
        "qkv_weight": centred(key_of[4], (3, D, D), (D * 2 // 3) ** -0.5, 0.21875, ((1, 4), (2, 8))),
        "qv_bias": centred(key_of[5], (2, D), 0.5, 2.5, ((1, 8),), jnp.float32),
        "out_weight": centred(key_of[6], (D, D), (D // 64) ** -0.5, 1.25, ((0, 8), (1, 4))),
        "out_bias": centred(key_of[7], (D,), 0.3, 1.5, ((0, 8),), jnp.float32),
        "ln2_gain": jnp.clip(1.0 + 0.15 * jax.random.normal(key_of[8], (D,), jnp.float32), 0.25, 1.75),
        "ln2_shift": centred(key_of[9], (D,), 0.3, 1.5, ((0, 8),), jnp.float32),
        "in_weight": centred(key_of[10], (D, FF), D ** -0.5, 0.15625, ((0, 4), (1, 8))),
        "in_bias": centred(key_of[11], (FF,), 0.5, 2.5, ((0, 8),), jnp.float32),
        "down_weight": centred(key_of[12], (FF, D), FF ** -0.5, 0.078125, ((0, 8), (1, 4))),
        "down_bias": centred(key_of[13], (D,), 0.3, 1.5, ((0, 8),), jnp.float32),
        "cotangent": centred(key_of[14], (D, TOKENS), 1.0, 6.0, ((0, 8), (1, 4)), jnp.float32),
    }


@jax.custom_vjp
def low(v):
    return lax.optimization_barrier(v.astype(jnp.bfloat16)).astype(jnp.float32)

@jax.custom_vjp
def low_back(v):
    return v

def low_keep(v):
    return (low(v), None)

def low_pass(kept, grad):
    return (grad,)

def back_keep(v):
    return (v, None)

def back_low(kept, grad):
    return (low(grad),)
low.defvjp(low_keep, low_pass)
low_back.defvjp(back_keep, back_low)
EPS = 1e-05
HIGH = lax.Precision.HIGHEST

def layer_norm(values, norm_gain, norm_shift):
    mean_rows = lax.optimization_barrier(jnp.mean(values, axis=-1, keepdims=True))
    centered = values - mean_rows
    var_rows = lax.optimization_barrier(jnp.mean(centered * centered, axis=-1, keepdims=True))
    return centered * lax.rsqrt(var_rows + EPS) * norm_gain + norm_shift

def project(values, matrix):
    return jnp.einsum('ctd,de->cte', values, matrix, precision=HIGH)

def pack_forward(params, clip_rows, clip_lengths):
    gain_one, shift_one, qkv_full, qv_full, out_full, out_shift, gain_two, shift_two, in_full, in_shift, down_full, down_shift = params
    pack_count, clip_len = (clip_rows.shape[0], clip_rows.shape[1])
    ln_one = low(layer_norm(clip_rows, gain_one, shift_one))
    queries = low(low_back(project(ln_one, qkv_full[0]) + qv_full[0]))
    key_rows = low(low_back(project(ln_one, qkv_full[1])))
    value_rows = low(low_back(project(ln_one, qkv_full[2]) + qv_full[1]))
    head_shape = (pack_count, clip_len, HEADS, HEAD_DIM)
    scores = jnp.einsum('cqhe,ckhe->chqk', queries.reshape(head_shape), key_rows.reshape(head_shape), precision=HIGH) * HEAD_DIM ** (-0.5)
    scores = low_back(scores)
    live_keys = jnp.arange(clip_len, dtype=jnp.int32)[None, :] < clip_lengths[:, None]
    scores = jnp.where(live_keys[:, None, None, :], scores, -1e+30)
    prob_low = low(jax.nn.softmax(scores, axis=-1))
    attended = jnp.einsum('chqk,ckhe->cqhe', prob_low, value_rows.reshape(head_shape), precision=HIGH)
    attended = low(low_back(attended.reshape(pack_count, clip_len, D)))
    hidden_mid = clip_rows + low_back(project(attended, out_full)) + out_shift
    ln_two = low(layer_norm(hidden_mid, gain_two, shift_two))
    pre_act = low_back(project(ln_two, in_full) + in_shift)
    act_low = low(jax.nn.gelu(pre_act, approximate=False))
    return hidden_mid + low_back(project(act_low, down_full)) + down_shift

def reference(hidden_in, lengths, ln1_gain, ln1_shift, qkv_weight, qv_bias, out_weight, out_bias, ln2_gain, ln2_shift, in_weight, in_bias, down_weight, down_bias, cotangent):
    params = (ln1_gain, ln1_shift, qkv_weight.astype(jnp.float32), qv_bias, out_weight.astype(jnp.float32), out_bias, ln2_gain, ln2_shift, in_weight.astype(jnp.float32), in_bias, down_weight.astype(jnp.float32), down_bias)
    pack_size = 2
    token_rows = jnp.transpose(hidden_in)
    cot_rows = jnp.transpose(cotangent)

    def layer_all(inputs, weights):
        clip_rows = inputs.reshape(CLIPS // pack_size, pack_size, CLIP, D)
        length_pack = lengths.reshape(CLIPS // pack_size, pack_size)

        def one_pack(pack_pair):
            return pack_forward(weights, pack_pair[0], pack_pair[1])
        outputs = lax.map(jax.checkpoint(one_pack), (clip_rows, length_pack))
        return outputs.reshape(TOKENS, D)
    hidden_out, pullback = jax.vjp(layer_all, token_rows, params)
    hidden_grad, weight_grads = pullback(cot_rows)
    g_one, s_one, g_qkv, g_qv, g_out, g_outb, g_two, s_two, g_in, g_inb, g_down, g_downb = weight_grads
    return (jnp.transpose(hidden_out), jnp.transpose(hidden_grad), g_one, s_one, g_qkv, g_qv, g_out, g_outb, g_two, s_two, g_in, g_inb, g_down, g_downb)
```

```python
import functools

import jax
import jax.numpy as jnp
from jax import lax
from jax.experimental import pallas as pl
from jax.experimental.pallas import tpu as pltpu
from jax.sharding import PartitionSpec as P

HEADS = 16
HEAD_DIM = 80
D = 1280
MICRO = 2
GROUP = 8


EPS = 1e-05


def partner(block, axis, distance):
    count = lax.axis_size(axis)
    route = []
    for low in range(count):
        high = low | 1 << distance
        if high != low and high < count:
            route += [(low, high), (high, low)]
    return lax.ppermute(block, axis, route)


def row_totals(first_sum, second_sum):
    return lax.psum((first_sum, second_sum), "col")


def widen(values):
    return lax.all_gather(values, "col", axis=1, tiled=True)


def narrow(values):
    return lax.psum_scatter(values, "col", scatter_dimension=1, tiled=True)


def to_clips(stacked):
    return lax.all_to_all(stacked, "col", split_axis=1, concat_axis=2, tiled=True)


def to_columns(stacked):
    return lax.all_to_all(stacked, "col", split_axis=2, concat_axis=1, tiled=True)


def contract_rows(left, right):
    return lax.dot_general(
        left, right, (((0,), (0,)), ((), ())), preferred_element_type=jnp.float32
    )


def contract_cols(left, right):
    return lax.dot_general(
        left, right, (((1,), (1,)), ((), ())), preferred_element_type=jnp.float32
    )


def exact_gelu(values):
    return jax.nn.gelu(values, approximate=False)


def norm_forward(values, norm_gain, norm_shift):
    first_sum, second_sum = row_totals(jnp.sum(values, axis=1), jnp.sum(values * values, axis=1))
    mean_rows = first_sum / D
    inv_std = lax.rsqrt(second_sum / D - mean_rows * mean_rows + EPS)
    normed = (values - mean_rows[:, None]) * inv_std[:, None]
    return (normed, inv_std, normed * norm_gain + norm_shift)


def norm_backward(grad_out, normed, inv_std, norm_gain):
    scaled = grad_out * norm_gain
    first_sum, second_sum = row_totals(jnp.sum(scaled, axis=1), jnp.sum(scaled * normed, axis=1))
    grad_input = inv_std[:, None] * (
        scaled - first_sum[:, None] / D - normed * (second_sum[:, None] / D)
    )
    return (grad_input, jnp.sum(grad_out * normed, axis=0), jnp.sum(grad_out, axis=0))


def split_heads(values):
    return values.reshape(values.shape[0], HEADS, HEAD_DIM)


def gather_clip(key_rows, value_rows):
    position = lax.axis_index("col")
    for bit_index in range(GROUP.bit_length() - 1):
        other_keys, other_values = partner((key_rows, value_rows), "col", bit_index)
        upper_half = position >> bit_index & 1 == 1
        key_rows = jnp.where(
            upper_half,
            jnp.concatenate([other_keys, key_rows]),
            jnp.concatenate([key_rows, other_keys]),
        )
        value_rows = jnp.where(
            upper_half,
            jnp.concatenate([other_values, value_rows]),
            jnp.concatenate([value_rows, other_values]),
        )
    return (key_rows, value_rows)


def scatter_clip(grad_keys, grad_values):
    position = lax.axis_index("col")
    for bit_index in reversed(range(GROUP.bit_length() - 1)):
        half_rows = grad_keys.shape[0] // 2
        upper_half = position >> bit_index & 1 == 1
        keep_keys = jnp.where(upper_half, grad_keys[half_rows:], grad_keys[:half_rows])
        send_keys = jnp.where(upper_half, grad_keys[:half_rows], grad_keys[half_rows:])
        keep_values = jnp.where(upper_half, grad_values[half_rows:], grad_values[:half_rows])
        send_values = jnp.where(upper_half, grad_values[:half_rows], grad_values[half_rows:])
        got_keys, got_values = partner((send_keys, send_values), "col", bit_index)
        grad_keys = keep_keys + got_keys
        grad_values = keep_values + got_values
    return (grad_keys, grad_values)


def clip_scores(queries, key_rows, valid_len):
    scale_factor = HEAD_DIM ** (-0.5)
    scores = (
        jnp.einsum(
            "qhe,khe->hqk",
            split_heads(queries),
            split_heads(key_rows),
            preferred_element_type=jnp.float32,
        )
        * scale_factor
    )
    live_keys = lax.broadcasted_iota(jnp.int32, (1, 1, key_rows.shape[0]), 2) < valid_len
    return jnp.where(live_keys, scores, -1e30)


def attend(queries, key_rows, value_rows, valid_len):
    scores = clip_scores(queries, key_rows, valid_len)
    top_score = jnp.max(scores, axis=2, keepdims=True)
    weights = jnp.exp(scores - top_score)
    weight_sum = jnp.sum(weights, axis=2, keepdims=True)
    prob_low = (weights / weight_sum).astype(jnp.bfloat16)
    attended = jnp.einsum(
        "hqk,khe->qhe", prob_low, split_heads(value_rows), preferred_element_type=jnp.float32
    )
    return (attended.reshape(queries.shape[0], -1), top_score + jnp.log(weight_sum))


def attend_back(queries, key_rows, value_rows, valid_len, log_sum, grad_low):
    scale_factor = HEAD_DIM ** (-0.5)
    scores = clip_scores(queries, key_rows, valid_len)
    probs_full = jnp.exp(scores - log_sum)
    grad_heads = split_heads(grad_low)
    grad_value = jnp.einsum(
        "hqk,qhe->khe",
        probs_full.astype(jnp.bfloat16),
        grad_heads,
        preferred_element_type=jnp.float32,
    )
    grad_probs = jnp.einsum(
        "qhe,khe->hqk", grad_heads, split_heads(value_rows), preferred_element_type=jnp.float32
    )
    row_dot = jnp.sum(probs_full * grad_probs, axis=2, keepdims=True)
    grad_scores = (probs_full * (grad_probs - row_dot)).astype(jnp.bfloat16)
    grad_query = (
        jnp.einsum(
            "hqk,khe->qhe", grad_scores, split_heads(key_rows), preferred_element_type=jnp.float32
        )
        * scale_factor
    )
    grad_key = (
        jnp.einsum(
            "hqk,qhe->khe", grad_scores, split_heads(queries), preferred_element_type=jnp.float32
        )
        * scale_factor
    )
    return (
        grad_query.reshape(queries.shape[0], -1),
        grad_key.reshape(key_rows.shape[0], -1),
        grad_value.reshape(key_rows.shape[0], -1),
    )


def layer_pass(input_rows, grad_rows, weights, vectors, valid_len):
    qkv_full, out_full, in_full, down_full = weights
    gain_one, shift_one, qv_full, out_shift, gain_two, shift_two, in_shift, down_shift = vectors
    bias_three = jnp.stack([qv_full[0], jnp.zeros_like(qv_full[0]), qv_full[1]])[:, None, :]
    normed_one, inv_one, ln_one = norm_forward(input_rows, gain_one, shift_one)
    wide_one = widen(ln_one.astype(jnp.bfloat16))
    projected = (
        jnp.einsum("td,sdc->stc", wide_one, qkv_full, preferred_element_type=jnp.float32)
        + bias_three
    )
    projected = to_clips(projected.astype(jnp.bfloat16))
    key_rows, value_rows = gather_clip(projected[1], projected[2])
    attended, log_sum = attend(projected[0], key_rows, value_rows, valid_len)
    attended_low = to_columns(attended.astype(jnp.bfloat16)[None])[0]
    hidden_mid = (
        input_rows
        + narrow(jnp.dot(attended_low, out_full, preferred_element_type=jnp.float32))
        + out_shift
    )
    normed_two, inv_two, ln_two = norm_forward(hidden_mid, gain_two, shift_two)
    wide_two = widen(ln_two.astype(jnp.bfloat16))
    pre_act = jnp.dot(wide_two, in_full, preferred_element_type=jnp.float32) + in_shift
    act_value, gelu_back = jax.vjp(exact_gelu, pre_act)
    act_low = act_value.astype(jnp.bfloat16)
    hidden_out = (
        hidden_mid
        + narrow(jnp.dot(act_low, down_full, preferred_element_type=jnp.float32))
        + down_shift
    )
    grad_wide = widen(grad_rows.astype(jnp.bfloat16))
    grad_down = contract_rows(act_low, grad_wide)
    grad_pre = gelu_back(contract_cols(grad_wide, down_full))[0].astype(jnp.bfloat16)
    grad_in = contract_rows(wide_two, grad_pre)
    grad_ln_two = narrow(contract_cols(grad_pre, in_full))
    grad_norm_two, grad_gain_two, grad_shift_two = norm_backward(
        grad_ln_two, normed_two, inv_two, gain_two
    )
    grad_mid = grad_rows + grad_norm_two
    grad_mid_wide = widen(grad_mid.astype(jnp.bfloat16))
    grad_out = contract_rows(attended_low, grad_mid_wide)
    grad_attended = to_clips(contract_cols(grad_mid_wide, out_full).astype(jnp.bfloat16)[None])[0]
    grad_query, grad_key, grad_value = attend_back(
        projected[0], key_rows, value_rows, valid_len, log_sum, grad_attended
    )
    grad_key, grad_value = scatter_clip(grad_key, grad_value)
    grad_proj = to_columns(jnp.stack([grad_query, grad_key, grad_value]).astype(jnp.bfloat16))
    grad_qkv = jnp.einsum("td,stc->sdc", wide_one, grad_proj, preferred_element_type=jnp.float32)
    grad_ln_one = narrow(
        jnp.einsum("stc,sdc->td", grad_proj, qkv_full, preferred_element_type=jnp.float32)
    )
    grad_norm_one, grad_gain_one, grad_shift_one = norm_backward(
        grad_ln_one, normed_one, inv_one, gain_one
    )
    grad_input = grad_mid + grad_norm_one
    proj_sums = jnp.sum(grad_proj, axis=1, dtype=jnp.float32)
    vector_parts = (
        grad_gain_one,
        grad_shift_one,
        jnp.stack([proj_sums[0], proj_sums[2]]),
        jnp.sum(grad_mid, axis=0),
        grad_gain_two,
        grad_shift_two,
        jnp.sum(grad_pre, axis=0, dtype=jnp.float32),
        jnp.sum(grad_rows, axis=0),
    )
    return (hidden_out, grad_input, (grad_qkv, grad_out, grad_in, grad_down), vector_parts)


def tile_grid(vector, row_count):
    return jnp.broadcast_to(vector[None], (row_count,) + vector.shape)


def grid_reduce(partials, vector_parts):
    row_count = lax.axis_size("row")
    qkv_part, out_part, in_part, down_part = partials
    qkv_blocks = qkv_part.reshape(3, row_count, -1, qkv_part.shape[2]).transpose(1, 0, 2, 3)
    out_blocks = out_part.reshape(out_part.shape[0], row_count, -1).transpose(1, 0, 2)
    in_blocks = in_part.reshape(row_count, -1, in_part.shape[1])
    down_blocks = down_part.reshape(down_part.shape[0], row_count, -1).transpose(1, 0, 2)
    tiled = [tile_grid(vector, row_count) for vector in vector_parts]
    reduced = (
        lax.psum_scatter(qkv_blocks, "row", scatter_dimension=0, tiled=True),
        lax.psum_scatter(out_blocks, "row", scatter_dimension=0, tiled=True),
        lax.psum_scatter(in_blocks, "row", scatter_dimension=0, tiled=True),
        lax.psum_scatter(down_blocks, "row", scatter_dimension=0, tiled=True),
        lax.psum_scatter(tiled[0], "row", scatter_dimension=0, tiled=True),
        lax.psum_scatter(tiled[1], "row", scatter_dimension=0, tiled=True),
        lax.psum_scatter(tiled[2], "row", scatter_dimension=0, tiled=True),
        lax.psum_scatter(tiled[3], "row", scatter_dimension=0, tiled=True),
        lax.psum_scatter(tiled[4], "row", scatter_dimension=0, tiled=True),
        lax.psum_scatter(tiled[5], "row", scatter_dimension=0, tiled=True),
        lax.psum_scatter(tiled[6], "row", scatter_dimension=0, tiled=True),
        lax.psum_scatter(tiled[7], "row", scatter_dimension=0, tiled=True),
    )
    return tuple((piece[0] for piece in reduced))


def local(
    hidden_in,
    lengths,
    ln1_gain,
    ln1_shift,
    qkv_weight,
    qv_bias,
    out_weight,
    out_bias,
    ln2_gain,
    ln2_shift,
    in_weight,
    in_bias,
    down_weight,
    down_bias,
    cotangent,
):
    col_count = lax.axis_size("col")
    token_rows = jnp.transpose(hidden_in)
    cot_rows = jnp.transpose(cotangent)
    rows_block = token_rows.shape[0] // MICRO
    weights = (
        lax.all_gather(qkv_weight, "row", axis=1, tiled=True),
        lax.all_gather(out_weight, "row", axis=1, tiled=True),
        lax.all_gather(in_weight, "row", axis=0, tiled=True),
        lax.all_gather(down_weight, "row", axis=1, tiled=True),
    )
    vectors = (ln1_gain, ln1_shift, qv_bias, out_bias, ln2_gain, ln2_shift, in_bias, down_bias)
    clip_slot = lax.axis_index("col") // GROUP
    outputs = []
    input_grads = []
    totals = None
    running = None
    for micro_index in range(MICRO):
        input_rows = token_rows[micro_index * rows_block : (micro_index + 1) * rows_block]
        grad_rows = cot_rows[micro_index * rows_block : (micro_index + 1) * rows_block]
        clip_id = (lax.axis_index("row") * MICRO + micro_index) * (col_count // GROUP) + clip_slot
        valid_len = lax.dynamic_index_in_dim(lengths, clip_id, keepdims=False)
        out_rows, back_rows, partials, vector_parts = layer_pass(
            input_rows, grad_rows, weights, vectors, valid_len
        )
        outputs.append(out_rows)
        input_grads.append(back_rows)
        current = (partials, vector_parts)
        running = current if running is None else jax.tree.map(jnp.add, running, current)
    totals = grid_reduce(running[0], running[1])
    (
        grad_qkv,
        grad_out,
        grad_in,
        grad_down,
        grad_gain_one,
        grad_shift_one,
        grad_qv,
        grad_out_shift,
        grad_gain_two,
        grad_shift_two,
        grad_in_shift,
        grad_down_shift,
    ) = totals
    hidden_out = jnp.transpose(jnp.concatenate(outputs, axis=0))
    hidden_grad = jnp.transpose(jnp.concatenate(input_grads, axis=0))
    return (
        hidden_out,
        hidden_grad,
        grad_gain_one,
        grad_shift_one,
        grad_qkv,
        grad_qv,
        grad_out,
        grad_out_shift,
        grad_gain_two,
        grad_shift_two,
        grad_in,
        grad_in_shift,
        grad_down,
        grad_down_shift,
    )


CLIP = 1024
FF = 5120
OWN = D // 4
UNITS = FF // 4
HALF = D // 2
BLOCK = 256
STEPS = CLIP // BLOCK
BF = jnp.bfloat16
F32 = jnp.float32


def swap_core(values):
    return lax.ppermute(values, "row", [(i, i ^ 1) for i in range(4)])


def swap_y(values):
    return lax.ppermute(values, "row", [(i, i ^ 2) for i in range(4)])


def swap_x(values):
    return lax.ppermute(values, "col", [(i, i ^ 1) for i in range(8)])


def swap_zl(values):
    return lax.ppermute(values, "col", [(i, i ^ 2) for i in range(8)])


def swap_zh(values):
    return lax.ppermute(values, "col", [(i, i ^ 4) for i in range(8)])


def pick(values, index, axis=0):
    return lax.dynamic_index_in_dim(values, index, axis, keepdims=False)


def mm(left, right, left_dim, right_dim):
    return lax.dot_general(
        left, right, (((left_dim,), (right_dim,)), ((), ())), preferred_element_type=F32
    )


def shaped(dims, kind=BF):
    return jax.ShapeDtypeStruct(dims, kind)


def spots_spec():
    return pl.BlockSpec(memory_space=pltpu.SMEM)


def fixed(array):
    rank = len(array.shape)
    return pl.BlockSpec(array.shape, lambda i: (0,) * rank)


def tokens_spec(dims):
    lead = tuple(dims[:-1])
    return pl.BlockSpec(lead + (BLOCK,), lambda i: (0,) * len(lead) + (i,))


def cost(flops, moved):
    return pl.CostEstimate(flops=1, transcendentals=0, bytes_accessed=1)


def attend_kernel(len_ref, q_ref, k_ref, v_ref, out_ref, lse_ref):
    scores = mm(k_ref[...], q_ref[...], 0, 0) * (HEAD_DIM**-0.5)
    live = lax.broadcasted_iota(jnp.int32, scores.shape, 0) < len_ref[0]
    scores = jnp.where(live, scores, -1e30)
    top = jnp.max(scores, axis=0, keepdims=True)
    weights = jnp.exp(scores - top)
    total = jnp.sum(weights, axis=0, keepdims=True)
    prob_low = (weights * (1.0 / total)).astype(BF)
    out_ref[...] = mm(v_ref[...], prob_low, 1, 0).astype(BF)
    lse_ref[...] = top + jnp.log(total)


def head_specs(block):
    return [
        pl.BlockSpec((None, None, HEAD_DIM, block), lambda h, i, n: (h, 0, 0, i)),
        pl.BlockSpec((None, None, HEAD_DIM, CLIP), lambda h, i, n: (h, 1, 0, 0)),
        pl.BlockSpec((None, HEAD_DIM, CLIP), lambda h, i, n: (h, 0, 0)),
    ]


def attend_clip(qk, values, clip_len, block):
    return pl.pallas_call(
        attend_kernel,
        grid_spec=pltpu.PrefetchScalarGridSpec(
            num_scalar_prefetch=1,
            grid=(4, CLIP // block),
            in_specs=head_specs(block),
            out_specs=[
                pl.BlockSpec((None, HEAD_DIM, block), lambda h, i, n: (h, 0, i)),
                pl.BlockSpec((None, 1, block), lambda h, i, n: (h, 0, i)),
            ],
        ),
        out_shape=[shaped((4, HEAD_DIM, CLIP)), shaped((4, 1, CLIP), F32)],
        cost_estimate=cost(16 * CLIP * CLIP * HEAD_DIM, 16 * HEAD_DIM * CLIP * 2),
        name="attend_clip",
    )(clip_len, qk, qk, values)


def attend_back_kernel(
    len_ref, q_ref, k_ref, v_ref, lse_ref, grad_ref, gqk_ref, gv_ref, ksum_ref, vsum_ref
):
    step = pl.program_id(1)
    scale = HEAD_DIM**-0.5
    queries, keys, values, grad = q_ref[...], k_ref[...], v_ref[...], grad_ref[...]
    block = queries.shape[1]
    scores = mm(keys, queries, 0, 0) * scale
    live = lax.broadcasted_iota(jnp.int32, scores.shape, 0) < len_ref[0]
    scores = jnp.where(live, scores, -1e30)
    probs = jnp.exp(scores - lse_ref[...])
    grad_probs = mm(values, grad, 0, 0)
    row_dot = jnp.sum(probs * grad_probs, axis=0, keepdims=True)
    score_low = (probs * (grad_probs - row_dot)).astype(BF)
    grad_query = mm(keys, score_low, 1, 0) * scale
    grad_key = mm(queries, score_low, 1, 1)
    grad_value = mm(grad, probs.astype(BF), 1, 1)
    start = pl.multiple_of(step * block, block)
    gqk_ref[0, :, pl.ds(start, block)] = grad_query.astype(BF)

    @pl.when(step == 0)
    def _():
        ksum_ref[...] = grad_key
        vsum_ref[...] = grad_value

    @pl.when(step > 0)
    def _():
        ksum_ref[...] += grad_key
        vsum_ref[...] += grad_value

    @pl.when(step == pl.num_programs(1) - 1)
    def _():
        gqk_ref[1] = (ksum_ref[...] * scale).astype(BF)
        gv_ref[...] = vsum_ref[...].astype(BF)


def attend_clip_back(qk, values, log_sum, grad_attended, clip_len, block):
    return pl.pallas_call(
        attend_back_kernel,
        grid_spec=pltpu.PrefetchScalarGridSpec(
            num_scalar_prefetch=1,
            grid=(4, CLIP // block),
            in_specs=head_specs(block)
            + [
                pl.BlockSpec((None, 1, block), lambda h, i, n: (h, 0, i)),
                pl.BlockSpec((None, HEAD_DIM, block), lambda h, i, n: (h, 0, i)),
            ],
            out_specs=[
                pl.BlockSpec((None, 2, HEAD_DIM, CLIP), lambda h, i, n: (h, 0, 0, 0)),
                pl.BlockSpec((None, HEAD_DIM, CLIP), lambda h, i, n: (h, 0, 0)),
            ],
            scratch_shapes=[pltpu.VMEM((HEAD_DIM, CLIP), F32)] * 2,
        ),
        out_shape=[shaped((4, 2, HEAD_DIM, CLIP)), shaped((4, HEAD_DIM, CLIP))],
        cost_estimate=cost(40 * CLIP * CLIP * HEAD_DIM, 32 * HEAD_DIM * CLIP * 2),
        name="attend_clip_back",
    )(clip_len, qk, qk, values, log_sum, grad_attended)


WIDE = 384


def order_hot(core):
    place = lax.broadcasted_iota(jnp.int32, (OWN, OWN), 1)
    stored = lax.broadcasted_iota(jnp.int32, (OWN, OWN), 0)
    hot = jnp.zeros((OWN, OWN), jnp.bool_)
    for chunk in range(4):
        source = (2 * (chunk >> 1) + (core ^ (chunk & 1))) * HEAD_DIM
        inside = (place >= chunk * HEAD_DIM) & (place < (chunk + 1) * HEAD_DIM)
        hot = hot | (inside & (stored - source == place - chunk * HEAD_DIM))
    return jnp.where(hot, 1.0, 0.0).astype(BF)


def whole():
    return pl.BlockSpec(memory_space=pltpu.VMEM)


def prepare_kernel(spots_ref, qkv_ref, out_ref, in_ref, down_ref, kept_ref, sent_ref):
    c = spots_ref[0]
    for ref, core in ((kept_ref, c), (sent_ref, 1 - c)):
        hot = order_hot(core)

        def half(value, count):
            return jnp.where(core == 0, value[:count], value[count:])

        for s in range(3):
            value = half(mm(qkv_ref[s], hot, 1, 0), HEAD_DIM)
            ref[s * HEAD_DIM : (s + 1) * HEAD_DIM, :OWN] = value.astype(BF)
        value = half(mm(out_ref[...], hot, 1, 0), HEAD_DIM)
        ref[3 * HEAD_DIM : OWN, :OWN] = value.astype(BF)
        ref[OWN : 2 * OWN, :OWN] = half(mm(in_ref[...], hot, 0, 0), OWN).astype(BF)
        ref[2 * OWN :, :OWN] = half(mm(down_ref[...], hot, 0, 0), OWN).astype(BF)
        ref[:, OWN:] = jnp.zeros((3 * OWN, WIDE - OWN), BF)


def prepare(spots, qkv_turned, out_weight, in_weight, down_turned):
    return pl.pallas_call(
        prepare_kernel,
        in_specs=[spots_spec()] + [whole()] * 4,
        out_specs=[whole()] * 2,
        out_shape=[shaped((3 * OWN, WIDE))] * 2,
        cost_estimate=cost(8 * 3 * OWN * OWN * OWN, 4 * 3 * OWN * OWN * 2),
        name="prepare_weights",
    )(spots, qkv_turned, out_weight, in_weight, down_turned)


def lanes_kernel(spots_ref, kept_ref, got_ref, *out_refs):
    def write(near_ref, far_ref):
        start = 0
        for ref in out_refs:
            rows = slice(start, start + ref.shape[0])
            ref[:, :OWN] = near_ref[rows, :OWN]
            ref[:, OWN:] = far_ref[rows, :OWN]
            start += ref.shape[0]

    @pl.when(spots_ref[1] == 1)
    def _():
        write(kept_ref, got_ref)

    @pl.when(spots_ref[1] == 0)
    def _():
        write(got_ref, kept_ref)


def join_lanes(spots, kept, got):
    return pl.pallas_call(
        lanes_kernel,
        in_specs=[spots_spec(), whole(), whole()],
        out_specs=[whole()] * 4,
        out_shape=[shaped((n, HALF)) for n in (OWN // 2, OWN // 2, OWN, OWN)],
        cost_estimate=cost(0, 4 * 3 * OWN * OWN * 2),
        name="join_lanes",
    )(spots, kept, got)


def two_terms(value):
    high = value.astype(BF)
    return high, (value - high.astype(F32)).astype(BF)


def store_ff_kernel(spots_ref, up_ref, down_ref, kept_ref, sent_ref):
    hot = order_hot(spots_ref[0])
    is_near = spots_ref[1] == 1
    for place, total_ref in ((0, up_ref), (1, down_ref)):
        near, far = total_ref[:, :OWN], total_ref[:, OWN:]
        lanes = slice(place * OWN, (place + 1) * OWN)
        for ref, value in (
            (kept_ref, jnp.where(is_near, near, far)),
            (sent_ref, jnp.where(is_near, far, near)),
        ):
            high, rest = two_terms(value)
            ref[:, lanes] = mm(hot, high, 1, 1) + mm(hot, rest, 1, 1)


def store_ff(spots, up_total, down_total):
    return pl.pallas_call(
        store_ff_kernel,
        in_specs=[spots_spec()] + [whole()] * 2,
        out_specs=[whole()] * 2,
        out_shape=[shaped((OWN, HALF), F32)] * 2,
        cost_estimate=cost(16 * OWN * OWN * OWN, 16 * OWN * OWN * 4),
        name="store_ff",
    )(spots, up_total, down_total)


def join_ff_kernel(spots_ref, kept_ref, got_ref, up_ref, down_ref):
    def write(first_ref, second_ref):
        for place, ref in ((0, up_ref), (1, down_ref)):
            lanes = slice(place * OWN, (place + 1) * OWN)
            ref[:, :OWN] = first_ref[:, lanes]
            ref[:, OWN:] = second_ref[:, lanes]

    @pl.when(spots_ref[0] == 0)
    def _():
        write(kept_ref, got_ref)

    @pl.when(spots_ref[0] == 1)
    def _():
        write(got_ref, kept_ref)


def join_ff(spots, kept, got):
    return pl.pallas_call(
        join_ff_kernel,
        in_specs=[spots_spec()] + [whole()] * 2,
        out_specs=[whole()] * 2,
        out_shape=[shaped((OWN, HALF), F32)] * 2,
        cost_estimate=cost(0, 16 * OWN * OWN * 4),
        name="join_ff",
    )(spots, kept, got)


def store_qkvo_kernel(spots_ref, qk_ref, vo_ref, kept_ref, sent_ref):
    hot = order_hot(spots_ref[0])
    is_near = spots_ref[1] == 1
    for place, total_ref in ((0, qk_ref), (1, vo_ref)):
        near, far = total_ref[:, :OWN], total_ref[:, OWN:]
        rows = slice(place * 2 * HEAD_DIM, (place + 1) * 2 * HEAD_DIM)
        for ref, value in (
            (kept_ref, jnp.where(is_near, near, far)),
            (sent_ref, jnp.where(is_near, far, near)),
        ):
            high, rest = two_terms(value)
            ref[rows, :OWN] = mm(high, hot, 1, 1) + mm(rest, hot, 1, 1)
    kept_ref[:, OWN:] = jnp.zeros((OWN, WIDE - OWN), F32)
    sent_ref[:, OWN:] = jnp.zeros((OWN, WIDE - OWN), F32)


def store_qkvo(spots, qk_total, vo_total):
    return pl.pallas_call(
        store_qkvo_kernel,
        in_specs=[spots_spec()] + [whole()] * 2,
        out_specs=[whole()] * 2,
        out_shape=[shaped((OWN, WIDE), F32)] * 2,
        cost_estimate=cost(8 * OWN * OWN * OWN, 16 * OWN * OWN * 4),
        name="store_qkvo",
    )(spots, qk_total, vo_total)


def join_qkvo_kernel(spots_ref, kept_ref, got_ref, qkv_ref, out_ref):
    def write(first_ref, second_ref):
        for place, ref in ((0, first_ref), (1, second_ref)):
            rows = slice(place * HEAD_DIM, (place + 1) * HEAD_DIM)
            for s in range(3):
                qkv_ref[s, rows] = ref[s * HEAD_DIM : (s + 1) * HEAD_DIM, :OWN]
            out_ref[rows] = ref[3 * HEAD_DIM : 4 * HEAD_DIM, :OWN]

    @pl.when(spots_ref[0] == 0)
    def _():
        write(kept_ref, got_ref)

    @pl.when(spots_ref[0] == 1)
    def _():
        write(got_ref, kept_ref)


def join_qkvo(spots, kept, got):
    return pl.pallas_call(
        join_qkvo_kernel,
        in_specs=[spots_spec()] + [whole()] * 2,
        out_specs=[whole()] * 2,
        out_shape=[shaped((3, 2 * HEAD_DIM, OWN), F32), shaped((2 * HEAD_DIM, OWN), F32)],
        cost_estimate=cost(0, 8 * OWN * OWN * 4),
        name="join_qkvo",
    )(spots, kept, got)


TAIL = 8


def split_kernel(spots_ref, hid_ref, cot_ref, hk_ref, hs_ref, ck_ref, cs_ref):
    c = spots_ref[0]
    data, tails, cots = [], [], []
    for half in (0, 1):
        rows = slice(half * HEAD_DIM, (half + 1) * HEAD_DIM)
        value = hid_ref[rows]
        mean = jnp.mean(value, axis=0, keepdims=True)
        data.append(value - mean)
        high = mean.astype(BF).astype(F32)
        middle = (mean - high).astype(BF).astype(F32)
        low = mean - high - middle
        spot = lax.broadcasted_iota(jnp.int32, (TAIL, value.shape[1]), 0)
        tails.append(
            jnp.where(
                spot == 0, high, jnp.where(spot == 1, middle, jnp.where(spot == 2, low, 0.0))
            )
        )
        cots.append(cot_ref[rows])
    for ref, cot, first in ((hk_ref, ck_ref, c == 0), (hs_ref, cs_ref, c == 1)):
        ref[:HEAD_DIM] = jnp.where(first, data[0], data[1]).astype(BF)
        ref[HEAD_DIM:] = jnp.where(first, tails[0], tails[1]).astype(BF)
        cot[...] = jnp.where(first, cots[0], cots[1]).astype(BF)


def split(spots, hidden_in, cotangent):
    block = pl.BlockSpec((2 * HEAD_DIM, CLIP // 2), lambda i: (0, i))
    specs = [
        pl.BlockSpec((n, CLIP // 2), lambda i: (0, i))
        for n in (HEAD_DIM + TAIL, HEAD_DIM + TAIL, HEAD_DIM, HEAD_DIM)
    ]
    return pl.pallas_call(
        split_kernel,
        grid=(4,),
        in_specs=[spots_spec(), block, block],
        out_specs=specs,
        out_shape=[
            shaped((n, 2 * CLIP)) for n in (HEAD_DIM + TAIL, HEAD_DIM + TAIL, HEAD_DIM, HEAD_DIM)
        ],
        cost_estimate=cost(0, 8 * HEAD_DIM * 2 * CLIP * 4),
        name="split_in",
    )(spots, hidden_in, cotangent)


def deal_kernel(spots_ref, kept_ref, got_ref, here_ref, send_ref):
    for is_own in (0, 1):
        for x in (0, 1):

            @pl.when((spots_ref[2] == is_own) & (spots_ref[3] == x))
            def _(is_own=is_own, x=x):
                pair = (kept_ref, got_ref) if is_own else (got_ref, kept_ref)
                near = slice(x * CLIP, (x + 1) * CLIP)
                away = slice((1 - x) * CLIP, (2 - x) * CLIP)
                for i in (0, 1):
                    here_ref[i] = pair[i][:, near]
                    send_ref[i] = pair[i][:, away]


def deal(spots, kept, got):
    return pl.pallas_call(
        deal_kernel,
        in_specs=[spots_spec(), whole(), whole()],
        out_specs=[whole()] * 2,
        out_shape=[shaped((2, kept.shape[0], CLIP))] * 2,
        cost_estimate=cost(0, 8 * kept.shape[0] * CLIP * 2),
        name="deal",
    )(spots, kept, got)


def place_kernel(spots_ref, here_ref, there_ref, far_ref, own_ref, *stats_ref):
    grid = ((here_ref, 0), (there_ref, 0)), ((far_ref, 0), (far_ref, 1))
    for same in (0, 1):
        for x in (0, 1):

            @pl.when((spots_ref[4] == same) & (spots_ref[3] == x))
            def _(same=same, x=x):
                for i in (0, 1):
                    for j in (0, 1):
                        ref, k = grid[i if same else 1 - i][j if x == 0 else 1 - j]
                        if stats_ref:
                            tail = ref[k, HEAD_DIM:].astype(F32)
                            mean = tail[0:1] + tail[1:2] + tail[2:3]
                            own_ref[i, j] = ref[k, :HEAD_DIM].astype(F32) + mean
                        else:
                            own_ref[i, j] = ref[k]

    if stats_ref:
        values = own_ref[...].reshape(OWN, own_ref.shape[-1])
        mean = jnp.mean(values, axis=0, keepdims=True)
        off = values - mean
        stats_ref[0][0:1] = mean
        stats_ref[0][1:2] = jnp.sum(off * off, axis=0, keepdims=True)


def place(spots, here, there, far, with_stats):
    rows = here.shape[1]
    spec = pl.BlockSpec((2, rows, BLOCK), lambda i: (0, 0, i))
    own = (2, 2, HEAD_DIM, CLIP)
    outs = [(own, F32), ((2, CLIP), F32)] if with_stats else [(own, BF)]
    return pl.pallas_call(
        place_kernel,
        grid=(STEPS,),
        in_specs=[spots_spec()] + [spec] * 3,
        out_specs=[tokens_spec(dims) for dims, _ in outs],
        out_shape=[shaped(dims, kind) for dims, kind in outs],
        cost_estimate=cost(0, 8 * rows * CLIP * 6),
        name="place_in",
    )(spots, here, there, far)


def leave_kernel(spots_ref, own_ref, near_ref, far_ref):
    for same in (0, 1):
        for x in (0, 1):

            @pl.when((spots_ref[4] == same) & (spots_ref[3] == x))
            def _(same=same, x=x):
                for j in (0, 1):
                    k = j if x == 0 else 1 - j
                    near_ref[j] = own_ref[1 - same, k].astype(BF)
                    far_ref[j] = own_ref[same, k].astype(BF)


def leave(spots, own):
    dims = (2, HEAD_DIM, CLIP)
    return pl.pallas_call(
        leave_kernel,
        grid=(STEPS,),
        in_specs=[spots_spec(), tokens_spec(own.shape)],
        out_specs=[tokens_spec(dims)] * 2,
        out_shape=[shaped(dims)] * 2,
        cost_estimate=cost(0, 4 * HEAD_DIM * CLIP * 6),
        name="leave",
    )(spots, own)


def undeal_kernel(spots_ref, near_ref, far_ref, there_ref, kept_ref, sent_ref):
    for is_own in (0, 1):
        for x in (0, 1):

            @pl.when((spots_ref[2] == is_own) & (spots_ref[3] == x))
            def _(is_own=is_own, x=x):
                own = slice(x * CLIP, (x + 1) * CLIP)
                other = slice((1 - x) * CLIP, (2 - x) * CLIP)
                pair = (kept_ref, sent_ref) if is_own else (sent_ref, kept_ref)
                for k, ref in enumerate((near_ref, far_ref)):
                    pair[k][:, own] = ref[0]
                    pair[k][:, other] = there_ref[k]


def undeal(spots, near, far, there):
    dims = (HEAD_DIM, 2 * CLIP)
    return pl.pallas_call(
        undeal_kernel,
        in_specs=[spots_spec()] + [whole()] * 3,
        out_specs=[whole()] * 2,
        out_shape=[shaped(dims)] * 2,
        cost_estimate=cost(0, 16 * HEAD_DIM * CLIP * 2),
        name="undeal",
    )(spots, near, far, there)


def finish_kernel(spots_ref, kept_ref, got_ref, base_ref, shift_ref, out_ref):
    c = spots_ref[0]
    kept, got = kept_ref[...].astype(F32), got_ref[...].astype(F32)
    for half in (0, 1):
        rows = slice(half * HEAD_DIM, (half + 1) * HEAD_DIM)
        value = jnp.where(c == half, kept, got)
        out_ref[rows] = base_ref[rows] + shift_ref[rows] + value


def finish(spots, kept, got, base, shift):
    spec = pl.BlockSpec((HEAD_DIM, CLIP // 2), lambda i: (0, i))
    wide = pl.BlockSpec((2 * HEAD_DIM, CLIP // 2), lambda i: (0, i))
    return pl.pallas_call(
        finish_kernel,
        grid=(4,),
        in_specs=[spots_spec(), spec, spec, wide, fixed(shift)],
        out_specs=wide,
        out_shape=shaped(base.shape, F32),
        cost_estimate=cost(0, 8 * HEAD_DIM * 2 * CLIP * 4),
        name="finish",
    )(spots, kept, got, base, shift)


def y_last(pair, yr, rows=slice(None)):
    return jnp.concatenate([pair[yr][xr, zhr, rows] for xr in (0, 1) for zhr in (0, 1)])


def x_last(pair, yr, rows=slice(None)):
    return jnp.concatenate([pair[xr][yr, zhr, rows] for xr in (0, 1) for zhr in (0, 1)])


def wide_rows(half, pair, rows=slice(None)):
    return jnp.concatenate([half(pair, 0, rows), half(pair, 1, rows)], axis=1)


def join_blocks(refs):
    return jnp.concatenate(
        [
            refs[2 * zlr + cr][yr, xr]
            for yr in (0, 1)
            for zlr in (0, 1)
            for xr in (0, 1)
            for cr in (0, 1)
        ]
    )


HEAD_ROWS = slice(0, HEAD_DIM)
OUT_ROWS = slice(HEAD_DIM, 2 * HEAD_DIM)


def project_kernel(b0, b1, b2, b3, qk0, qk1, vo0, vo1, qs_ref, vs_ref, qk_ref, v_ref, wide_ref):
    wide = join_blocks((b0, b1, b2, b3))
    wide_ref[...] = wide
    result = mm(wide_rows(y_last, (qk0, qk1)), wide, 1, 0)
    for t in range(4):
        first = t * 2 * HEAD_DIM
        queries = result[first : first + HEAD_DIM] + qs_ref[t]
        qk_ref[t, 0] = queries.astype(BF)
        qk_ref[t, 1] = result[first + HEAD_DIM : first + 2 * HEAD_DIM].astype(BF)
    result = mm(wide_rows(x_last, (vo0, vo1), HEAD_ROWS), wide, 1, 0)
    for t in range(4):
        v_ref[t] = (result[t * HEAD_DIM : (t + 1) * HEAD_DIM] + vs_ref[t]).astype(BF)


def project(blocks, qk, vo, q_shift, v_shift):
    operands = (*blocks, *qk, *vo, q_shift, v_shift)
    outs = ((4, 2, HEAD_DIM, CLIP), (4, HEAD_DIM, CLIP), (D, CLIP))
    return pl.pallas_call(
        project_kernel,
        grid=(STEPS,),
        in_specs=[tokens_spec(b.shape) for b in blocks] + [fixed(a) for a in operands[4:]],
        out_specs=[tokens_spec(dims) for dims in outs],
        out_shape=[shaped(dims) for dims in outs],
        cost_estimate=cost(2 * 3 * OWN * D * CLIP, 4 * D * CLIP * 2),
        name="project",
    )(*operands)


def up_kernel(b0, b1, b2, b3, up0, up1, shift_ref, act_ref, slope_ref, wide_ref):
    wide = join_blocks((b0, b1, b2, b3))
    wide_ref[...] = wide
    for xr in (0, 1):
        for zhr in (0, 1):
            first = (2 * xr + zhr) * OWN
            rows = slice(first, first + OWN)
            weight = jnp.concatenate([up0[xr, zhr], up1[xr, zhr]], axis=1)
            pre = mm(weight, wide, 1, 0) + shift_ref[rows]
            cdf = 0.5 * (1.0 + lax.erf(pre * (0.5**0.5)))
            act_ref[rows] = (pre * cdf).astype(BF)
            slope_ref[rows] = cdf + pre * jnp.exp(-0.5 * pre * pre) * 0.3989422804014327


def up_project(blocks, up, in_shift):
    operands = (*blocks, *up, in_shift)
    outs = (((UNITS, CLIP), BF), ((UNITS, CLIP), F32), ((D, CLIP), BF))
    return pl.pallas_call(
        up_kernel,
        grid=(STEPS,),
        in_specs=[tokens_spec(b.shape) for b in blocks] + [fixed(a) for a in operands[4:]],
        out_specs=[tokens_spec(dims) for dims, _ in outs],
        out_shape=[shaped(dims, kind) for dims, kind in outs],
        cost_estimate=cost(2 * UNITS * D * CLIP, 6 * D * CLIP * 2),
        name="up_project",
    )(*operands)


def grad_act_kernel(b0, b1, b2, b3, down0, down1, slope_ref, out_ref, wide_ref):
    wide = join_blocks((b0, b1, b2, b3))
    wide_ref[...] = wide
    for xr in (0, 1):
        for zhr in (0, 1):
            first = (2 * xr + zhr) * OWN
            rows = slice(first, first + OWN)
            pair = (down0, down1)[xr]
            weight = jnp.concatenate([pair[0, zhr], pair[1, zhr]], axis=1)
            out_ref[rows] = (mm(weight, wide, 1, 0) * slope_ref[rows]).astype(BF)


def grad_act(blocks, down, slope):
    operands = (*blocks, *down, slope)
    outs = ((UNITS, CLIP), (D, CLIP))
    return pl.pallas_call(
        grad_act_kernel,
        grid=(STEPS,),
        in_specs=[tokens_spec(b.shape) for b in blocks]
        + [fixed(a) for a in down]
        + [tokens_spec(slope.shape)],
        out_specs=[tokens_spec(dims) for dims in outs],
        out_shape=[shaped(dims) for dims in outs],
        cost_estimate=cost(2 * UNITS * D * CLIP, 6 * D * CLIP * 2),
        name="grad_act",
    )(*operands)


def grad_attended_kernel(b0, b1, b2, b3, vo0, vo1, out_ref, wide_ref):
    wide = join_blocks((b0, b1, b2, b3))
    wide_ref[...] = wide
    result = mm(wide_rows(x_last, (vo0, vo1), OUT_ROWS), wide, 1, 0)
    for t in range(4):
        out_ref[t] = result[t * HEAD_DIM : (t + 1) * HEAD_DIM].astype(BF)


def grad_attended_of(blocks, vo):
    outs = ((4, HEAD_DIM, CLIP), (D, CLIP))
    return pl.pallas_call(
        grad_attended_kernel,
        grid=(STEPS,),
        in_specs=[tokens_spec(b.shape) for b in blocks] + [fixed(a) for a in vo],
        out_specs=[tokens_spec(dims) for dims in outs],
        out_shape=[shaped(dims) for dims in outs],
        cost_estimate=cost(2 * OWN * D * CLIP, 4 * D * CLIP * 2),
        name="grad_attended",
    )(*blocks, *vo)


def fold_kernel(fill, counts, *refs):
    sources, values = refs[: counts[0]], refs[counts[0] : sum(counts)]
    keep_ref, send_ref, turned_ref = refs[sum(counts) :]

    @pl.when(pl.program_id(0) == 0)
    def _():
        for yr in (0, 1):
            turned_ref[yr * HALF : (yr + 1) * HALF] = jnp.transpose(fill(sources, yr))

    value = jnp.concatenate([ref[...].reshape(-1, BLOCK) for ref in values])
    for yr in (0, 1):
        result = mm(turned_ref[yr * HALF : (yr + 1) * HALF], value, 1, 0)
        for spot in range(8):
            part = result[spot * HEAD_DIM : (spot + 1) * HEAD_DIM]
            zlr, xr, cr = spot >> 2, spot >> 1 & 1, spot & 1
            if cr == 0:
                keep_ref[yr, zlr, xr] = part
            else:
                send_ref[yr, zlr, xr] = part.astype(BF)


def fold(fill, sources, values, name):
    depth = sum(v.size // CLIP for v in values)
    dims = (2, 2, 2, HEAD_DIM, CLIP)
    return pl.pallas_call(
        functools.partial(fold_kernel, fill, (len(sources), len(values))),
        grid=(STEPS,),
        in_specs=[fixed(a) for a in sources] + [tokens_spec(v.shape) for v in values],
        out_specs=[tokens_spec(dims)] * 2,
        out_shape=[shaped(dims, F32), shaped(dims)],
        scratch_shapes=[pltpu.VMEM((D, depth), BF)],
        cost_estimate=cost(2 * D * depth * CLIP, 6 * D * CLIP * 2),
        name=name,
    )(*sources, *values)


def fill_out(sources, yr):
    return x_last(sources, yr, OUT_ROWS)


def fill_up(sources, yr):
    return y_last(sources, yr)


def fill_down(sources, yr):
    return x_last(sources, yr)


def fill_project(sources, yr):
    return jnp.concatenate([y_last(sources[:2], yr), x_last(sources[2:], yr, HEAD_ROWS)])


def pair_y_kernel(left_ref, right_ref, keep_ref, send_ref):
    result = mm(left_ref[0], right_ref[...], 1, 1)
    keep_ref[0] = result[:, :HALF]
    send_ref[0] = result[:, HALF:].astype(BF)


def grad_y_first(left, right, name):
    rows = left.shape[1]
    dims = (4, rows, HALF)
    spec = pl.BlockSpec((1, rows, HALF), lambda i: (i, 0, 0))
    return pl.pallas_call(
        pair_y_kernel,
        grid=(4,),
        in_specs=[pl.BlockSpec((1, rows, CLIP), lambda i: (i, 0, 0)), fixed(right)],
        out_specs=[spec] * 2,
        out_shape=[shaped(dims, F32), shaped(dims)],
        cost_estimate=cost(2 * 4 * rows * D * CLIP, 4 * rows * D * 6),
        name=name,
    )(left, right)


def pair_x_kernel(count, *refs):
    keep_ref, send_ref = refs[2 * count :]
    start = 0
    for left_ref, right_ref in zip(refs[:count], refs[count : 2 * count]):
        rows = slice(start, start + left_ref.shape[2])
        start += left_ref.shape[2]
        for xr in (0, 1):
            result = mm(left_ref[xr, 0], right_ref[...], 1, 1)
            for yr in (0, 1):
                part = result[:, yr * HALF : (yr + 1) * HALF]
                if xr == 0:
                    keep_ref[yr, 0, rows] = part
                else:
                    send_ref[yr, 0, rows] = part.astype(BF)


def grad_x_first(lefts, rights, name):
    rows = sum(v.shape[2] for v in lefts)
    dims = (2, 2, rows, HALF)
    spec = pl.BlockSpec((2, 1, rows, HALF), lambda i: (0, i, 0, 0))
    return pl.pallas_call(
        functools.partial(pair_x_kernel, len(lefts)),
        grid=(2,),
        in_specs=[pl.BlockSpec((2, 1) + v.shape[2:], lambda i: (0, i, 0, 0)) for v in lefts]
        + [fixed(v) for v in rights],
        out_specs=[spec] * 2,
        out_shape=[shaped(dims, F32), shaped(dims)],
        cost_estimate=cost(2 * 4 * rows * D * CLIP, 4 * rows * D * 6),
        name=name,
    )(*lefts, *rights)


def token_stats(values):
    mean = jnp.mean(values, axis=0)
    off = values - mean
    return jnp.stack([mean, jnp.sum(off * off, axis=0)])


def merge_stats(stats, count, swap):
    other = swap(stats)
    apart = other[0] - stats[0]
    return jnp.stack(
        [0.5 * (stats[0] + other[0]), stats[1] + other[1] + apart * apart * (0.5 * count)]
    )


def after(values, *others):
    return lax.optimization_barrier((values, others))[0]


def local_clip(
    hidden_in,
    lengths,
    ln1_gain,
    ln1_shift,
    qkv_weight,
    qv_bias,
    out_weight,
    out_bias,
    ln2_gain,
    ln2_shift,
    in_weight,
    in_bias,
    down_weight,
    down_bias,
    cotangent,
):
    row, col = lax.axis_index("row"), lax.axis_index("col")
    y, c = row // 2, row % 2
    zh, zl, x = col // 4, col // 2 % 2, col % 2
    same_zy = y == zh
    spots = jnp.stack([c, zl == c, zh == c, x, same_zy]).astype(jnp.int32)

    def flip(grid):
        grid = jnp.where(same_zy, grid, grid[::-1])
        return jnp.where(x == 0, grid, grid[:, ::-1])

    def fold_cores(parts):
        keep = parts[0] + swap_core(parts[1])
        return keep[:, 0], keep[:, 1].astype(BF)

    kept, sent = prepare(
        spots,
        jnp.swapaxes(qkv_weight, 1, 2),
        out_weight,
        in_weight,
        jnp.swapaxes(down_weight, 0, 1),
    )
    weights_got = swap_core(sent)
    h_kept, h_sent, c_kept, c_sent = split(spots, hidden_in, cotangent)
    h_here, h_send = deal(spots, h_kept, swap_core(h_sent))
    s_qk, s_vo, s_up, s_down = join_lanes(spots, kept, weights_got)
    h_there = swap_x(h_send)
    qk_zh, vo_zh = swap_zh(s_qk), swap_zh(s_vo)

    pack = jnp.stack(
        [ln1_gain, ln1_shift, ln2_gain, ln2_shift, out_bias, qv_bias[0], qv_bias[1]]
    )
    pack = jnp.where(c == 0, pack[:, :HEAD_DIM], pack[:, HEAD_DIM:])
    hidden_shift = jnp.where(c == 0, in_bias[:OWN], in_bias[OWN:])
    pack = jnp.concatenate([pack, hidden_shift.reshape(4, HEAD_DIM)])
    pack = jnp.stack([pack, swap_x(pack)])
    pack = jnp.stack([pack, swap_zh(pack)])

    h_message = jnp.stack([h_here[1], h_there[1]])
    h_message, qk_zh, vo_zh = lax.optimization_barrier((h_message, qk_zh, vo_zh))
    h_far = swap_zh(h_message)
    qk_one = jnp.stack([s_qk, qk_zh])
    vo_one = jnp.stack([s_vo, vo_zh])
    qk_two, vo_two = swap_x(qk_one), swap_y(vo_one)
    h_far, qk_two, vo_two = lax.optimization_barrier((h_far, qk_two, vo_two))
    w_qk = jnp.stack([qk_one, qk_two])
    w_vo = jnp.stack([vo_one, vo_two])
    w_qk = w_qk, swap_y(w_qk)
    w_vo = w_vo, swap_x(w_vo)
    s_up = after(s_up, h_far)
    up_zh = swap_zh(s_up)

    owned = flip(pack)
    gain_one, shift_one, gain_two, shift_two, out_shift = (
        owned[:, :, i, :, None] for i in range(5)
    )
    by_head = pack.transpose(1, 0, 2, 3)
    q_shift = by_head[:, :, 5].reshape(4, HEAD_DIM, 1)
    v_shift = by_head[:, :, 6].reshape(4, HEAD_DIM, 1)
    in_shift = by_head[:, :, 7:].reshape(UNITS, 1)

    hidden_own, stats = place(spots, h_here, h_there, h_far, True)
    stats = merge_stats(stats, OWN, swap_core)
    stats = merge_stats(stats, 2 * OWN, swap_zl)
    inv_one = lax.rsqrt(stats[1] / D + EPS)
    own_one = (hidden_own - stats[0]) * inv_one
    low_one = (own_one * gain_one + shift_one).astype(BF)
    low_one_z = swap_zl(low_one)
    s_down = after(s_down, low_one_z)
    down_zh = swap_zh(s_down)
    c_here, c_send = deal(spots, c_kept, swap_core(after(c_sent, low_one)))
    c_there = swap_x(after(c_send, w_vo[1]))
    wide_one = low_one, swap_core(low_one), low_one_z, swap_core(low_one_z)
    wide_one = after(wide_one, c_send, s_down)

    qk, values, ln_one = project(wide_one, w_qk, w_vo, q_shift, v_shift)
    clip_len = lax.dynamic_slice_in_dim(lengths, 4 * y + 2 * zh + x, 1)
    attended, log_sum = attend_clip(qk, values, clip_len, CLIP)
    attended, up_zh, down_zh, c_there = lax.optimization_barrier(
        (attended, up_zh, down_zh, c_there)
    )
    up_one = jnp.stack([s_up, up_zh])
    down_one = jnp.stack([s_down, down_zh])
    c_message = jnp.stack([c_here[1], c_there[1]])
    up_two, down_two, c_far = swap_x(up_one), swap_y(down_one), swap_zh(c_message)
    delta_near, delta_send = fold_cores(
        fold(fill_out, w_vo, (after(attended, up_one, down_one, c_message),), "fold_out")
    )
    delta_got = swap_zl(delta_send)
    delta_got, up_two, down_two, c_far = lax.optimization_barrier(
        (delta_got, up_two, down_two, c_far)
    )
    delta_mid = delta_near + delta_got + out_shift
    w_up = jnp.stack([up_one, up_two])
    w_down = jnp.stack([down_one, down_two])
    w_up = w_up, swap_y(w_up)
    w_down = w_down, swap_x(w_down)

    hidden_mid = hidden_own + delta_mid
    stats = token_stats(hidden_mid.reshape(OWN, CLIP))
    stats = merge_stats(stats, OWN, swap_core)
    stats = merge_stats(stats, 2 * OWN, swap_zl)
    inv_two = lax.rsqrt(stats[1] / D + EPS)
    own_two = (hidden_mid - stats[0]) * inv_two
    low_two = (own_two * gain_two + shift_two).astype(BF)
    low_two_z = swap_zl(low_two)
    (cot_own,) = place(spots, c_here, c_there, after(c_far, low_two), False)
    cot_own = after(cot_own, low_two_z)
    cot_z = swap_zl(cot_own)
    wide_cot = cot_own, swap_core(cot_own), cot_z, swap_core(cot_z)
    wide_two = low_two, swap_core(low_two), low_two_z, swap_core(low_two_z)
    act_low, slope, ln_two = up_project(after(wide_two, cot_own), w_up, in_shift)
    out_near, out_send = fold_cores(fold(fill_down, w_down, (act_low,), "fold_down"))
    out_send = after(out_send, cot_z)
    out_got = swap_zl(out_send)

    grad_pre, cot_all = grad_act(after(wide_cot, out_send), w_down, slope)
    two_near, two_send = fold_cores(fold(fill_up, w_up, (grad_pre,), "fold_up"))
    two_send, out_got = lax.optimization_barrier((two_send, out_got))
    two_got = swap_zl(two_send)
    by_unit = (2, 2, OWN, CLIP)
    act_low_after, cot_all_after = after((act_low, cot_all), two_send)
    part_down = grad_x_first((act_low_after.reshape(by_unit),), (cot_all_after,), "grad_down")
    down_first = swap_x(part_down[1])
    part_up = grad_y_first(
        after(grad_pre, part_down[1]).reshape(4, OWN, CLIP), ln_two, "grad_up"
    )
    up_first = swap_y(part_up[1])
    two_got = after(two_got, part_up[1])
    grad_two = two_near + two_got

    def norm_back(grad, normed, inv, gain):
        scaled = grad * gain
        sums = jnp.stack([jnp.sum(scaled, axis=(0, 1, 2)), jnp.sum(scaled * normed, axis=(0, 1, 2))])
        sums = sums + swap_core(sums)
        sums = (sums + swap_zl(sums)) / D
        return inv * (scaled - sums[0] - normed * sums[1])

    norm_two_grad = norm_back(grad_two, own_two, inv_two, gain_two)
    mid_own = cot_own.astype(F32) + norm_two_grad
    mid_low = mid_own.astype(BF)
    mid_z = swap_zl(mid_low)
    out_leave, out_leave_far = leave(spots, delta_mid + after(out_near, mid_low) + out_got)
    out_leave_far, mid_z = lax.optimization_barrier((out_leave_far, mid_z))
    out_far = swap_zh(out_leave_far)
    wide_mid = mid_low, swap_core(mid_low), mid_z, swap_core(mid_z)
    wide_mid = after(wide_mid, out_leave_far)

    def second_step(keep, got):
        keep = keep.reshape(2, 2, -1, HALF) + got.reshape(2, 2, -1, HALF)
        return keep[0], keep[1].astype(BF)

    def third_step(keep, got):
        keep = keep + got
        return keep[0], keep[1].astype(BF)

    grad_attended, mid_all = grad_attended_of(wide_mid, w_vo)
    grad_attended, down_first, up_first = lax.optimization_barrier(
        (grad_attended, down_first, up_first)
    )
    down_keep, down_send = second_step(part_down[0], down_first)
    up_keep, up_send = second_step(part_up[0], up_first)
    down_second, up_second = swap_y(down_send), swap_x(up_send)
    grad_attended = after(grad_attended, down_send, up_send)
    grad_qk, grad_v = attend_clip_back(qk, values, log_sum, grad_attended, clip_len, CLIP)
    grad_qk, grad_v, down_second, up_second, out_far = lax.optimization_barrier(
        (grad_qk, grad_v, down_second, up_second, out_far)
    )
    down_keep, down_send = third_step(down_keep, down_second)
    up_keep, up_send = third_step(up_keep, up_second)
    down_third, up_third = swap_zh(down_send), swap_zh(up_send)
    out_message = jnp.stack([out_leave[1], out_far[1]])
    out_there = swap_x(out_message)
    folded = fold(
        fill_project,
        (*w_qk, *w_vo),
        after((grad_qk, grad_v), down_send, up_send, out_message),
        "fold_project",
    )
    one_near, one_send = fold_cores(folded)
    one_got = swap_zl(one_send)
    by_head_dims = (2, 2, HEAD_DIM, CLIP)
    grad_v, grad_qk = after((grad_v, grad_qk), one_send)
    part_vo = grad_x_first(
        (grad_v.reshape(by_head_dims), attended.reshape(by_head_dims)),
        (ln_one, mid_all),
        "grad_vo",
    )
    vo_first = swap_x(part_vo[1])
    part_qk = grad_y_first(
        after(grad_qk, part_vo[1]).reshape(4, 2 * HEAD_DIM, CLIP), ln_one, "grad_qk"
    )
    qk_first = swap_y(part_qk[1])
    out_kept, out_sent = undeal(spots, out_leave, out_far, after(out_there, part_qk[1]))
    hidden_out = finish(spots, out_kept, swap_core(out_sent), hidden_in, down_bias[:, None])

    one_got = after(one_got, out_sent)
    grad_one = one_near + one_got
    norm_one_grad = norm_back(grad_one, own_one, inv_one, gain_one)
    in_leave, in_leave_far = leave(spots, norm_two_grad + norm_one_grad)
    in_far = swap_zh(in_leave_far)

    vo_first, qk_first, down_third, up_third = after(
        (vo_first, qk_first, down_third, up_third), in_leave_far
    )
    vo_keep, vo_send = second_step(part_vo[0], vo_first)
    qk_keep, qk_send = second_step(part_qk[0], qk_first)
    vo_second, qk_second = swap_y(vo_send), swap_x(qk_send)
    ff_kept, ff_sent = store_ff(
        spots, after(up_keep + up_third, vo_send, qk_send), down_keep + down_third
    )
    ff_got = swap_core(ff_sent)
    in_far, vo_second, qk_second = lax.optimization_barrier(
        after((in_far, vo_second, qk_second), ff_sent)
    )
    in_message = jnp.stack([in_leave[1], in_far[1]])
    in_there = swap_x(in_message)
    vo_keep, vo_send = third_step(vo_keep, vo_second)
    qk_keep, qk_send = third_step(qk_keep, qk_second)
    vo_third, qk_third = swap_zh(vo_send), swap_zh(qk_send)
    g_up, g_down = join_ff(spots, ff_kept, after(ff_got, vo_send, qk_send, in_message))
    in_kept, in_sent = undeal(spots, in_leave, in_far, in_there)
    no_shift = jnp.zeros((2 * HEAD_DIM, 1), F32)
    hidden_grad = finish(spots, in_kept, swap_core(in_sent), cotangent, no_shift)
    at_kept, at_sent = store_qkvo(spots, qk_keep + qk_third, vo_keep + vo_third)
    g_qkv, g_out = join_qkvo(spots, at_kept, swap_core(at_sent))

    def over_tokens(values):
        return jnp.sum(values, axis=-1, dtype=F32)

    owned = jnp.stack(
        [
            over_tokens(v)
            for v in (
                grad_one * own_one,
                grad_one,
                grad_two * own_two,
                grad_two,
                mid_own,
                cot_own.astype(F32),
            )
        ],
        axis=2,
    ).reshape(2, 2, -1)
    heads = jnp.concatenate(
        [
            over_tokens(grad_qk[:, 0].astype(F32)),
            over_tokens(grad_v.astype(F32)),
            over_tokens(grad_pre.astype(F32)).reshape(4, OWN),
        ],
        axis=1,
    )
    vectors = jnp.concatenate([flip(owned), heads.reshape(2, 2, -1).transpose(1, 0, 2)], axis=2)
    total = vectors[0] + swap_zh(vectors[1])
    total = total[0] + swap_x(total[1])
    total = total + swap_y(total)
    other = swap_core(total)
    both = jnp.where(c == 0, jnp.stack([total, other]), jnp.stack([other, total]))
    singles = both[:, : 8 * HEAD_DIM].reshape(2, 8, HEAD_DIM).transpose(1, 0, 2).reshape(8, -1)

    return (
        hidden_out,
        hidden_grad,
        singles[0],
        singles[1],
        jnp.swapaxes(g_qkv, 1, 2),
        singles[6:8],
        g_out,
        singles[4],
        singles[2],
        singles[3],
        g_up,
        both[:, 8 * HEAD_DIM :].reshape(-1),
        jnp.swapaxes(g_down, 0, 1),
        singles[5],
    )


def solution(mesh):
    sizes = dict(mesh.shape)

    def program(*arrays):
        small = sizes == {"row": 4, "col": 8} and arrays[0].shape == (D, 2 * sizes["row"] * CLIP)
        return mapped(local_clip if small else local, mesh)(*arrays)

    return program


def mapped(body, mesh):
    return jax.shard_map(
        body,
        mesh=mesh,
        in_specs=(
            P("col", "row"),
            P(),
            P("col"),
            P("col"),
            P(None, "row", "col"),
            P(None, "col"),
            P("col", "row"),
            P("col"),
            P("col"),
            P("col"),
            P("row", "col"),
            P("col"),
            P("col", "row"),
            P("col"),
            P("col", "row"),
        ),
        out_specs=(
            P("col", "row"),
            P("col", "row"),
            P("col"),
            P("col"),
            P(None, "row", "col"),
            P(None, "col"),
            P("col", "row"),
            P("col"),
            P("col"),
            P("col"),
            P("row", "col"),
            P("col"),
            P("col", "row"),
            P("col"),
        ),
        check_vma=False,
    )
```

```python
import functools

import jax
import jax.numpy as jnp
from jax import lax
from jax.experimental import pallas as pl
from jax.experimental.pallas import tpu as pltpu
from jax.sharding import PartitionSpec as P

HEADS = 16
HEAD_DIM = 80
D = 1280
MICRO = 2
GROUP = 8


EPS = 1e-05


def partner(block, axis, distance):
    count = lax.axis_size(axis)
    route = []
    for low in range(count):
        high = low | 1 << distance
        if high != low and high < count:
            route += [(low, high), (high, low)]
    return lax.ppermute(block, axis, route)


def row_totals(first_sum, second_sum):
    return lax.psum((first_sum, second_sum), "col")


def widen(values):
    return lax.all_gather(values, "col", axis=1, tiled=True)


def narrow(values):
    return lax.psum_scatter(values, "col", scatter_dimension=1, tiled=True)


def to_clips(stacked):
    return lax.all_to_all(stacked, "col", split_axis=1, concat_axis=2, tiled=True)


def to_columns(stacked):
    return lax.all_to_all(stacked, "col", split_axis=2, concat_axis=1, tiled=True)


def contract_rows(left, right):
    return lax.dot_general(
        left, right, (((0,), (0,)), ((), ())), preferred_element_type=jnp.float32
    )


def contract_cols(left, right):
    return lax.dot_general(
        left, right, (((1,), (1,)), ((), ())), preferred_element_type=jnp.float32
    )


def exact_gelu(values):
    return jax.nn.gelu(values, approximate=False)


def norm_forward(values, norm_gain, norm_shift):
    first_sum, second_sum = row_totals(jnp.sum(values, axis=1), jnp.sum(values * values, axis=1))
    mean_rows = first_sum / D
    inv_std = lax.rsqrt(second_sum / D - mean_rows * mean_rows + EPS)
    normed = (values - mean_rows[:, None]) * inv_std[:, None]
    return (normed, inv_std, normed * norm_gain + norm_shift)


def norm_backward(grad_out, normed, inv_std, norm_gain):
    scaled = grad_out * norm_gain
    first_sum, second_sum = row_totals(jnp.sum(scaled, axis=1), jnp.sum(scaled * normed, axis=1))
    grad_input = inv_std[:, None] * (
        scaled - first_sum[:, None] / D - normed * (second_sum[:, None] / D)
    )
    return (grad_input, jnp.sum(grad_out * normed, axis=0), jnp.sum(grad_out, axis=0))


def split_heads(values):
    return values.reshape(values.shape[0], HEADS, HEAD_DIM)


def gather_clip(key_rows, value_rows):
    position = lax.axis_index("col")
    for bit_index in range(GROUP.bit_length() - 1):
        other_keys, other_values = partner((key_rows, value_rows), "col", bit_index)
        upper_half = position >> bit_index & 1 == 1
        key_rows = jnp.where(
            upper_half,
            jnp.concatenate([other_keys, key_rows]),
            jnp.concatenate([key_rows, other_keys]),
        )
        value_rows = jnp.where(
            upper_half,
            jnp.concatenate([other_values, value_rows]),
            jnp.concatenate([value_rows, other_values]),
        )
    return (key_rows, value_rows)


def scatter_clip(grad_keys, grad_values):
    position = lax.axis_index("col")
    for bit_index in reversed(range(GROUP.bit_length() - 1)):
        half_rows = grad_keys.shape[0] // 2
        upper_half = position >> bit_index & 1 == 1
        keep_keys = jnp.where(upper_half, grad_keys[half_rows:], grad_keys[:half_rows])
        send_keys = jnp.where(upper_half, grad_keys[:half_rows], grad_keys[half_rows:])
        keep_values = jnp.where(upper_half, grad_values[half_rows:], grad_values[:half_rows])
        send_values = jnp.where(upper_half, grad_values[:half_rows], grad_values[half_rows:])
        got_keys, got_values = partner((send_keys, send_values), "col", bit_index)
        grad_keys = keep_keys + got_keys
        grad_values = keep_values + got_values
    return (grad_keys, grad_values)


def clip_scores(queries, key_rows, valid_len):
    scale_factor = HEAD_DIM ** (-0.5)
    scores = (
        jnp.einsum(
            "qhe,khe->hqk",
            split_heads(queries),
            split_heads(key_rows),
            preferred_element_type=jnp.float32,
        )
        * scale_factor
    )
    live_keys = lax.broadcasted_iota(jnp.int32, (1, 1, key_rows.shape[0]), 2) < valid_len
    return jnp.where(live_keys, scores, -1e30)


def attend(queries, key_rows, value_rows, valid_len):
    scores = clip_scores(queries, key_rows, valid_len)
    top_score = jnp.max(scores, axis=2, keepdims=True)
    weights = jnp.exp(scores - top_score)
    weight_sum = jnp.sum(weights, axis=2, keepdims=True)
    prob_low = (weights / weight_sum).astype(jnp.bfloat16)
    attended = jnp.einsum(
        "hqk,khe->qhe", prob_low, split_heads(value_rows), preferred_element_type=jnp.float32
    )
    return (attended.reshape(queries.shape[0], -1), top_score + jnp.log(weight_sum))


def attend_back(queries, key_rows, value_rows, valid_len, log_sum, grad_low):
    scale_factor = HEAD_DIM ** (-0.5)
    scores = clip_scores(queries, key_rows, valid_len)
    probs_full = jnp.exp(scores - log_sum)
    grad_heads = split_heads(grad_low)
    grad_value = jnp.einsum(
        "hqk,qhe->khe",
        probs_full.astype(jnp.bfloat16),
        grad_heads,
        preferred_element_type=jnp.float32,
    )
    grad_probs = jnp.einsum(
        "qhe,khe->hqk", grad_heads, split_heads(value_rows), preferred_element_type=jnp.float32
    )
    row_dot = jnp.sum(probs_full * grad_probs, axis=2, keepdims=True)
    grad_scores = (probs_full * (grad_probs - row_dot)).astype(jnp.bfloat16)
    grad_query = (
        jnp.einsum(
            "hqk,khe->qhe", grad_scores, split_heads(key_rows), preferred_element_type=jnp.float32
        )
        * scale_factor
    )
    grad_key = (
        jnp.einsum(
            "hqk,qhe->khe", grad_scores, split_heads(queries), preferred_element_type=jnp.float32
        )
        * scale_factor
    )
    return (
        grad_query.reshape(queries.shape[0], -1),
        grad_key.reshape(key_rows.shape[0], -1),
        grad_value.reshape(key_rows.shape[0], -1),
    )


def layer_pass(input_rows, grad_rows, weights, vectors, valid_len):
    qkv_full, out_full, in_full, down_full = weights
    gain_one, shift_one, qv_full, out_shift, gain_two, shift_two, in_shift, down_shift = vectors
    bias_three = jnp.stack([qv_full[0], jnp.zeros_like(qv_full[0]), qv_full[1]])[:, None, :]
    normed_one, inv_one, ln_one = norm_forward(input_rows, gain_one, shift_one)
    wide_one = widen(ln_one.astype(jnp.bfloat16))
    projected = (
        jnp.einsum("td,sdc->stc", wide_one, qkv_full, preferred_element_type=jnp.float32)
        + bias_three
    )
    projected = to_clips(projected.astype(jnp.bfloat16))
    key_rows, value_rows = gather_clip(projected[1], projected[2])
    attended, log_sum = attend(projected[0], key_rows, value_rows, valid_len)
    attended_low = to_columns(attended.astype(jnp.bfloat16)[None])[0]
    hidden_mid = (
        input_rows
        + narrow(jnp.dot(attended_low, out_full, preferred_element_type=jnp.float32))
        + out_shift
    )
    normed_two, inv_two, ln_two = norm_forward(hidden_mid, gain_two, shift_two)
    wide_two = widen(ln_two.astype(jnp.bfloat16))
    pre_act = jnp.dot(wide_two, in_full, preferred_element_type=jnp.float32) + in_shift
    act_value, gelu_back = jax.vjp(exact_gelu, pre_act)
    act_low = act_value.astype(jnp.bfloat16)
    hidden_out = (
        hidden_mid
        + narrow(jnp.dot(act_low, down_full, preferred_element_type=jnp.float32))
        + down_shift
    )
    grad_wide = widen(grad_rows.astype(jnp.bfloat16))
    grad_down = contract_rows(act_low, grad_wide)
    grad_pre = gelu_back(contract_cols(grad_wide, down_full))[0].astype(jnp.bfloat16)
    grad_in = contract_rows(wide_two, grad_pre)
    grad_ln_two = narrow(contract_cols(grad_pre, in_full))
    grad_norm_two, grad_gain_two, grad_shift_two = norm_backward(
        grad_ln_two, normed_two, inv_two, gain_two
    )
    grad_mid = grad_rows + grad_norm_two
    grad_mid_wide = widen(grad_mid.astype(jnp.bfloat16))
    grad_out = contract_rows(attended_low, grad_mid_wide)
    grad_attended = to_clips(contract_cols(grad_mid_wide, out_full).astype(jnp.bfloat16)[None])[0]
    grad_query, grad_key, grad_value = attend_back(
        projected[0], key_rows, value_rows, valid_len, log_sum, grad_attended
    )
    grad_key, grad_value = scatter_clip(grad_key, grad_value)
    grad_proj = to_columns(jnp.stack([grad_query, grad_key, grad_value]).astype(jnp.bfloat16))
    grad_qkv = jnp.einsum("td,stc->sdc", wide_one, grad_proj, preferred_element_type=jnp.float32)
    grad_ln_one = narrow(
        jnp.einsum("stc,sdc->td", grad_proj, qkv_full, preferred_element_type=jnp.float32)
    )
    grad_norm_one, grad_gain_one, grad_shift_one = norm_backward(
        grad_ln_one, normed_one, inv_one, gain_one
    )
    grad_input = grad_mid + grad_norm_one
    proj_sums = jnp.sum(grad_proj, axis=1, dtype=jnp.float32)
    vector_parts = (
        grad_gain_one,
        grad_shift_one,
        jnp.stack([proj_sums[0], proj_sums[2]]),
        jnp.sum(grad_mid, axis=0),
        grad_gain_two,
        grad_shift_two,
        jnp.sum(grad_pre, axis=0, dtype=jnp.float32),
        jnp.sum(grad_rows, axis=0),
    )
    return (hidden_out, grad_input, (grad_qkv, grad_out, grad_in, grad_down), vector_parts)


def tile_grid(vector, row_count):
    return jnp.broadcast_to(vector[None], (row_count,) + vector.shape)


def grid_reduce(partials, vector_parts):
    row_count = lax.axis_size("row")
    qkv_part, out_part, in_part, down_part = partials
    qkv_blocks = qkv_part.reshape(3, row_count, -1, qkv_part.shape[2]).transpose(1, 0, 2, 3)
    out_blocks = out_part.reshape(out_part.shape[0], row_count, -1).transpose(1, 0, 2)
    in_blocks = in_part.reshape(row_count, -1, in_part.shape[1])
    down_blocks = down_part.reshape(down_part.shape[0], row_count, -1).transpose(1, 0, 2)
    tiled = [tile_grid(vector, row_count) for vector in vector_parts]
    reduced = (
        lax.psum_scatter(qkv_blocks, "row", scatter_dimension=0, tiled=True),
        lax.psum_scatter(out_blocks, "row", scatter_dimension=0, tiled=True),
        lax.psum_scatter(in_blocks, "row", scatter_dimension=0, tiled=True),
        lax.psum_scatter(down_blocks, "row", scatter_dimension=0, tiled=True),
        lax.psum_scatter(tiled[0], "row", scatter_dimension=0, tiled=True),
        lax.psum_scatter(tiled[1], "row", scatter_dimension=0, tiled=True),
        lax.psum_scatter(tiled[2], "row", scatter_dimension=0, tiled=True),
        lax.psum_scatter(tiled[3], "row", scatter_dimension=0, tiled=True),
        lax.psum_scatter(tiled[4], "row", scatter_dimension=0, tiled=True),
        lax.psum_scatter(tiled[5], "row", scatter_dimension=0, tiled=True),
        lax.psum_scatter(tiled[6], "row", scatter_dimension=0, tiled=True),
        lax.psum_scatter(tiled[7], "row", scatter_dimension=0, tiled=True),
    )
    return tuple((piece[0] for piece in reduced))


def local(
    hidden_in,
    lengths,
    ln1_gain,
    ln1_shift,
    qkv_weight,
    qv_bias,
    out_weight,
    out_bias,
    ln2_gain,
    ln2_shift,
    in_weight,
    in_bias,
    down_weight,
    down_bias,
    cotangent,
):
    col_count = lax.axis_size("col")
    token_rows = jnp.transpose(hidden_in)
    cot_rows = jnp.transpose(cotangent)
    rows_block = token_rows.shape[0] // MICRO
    weights = (
        lax.all_gather(qkv_weight, "row", axis=1, tiled=True),
        lax.all_gather(out_weight, "row", axis=1, tiled=True),
        lax.all_gather(in_weight, "row", axis=0, tiled=True),
        lax.all_gather(down_weight, "row", axis=1, tiled=True),
    )
    vectors = (ln1_gain, ln1_shift, qv_bias, out_bias, ln2_gain, ln2_shift, in_bias, down_bias)
    clip_slot = lax.axis_index("col") // GROUP
    outputs = []
    input_grads = []
    totals = None
    running = None
    for micro_index in range(MICRO):
        input_rows = token_rows[micro_index * rows_block : (micro_index + 1) * rows_block]
        grad_rows = cot_rows[micro_index * rows_block : (micro_index + 1) * rows_block]
        clip_id = (lax.axis_index("row") * MICRO + micro_index) * (col_count // GROUP) + clip_slot
        valid_len = lax.dynamic_index_in_dim(lengths, clip_id, keepdims=False)
        out_rows, back_rows, partials, vector_parts = layer_pass(
            input_rows, grad_rows, weights, vectors, valid_len
        )
        outputs.append(out_rows)
        input_grads.append(back_rows)
        current = (partials, vector_parts)
        running = current if running is None else jax.tree.map(jnp.add, running, current)
    totals = grid_reduce(running[0], running[1])
    (
        grad_qkv,
        grad_out,
        grad_in,
        grad_down,
        grad_gain_one,
        grad_shift_one,
        grad_qv,
        grad_out_shift,
        grad_gain_two,
        grad_shift_two,
        grad_in_shift,
        grad_down_shift,
    ) = totals
    hidden_out = jnp.transpose(jnp.concatenate(outputs, axis=0))
    hidden_grad = jnp.transpose(jnp.concatenate(input_grads, axis=0))
    return (
        hidden_out,
        hidden_grad,
        grad_gain_one,
        grad_shift_one,
        grad_qkv,
        grad_qv,
        grad_out,
        grad_out_shift,
        grad_gain_two,
        grad_shift_two,
        grad_in,
        grad_in_shift,
        grad_down,
        grad_down_shift,
    )


CLIP = 1024
FF = 5120
OWN = D // 4
UNITS = FF // 4
HALF = D // 2
BLOCK = 256
STEPS = CLIP // BLOCK
BF = jnp.bfloat16
F32 = jnp.float32


def swap_core(values):
    return lax.ppermute(values, "row", [(i, i ^ 1) for i in range(4)])


def swap_y(values):
    return lax.ppermute(values, "row", [(i, i ^ 2) for i in range(4)])


def swap_x(values):
    return lax.ppermute(values, "col", [(i, i ^ 1) for i in range(8)])


def swap_zl(values):
    return lax.ppermute(values, "col", [(i, i ^ 2) for i in range(8)])


def swap_zh(values):
    return lax.ppermute(values, "col", [(i, i ^ 4) for i in range(8)])


def pick(values, index, axis=0):
    return lax.dynamic_index_in_dim(values, index, axis, keepdims=False)


def mm(left, right, left_dim, right_dim):
    return lax.dot_general(
        left, right, (((left_dim,), (right_dim,)), ((), ())), preferred_element_type=F32
    )


def shaped(dims, kind=BF):
    return jax.ShapeDtypeStruct(dims, kind)


def spots_spec():
    return pl.BlockSpec(memory_space=pltpu.SMEM)


def fixed(array):
    rank = len(array.shape)
    return pl.BlockSpec(array.shape, lambda i: (0,) * rank)


def tokens_spec(dims):
    lead = tuple(dims[:-1])
    return pl.BlockSpec(lead + (BLOCK,), lambda i: (0,) * len(lead) + (i,))


def cost(flops, moved):
    return pl.CostEstimate(flops=1, transcendentals=0, bytes_accessed=1)


def attend_kernel(len_ref, q_ref, k_ref, v_ref, out_ref, lse_ref):
    scores = mm(k_ref[...], q_ref[...], 0, 0) * (HEAD_DIM**-0.5)
    live = lax.broadcasted_iota(jnp.int32, scores.shape, 0) < len_ref[0]
    scores = jnp.where(live, scores, -1e30)
    top = jnp.max(scores, axis=0, keepdims=True)
    weights = jnp.exp(scores - top)
    total = jnp.sum(weights, axis=0, keepdims=True)
    prob_low = (weights * (1.0 / total)).astype(BF)
    out_ref[...] = mm(v_ref[...], prob_low, 1, 0).astype(BF)
    lse_ref[...] = top + jnp.log(total)


def head_specs(block):
    return [
        pl.BlockSpec((None, None, HEAD_DIM, block), lambda h, i, n: (h, 0, 0, i)),
        pl.BlockSpec((None, None, HEAD_DIM, CLIP), lambda h, i, n: (h, 1, 0, 0)),
        pl.BlockSpec((None, HEAD_DIM, CLIP), lambda h, i, n: (h, 0, 0)),
    ]


def attend_clip(qk, values, clip_len, block):
    return pl.pallas_call(
        attend_kernel,
        grid_spec=pltpu.PrefetchScalarGridSpec(
            num_scalar_prefetch=1,
            grid=(4, CLIP // block),
            in_specs=head_specs(block),
            out_specs=[
                pl.BlockSpec((None, HEAD_DIM, block), lambda h, i, n: (h, 0, i)),
                pl.BlockSpec((None, 1, block), lambda h, i, n: (h, 0, i)),
            ],
        ),
        out_shape=[shaped((4, HEAD_DIM, CLIP)), shaped((4, 1, CLIP), F32)],
        cost_estimate=cost(16 * CLIP * CLIP * HEAD_DIM, 16 * HEAD_DIM * CLIP * 2),
        name="attend_clip",
    )(clip_len, qk, qk, values)


def attend_back_kernel(
    len_ref, q_ref, k_ref, v_ref, lse_ref, grad_ref, *refs
):
    gqk_ref, gv_ref = refs[-2:]
    scale = HEAD_DIM**-0.5
    queries, keys, values, grad = q_ref[...], k_ref[...], v_ref[...], grad_ref[...]
    scores = mm(keys, queries, 0, 0) * scale
    live = lax.broadcasted_iota(jnp.int32, scores.shape, 0) < len_ref[0]
    scores = jnp.where(live, scores, -1e30)
    probs = jnp.exp(scores - lse_ref[...])
    grad_probs = mm(values, grad, 0, 0)
    row_dot = jnp.sum(probs * grad_probs, axis=0, keepdims=True)
    score_low = (probs * (grad_probs - row_dot)).astype(BF)
    grad_query = mm(keys, score_low, 1, 0) * scale
    grad_key = mm(queries, score_low, 1, 1)
    grad_value = mm(grad, probs.astype(BF), 1, 1)
    gqk_ref[0] = grad_query.astype(BF)
    gqk_ref[1] = (grad_key * scale).astype(BF)
    gv_ref[...] = grad_value.astype(BF)


def attend_clip_back(qk, values, log_sum, grad_attended, clip_len, first, earlier=()):
    def heads(*dims):
        return pl.BlockSpec(
            (None,) + dims, lambda h, n: (h + first,) + (0,) * len(dims)
        )

    def part(i):
        return pl.BlockSpec((None, None, HEAD_DIM, CLIP), lambda h, n: (h + first, i, 0, 0))

    operands = (qk, qk, values, log_sum, grad_attended)
    return pl.pallas_call(
        attend_back_kernel,
        grid_spec=pltpu.PrefetchScalarGridSpec(
            num_scalar_prefetch=1,
            grid=(2,),
            in_specs=[
                part(0),
                part(1),
                heads(HEAD_DIM, CLIP),
                heads(1, CLIP),
                heads(HEAD_DIM, CLIP),
            ]
            + [pl.BlockSpec(memory_space=pl.ANY)] * len(earlier),
            out_specs=[heads(2, HEAD_DIM, CLIP), heads(HEAD_DIM, CLIP)],
        ),
        out_shape=[shaped((4, 2, HEAD_DIM, CLIP)), shaped((4, HEAD_DIM, CLIP))],
        input_output_aliases={6: 0, 7: 1} if earlier else {},
        cost_estimate=cost(20 * CLIP * CLIP * HEAD_DIM, 16 * HEAD_DIM * CLIP * 2),
        name="attend_clip_back",
    )(clip_len, *operands, *earlier)


WIDE = 384


def order_hot(core):
    place = lax.broadcasted_iota(jnp.int32, (OWN, OWN), 1)
    stored = lax.broadcasted_iota(jnp.int32, (OWN, OWN), 0)
    hot = jnp.zeros((OWN, OWN), jnp.bool_)
    for chunk in range(4):
        source = (2 * (chunk >> 1) + (core ^ (chunk & 1))) * HEAD_DIM
        inside = (place >= chunk * HEAD_DIM) & (place < (chunk + 1) * HEAD_DIM)
        hot = hot | (inside & (stored - source == place - chunk * HEAD_DIM))
    return jnp.where(hot, 1.0, 0.0).astype(BF)


def whole():
    return pl.BlockSpec(memory_space=pltpu.VMEM)


def prepare_kernel(spots_ref, qkv_ref, out_ref, in_ref, down_ref, kept_ref, sent_ref):
    c = spots_ref[0]
    for ref, core in ((kept_ref, c), (sent_ref, 1 - c)):
        hot = order_hot(core)

        def half(value, count):
            return jnp.where(core == 0, value[:count], value[count:])

        for s in range(3):
            value = half(mm(qkv_ref[s], hot, 1, 0), HEAD_DIM)
            ref[s * HEAD_DIM : (s + 1) * HEAD_DIM, :OWN] = value.astype(BF)
        value = half(mm(out_ref[...], hot, 1, 0), HEAD_DIM)
        ref[3 * HEAD_DIM : OWN, :OWN] = value.astype(BF)
        ref[OWN : 2 * OWN, :OWN] = half(mm(in_ref[...], hot, 0, 0), OWN).astype(BF)
        ref[2 * OWN :, :OWN] = half(mm(down_ref[...], hot, 0, 0), OWN).astype(BF)
        ref[:, OWN:] = jnp.zeros((3 * OWN, WIDE - OWN), BF)


def prepare(spots, qkv_turned, out_weight, in_weight, down_turned):
    return pl.pallas_call(
        prepare_kernel,
        in_specs=[spots_spec()] + [whole()] * 4,
        out_specs=[whole()] * 2,
        out_shape=[shaped((3 * OWN, WIDE))] * 2,
        cost_estimate=cost(8 * 3 * OWN * OWN * OWN, 4 * 3 * OWN * OWN * 2),
        name="prepare_weights",
    )(spots, qkv_turned, out_weight, in_weight, down_turned)


def lanes_kernel(spots_ref, kept_ref, got_ref, *out_refs):
    def write(near_ref, far_ref):
        start = 0
        for ref in out_refs:
            rows = slice(start, start + ref.shape[0])
            ref[:, :OWN] = near_ref[rows, :OWN]
            ref[:, OWN:] = far_ref[rows, :OWN]
            start += ref.shape[0]

    @pl.when(spots_ref[1] == 1)
    def _():
        write(kept_ref, got_ref)

    @pl.when(spots_ref[1] == 0)
    def _():
        write(got_ref, kept_ref)


def join_lanes(spots, kept, got):
    return pl.pallas_call(
        lanes_kernel,
        in_specs=[spots_spec(), whole(), whole()],
        out_specs=[whole()] * 4,
        out_shape=[shaped((n, HALF)) for n in (OWN // 2, OWN // 2, OWN, OWN)],
        cost_estimate=cost(0, 4 * 3 * OWN * OWN * 2),
        name="join_lanes",
    )(spots, kept, got)


def two_terms(value):
    high = value.astype(BF)
    return high, (value - high.astype(F32)).astype(BF)


def store_ff_kernel(spots_ref, up_ref, down_ref, kept_ref, sent_ref):
    hot = order_hot(spots_ref[0])
    is_near = spots_ref[1] == 1
    for place, total_ref in ((0, up_ref), (1, down_ref)):
        near, far = total_ref[:, :OWN], total_ref[:, OWN:]
        lanes = slice(place * OWN, (place + 1) * OWN)
        for ref, value in (
            (kept_ref, jnp.where(is_near, near, far)),
            (sent_ref, jnp.where(is_near, far, near)),
        ):
            high, rest = two_terms(value)
            ref[:, lanes] = mm(hot, high, 1, 1) + mm(hot, rest, 1, 1)


def store_ff(spots, up_total, down_total):
    return pl.pallas_call(
        store_ff_kernel,
        in_specs=[spots_spec()] + [whole()] * 2,
        out_specs=[whole()] * 2,
        out_shape=[shaped((OWN, HALF), F32)] * 2,
        cost_estimate=cost(16 * OWN * OWN * OWN, 16 * OWN * OWN * 4),
        name="store_ff",
    )(spots, up_total, down_total)


def join_ff_kernel(spots_ref, kept_ref, got_ref, up_ref, down_ref):
    def write(first_ref, second_ref):
        for place, ref in ((0, up_ref), (1, down_ref)):
            lanes = slice(place * OWN, (place + 1) * OWN)
            ref[:, :OWN] = first_ref[:, lanes]
            ref[:, OWN:] = second_ref[:, lanes]

    @pl.when(spots_ref[0] == 0)
    def _():
        write(kept_ref, got_ref)

    @pl.when(spots_ref[0] == 1)
    def _():
        write(got_ref, kept_ref)


def join_ff(spots, kept, got):
    return pl.pallas_call(
        join_ff_kernel,
        in_specs=[spots_spec()] + [whole()] * 2,
        out_specs=[whole()] * 2,
        out_shape=[shaped((OWN, HALF), F32)] * 2,
        cost_estimate=cost(0, 16 * OWN * OWN * 4),
        name="join_ff",
    )(spots, kept, got)


def store_qkvo_kernel(spots_ref, qk_ref, vo_ref, kept_ref, sent_ref):
    hot = order_hot(spots_ref[0])
    is_near = spots_ref[1] == 1
    for place, total_ref in ((0, qk_ref), (1, vo_ref)):
        near, far = total_ref[:, :OWN], total_ref[:, OWN:]
        rows = slice(place * 2 * HEAD_DIM, (place + 1) * 2 * HEAD_DIM)
        for ref, value in (
            (kept_ref, jnp.where(is_near, near, far)),
            (sent_ref, jnp.where(is_near, far, near)),
        ):
            high, rest = two_terms(value)
            ref[rows, :OWN] = mm(high, hot, 1, 1) + mm(rest, hot, 1, 1)
    kept_ref[:, OWN:] = jnp.zeros((OWN, WIDE - OWN), F32)
    sent_ref[:, OWN:] = jnp.zeros((OWN, WIDE - OWN), F32)


def store_qkvo(spots, qk_total, vo_total):
    return pl.pallas_call(
        store_qkvo_kernel,
        in_specs=[spots_spec()] + [whole()] * 2,
        out_specs=[whole()] * 2,
        out_shape=[shaped((OWN, WIDE), F32)] * 2,
        cost_estimate=cost(8 * OWN * OWN * OWN, 16 * OWN * OWN * 4),
        name="store_qkvo",
    )(spots, qk_total, vo_total)


def join_qkvo_kernel(spots_ref, kept_ref, got_ref, qkv_ref, out_ref):
    def write(first_ref, second_ref):
        for place, ref in ((0, first_ref), (1, second_ref)):
            rows = slice(place * HEAD_DIM, (place + 1) * HEAD_DIM)
            for s in range(3):
                qkv_ref[s, rows] = ref[s * HEAD_DIM : (s + 1) * HEAD_DIM, :OWN]
            out_ref[rows] = ref[3 * HEAD_DIM : 4 * HEAD_DIM, :OWN]

    @pl.when(spots_ref[0] == 0)
    def _():
        write(kept_ref, got_ref)

    @pl.when(spots_ref[0] == 1)
    def _():
        write(got_ref, kept_ref)


def join_qkvo(spots, kept, got):
    return pl.pallas_call(
        join_qkvo_kernel,
        in_specs=[spots_spec()] + [whole()] * 2,
        out_specs=[whole()] * 2,
        out_shape=[shaped((3, 2 * HEAD_DIM, OWN), F32), shaped((2 * HEAD_DIM, OWN), F32)],
        cost_estimate=cost(0, 8 * OWN * OWN * 4),
        name="join_qkvo",
    )(spots, kept, got)


TAIL = 8


def split_kernel(spots_ref, hid_ref, cot_ref, hk_ref, hs_ref, ck_ref, cs_ref):
    c = spots_ref[0]
    data, tails, cots = [], [], []
    for half in (0, 1):
        rows = slice(half * HEAD_DIM, (half + 1) * HEAD_DIM)
        value = hid_ref[rows]
        mean = jnp.mean(value, axis=0, keepdims=True)
        data.append(value - mean)
        high = mean.astype(BF).astype(F32)
        middle = (mean - high).astype(BF).astype(F32)
        low = mean - high - middle
        spot = lax.broadcasted_iota(jnp.int32, (TAIL, value.shape[1]), 0)
        tails.append(
            jnp.where(
                spot == 0, high, jnp.where(spot == 1, middle, jnp.where(spot == 2, low, 0.0))
            )
        )
        cots.append(cot_ref[rows])
    for ref, cot, first in ((hk_ref, ck_ref, c == 0), (hs_ref, cs_ref, c == 1)):
        ref[:HEAD_DIM] = jnp.where(first, data[0], data[1]).astype(BF)
        ref[HEAD_DIM:] = jnp.where(first, tails[0], tails[1]).astype(BF)
        cot[...] = jnp.where(first, cots[0], cots[1]).astype(BF)


def split(spots, hidden_in, cotangent):
    block = pl.BlockSpec((2 * HEAD_DIM, CLIP // 2), lambda i: (0, i))
    specs = [
        pl.BlockSpec((n, CLIP // 2), lambda i: (0, i))
        for n in (HEAD_DIM + TAIL, HEAD_DIM + TAIL, HEAD_DIM, HEAD_DIM)
    ]
    return pl.pallas_call(
        split_kernel,
        grid=(4,),
        in_specs=[spots_spec(), block, block],
        out_specs=specs,
        out_shape=[
            shaped((n, 2 * CLIP)) for n in (HEAD_DIM + TAIL, HEAD_DIM + TAIL, HEAD_DIM, HEAD_DIM)
        ],
        cost_estimate=cost(0, 8 * HEAD_DIM * 2 * CLIP * 4),
        name="split_in",
    )(spots, hidden_in, cotangent)


def deal_kernel(spots_ref, kept_ref, got_ref, here_ref, send_ref):
    for is_own in (0, 1):
        for x in (0, 1):

            @pl.when((spots_ref[2] == is_own) & (spots_ref[3] == x))
            def _(is_own=is_own, x=x):
                pair = (kept_ref, got_ref) if is_own else (got_ref, kept_ref)
                near = slice(x * CLIP, (x + 1) * CLIP)
                away = slice((1 - x) * CLIP, (2 - x) * CLIP)
                for i in (0, 1):
                    here_ref[i] = pair[i][:, near]
                    send_ref[i] = pair[i][:, away]


def deal(spots, kept, got):
    return pl.pallas_call(
        deal_kernel,
        in_specs=[spots_spec(), whole(), whole()],
        out_specs=[whole()] * 2,
        out_shape=[shaped((2, kept.shape[0], CLIP))] * 2,
        cost_estimate=cost(0, 8 * kept.shape[0] * CLIP * 2),
        name="deal",
    )(spots, kept, got)


def place_kernel(spots_ref, here_ref, there_ref, far_ref, own_ref, *stats_ref):
    grid = ((here_ref, 0), (there_ref, 0)), ((far_ref, 0), (far_ref, 1))
    for same in (0, 1):
        for x in (0, 1):

            @pl.when((spots_ref[4] == same) & (spots_ref[3] == x))
            def _(same=same, x=x):
                for i in (0, 1):
                    for j in (0, 1):
                        ref, k = grid[i if same else 1 - i][j if x == 0 else 1 - j]
                        if stats_ref:
                            tail = ref[k, HEAD_DIM:].astype(F32)
                            mean = tail[0:1] + tail[1:2] + tail[2:3]
                            own_ref[i, j] = ref[k, :HEAD_DIM].astype(F32) + mean
                        else:
                            own_ref[i, j] = ref[k]

    if stats_ref:
        values = own_ref[...].reshape(OWN, own_ref.shape[-1])
        mean = jnp.mean(values, axis=0, keepdims=True)
        off = values - mean
        stats_ref[0][0:1] = mean
        stats_ref[0][1:2] = jnp.sum(off * off, axis=0, keepdims=True)


def place(spots, here, there, far, with_stats):
    rows = here.shape[1]
    own = (2, 2, HEAD_DIM, CLIP)
    outs = [(own, F32), ((2, CLIP), F32)] if with_stats else [(own, BF)]
    return pl.pallas_call(
        place_kernel,
        in_specs=[spots_spec()] + [whole()] * 3,
        out_specs=[whole()] * len(outs),
        out_shape=[shaped(dims, kind) for dims, kind in outs],
        cost_estimate=cost(0, 8 * rows * CLIP * 6),
        name="place_in",
    )(spots, here, there, far)


def leave_kernel(spots_ref, own_ref, near_ref, far_ref):
    for same in (0, 1):
        for x in (0, 1):

            @pl.when((spots_ref[4] == same) & (spots_ref[3] == x))
            def _(same=same, x=x):
                for j in (0, 1):
                    k = j if x == 0 else 1 - j
                    near_ref[j] = own_ref[1 - same, k].astype(BF)
                    far_ref[j] = own_ref[same, k].astype(BF)


def leave(spots, own):
    dims = (2, HEAD_DIM, CLIP)
    return pl.pallas_call(
        leave_kernel,
        in_specs=[spots_spec(), whole()],
        out_specs=[whole()] * 2,
        out_shape=[shaped(dims)] * 2,
        cost_estimate=cost(0, 4 * HEAD_DIM * CLIP * 6),
        name="leave",
    )(spots, own)


def undeal_kernel(spots_ref, near_ref, far_ref, there_ref, kept_ref, sent_ref):
    for is_own in (0, 1):
        for x in (0, 1):

            @pl.when((spots_ref[2] == is_own) & (spots_ref[3] == x))
            def _(is_own=is_own, x=x):
                own = slice(x * CLIP, (x + 1) * CLIP)
                other = slice((1 - x) * CLIP, (2 - x) * CLIP)
                pair = (kept_ref, sent_ref) if is_own else (sent_ref, kept_ref)
                for k, ref in enumerate((near_ref, far_ref)):
                    pair[k][:, own] = ref[0]
                    pair[k][:, other] = there_ref[k]


def undeal(spots, near, far, there):
    dims = (HEAD_DIM, 2 * CLIP)
    return pl.pallas_call(
        undeal_kernel,
        in_specs=[spots_spec()] + [whole()] * 3,
        out_specs=[whole()] * 2,
        out_shape=[shaped(dims)] * 2,
        cost_estimate=cost(0, 16 * HEAD_DIM * CLIP * 2),
        name="undeal",
    )(spots, near, far, there)


def finish_kernel(spots_ref, kept_ref, got_ref, base_ref, shift_ref, out_ref):
    c = spots_ref[0]
    kept, got = kept_ref[...].astype(F32), got_ref[...].astype(F32)
    for half in (0, 1):
        rows = slice(half * HEAD_DIM, (half + 1) * HEAD_DIM)
        value = jnp.where(c == half, kept, got)
        out_ref[rows] = base_ref[rows] + shift_ref[rows] + value


def finish(spots, kept, got, base, shift):
    spec = pl.BlockSpec((HEAD_DIM, CLIP // 2), lambda i: (0, i))
    wide = pl.BlockSpec((2 * HEAD_DIM, CLIP // 2), lambda i: (0, i))
    return pl.pallas_call(
        finish_kernel,
        grid=(4,),
        in_specs=[spots_spec(), spec, spec, wide, fixed(shift)],
        out_specs=wide,
        out_shape=shaped(base.shape, F32),
        cost_estimate=cost(0, 8 * HEAD_DIM * 2 * CLIP * 4),
        name="finish",
    )(spots, kept, got, base, shift)


def y_last(pair, yr, rows=slice(None)):
    return jnp.concatenate([pair[yr][xr, zhr, rows] for xr in (0, 1) for zhr in (0, 1)])


def x_last(pair, yr, rows=slice(None)):
    return jnp.concatenate([pair[xr][yr, zhr, rows] for xr in (0, 1) for zhr in (0, 1)])


def wide_rows(half, pair, rows=slice(None)):
    return jnp.concatenate([half(pair, 0, rows), half(pair, 1, rows)], axis=1)


def join_blocks(refs):
    return jnp.concatenate(
        [
            refs[2 * zlr + cr][yr, xr]
            for yr in (0, 1)
            for zlr in (0, 1)
            for xr in (0, 1)
            for cr in (0, 1)
        ]
    )


HEAD_ROWS = slice(0, HEAD_DIM)
OUT_ROWS = slice(HEAD_DIM, 2 * HEAD_DIM)


def project_kernel(b0, b1, b2, b3, qk0, qk1, vo0, vo1, qs_ref, vs_ref, qk_ref, v_ref, wide_ref):
    wide = join_blocks((b0, b1, b2, b3))
    wide_ref[...] = wide
    result = mm(wide_rows(y_last, (qk0, qk1)), wide, 1, 0)
    for t in range(4):
        first = t * 2 * HEAD_DIM
        queries = result[first : first + HEAD_DIM] + qs_ref[t]
        qk_ref[t, 0] = queries.astype(BF)
        qk_ref[t, 1] = result[first + HEAD_DIM : first + 2 * HEAD_DIM].astype(BF)
    result = mm(wide_rows(x_last, (vo0, vo1), HEAD_ROWS), wide, 1, 0)
    for t in range(4):
        v_ref[t] = (result[t * HEAD_DIM : (t + 1) * HEAD_DIM] + vs_ref[t]).astype(BF)


def project(blocks, qk, vo, q_shift, v_shift):
    operands = (*blocks, *qk, *vo, q_shift, v_shift)
    outs = ((4, 2, HEAD_DIM, CLIP), (4, HEAD_DIM, CLIP), (D, CLIP))
    return pl.pallas_call(
        project_kernel,
        grid=(STEPS,),
        in_specs=[tokens_spec(b.shape) for b in blocks] + [fixed(a) for a in operands[4:]],
        out_specs=[tokens_spec(dims) for dims in outs],
        out_shape=[shaped(dims) for dims in outs],
        cost_estimate=cost(2 * 3 * OWN * D * CLIP, 4 * D * CLIP * 2),
        name="project",
    )(*operands)


def up_kernel(b0, b1, b2, b3, up0, up1, shift_ref, act_ref, slope_ref, wide_ref):
    wide = join_blocks((b0, b1, b2, b3))
    wide_ref[...] = wide
    for xr in (0, 1):
        for zhr in (0, 1):
            first = (2 * xr + zhr) * OWN
            rows = slice(first, first + OWN)
            weight = jnp.concatenate([up0[xr, zhr], up1[xr, zhr]], axis=1)
            pre = mm(weight, wide, 1, 0) + shift_ref[rows]
            cdf = 0.5 * (1.0 + lax.erf(pre * (0.5**0.5)))
            act_ref[rows] = (pre * cdf).astype(BF)
            slope_ref[rows] = cdf + pre * jnp.exp(-0.5 * pre * pre) * 0.3989422804014327


def up_project(blocks, up, in_shift):
    operands = (*blocks, *up, in_shift)
    outs = (((UNITS, CLIP), BF), ((UNITS, CLIP), F32), ((D, CLIP), BF))
    return pl.pallas_call(
        up_kernel,
        grid=(STEPS,),
        in_specs=[tokens_spec(b.shape) for b in blocks] + [fixed(a) for a in operands[4:]],
        out_specs=[tokens_spec(dims) for dims, _ in outs],
        out_shape=[shaped(dims, kind) for dims, kind in outs],
        cost_estimate=cost(2 * UNITS * D * CLIP, 6 * D * CLIP * 2),
        name="up_project",
    )(*operands)


def grad_act_kernel(b0, b1, b2, b3, down0, down1, slope_ref, out_ref, wide_ref):
    wide = join_blocks((b0, b1, b2, b3))
    wide_ref[...] = wide
    for xr in (0, 1):
        for zhr in (0, 1):
            first = (2 * xr + zhr) * OWN
            rows = slice(first, first + OWN)
            pair = (down0, down1)[xr]
            weight = jnp.concatenate([pair[0, zhr], pair[1, zhr]], axis=1)
            out_ref[rows] = (mm(weight, wide, 1, 0) * slope_ref[rows]).astype(BF)


def grad_act(blocks, down, slope):
    operands = (*blocks, *down, slope)
    outs = ((UNITS, CLIP), (D, CLIP))
    return pl.pallas_call(
        grad_act_kernel,
        grid=(STEPS,),
        in_specs=[tokens_spec(b.shape) for b in blocks]
        + [fixed(a) for a in down]
        + [tokens_spec(slope.shape)],
        out_specs=[tokens_spec(dims) for dims in outs],
        out_shape=[shaped(dims) for dims in outs],
        cost_estimate=cost(2 * UNITS * D * CLIP, 6 * D * CLIP * 2),
        name="grad_act",
    )(*operands)


def grad_attended_kernel(b0, b1, b2, b3, vo0, vo1, out_ref, wide_ref):
    wide = join_blocks((b0, b1, b2, b3))
    wide_ref[...] = wide
    result = mm(wide_rows(x_last, (vo0, vo1), OUT_ROWS), wide, 1, 0)
    for t in range(4):
        out_ref[t] = result[t * HEAD_DIM : (t + 1) * HEAD_DIM].astype(BF)


def grad_attended_of(blocks, vo):
    outs = ((4, HEAD_DIM, CLIP), (D, CLIP))
    return pl.pallas_call(
        grad_attended_kernel,
        grid=(STEPS,),
        in_specs=[tokens_spec(b.shape) for b in blocks] + [fixed(a) for a in vo],
        out_specs=[tokens_spec(dims) for dims in outs],
        out_shape=[shaped(dims) for dims in outs],
        cost_estimate=cost(2 * OWN * D * CLIP, 4 * D * CLIP * 2),
        name="grad_attended",
    )(*blocks, *vo)


def fold_kernel(fill, counts, *refs):
    sources, values = refs[: counts[0]], refs[counts[0] : sum(counts)]
    keep_ref, send_ref, turned_ref = refs[sum(counts) :]

    @pl.when(pl.program_id(0) == 0)
    def _():
        for yr in (0, 1):
            turned_ref[yr * HALF : (yr + 1) * HALF] = jnp.transpose(fill(sources, yr))

    value = jnp.concatenate([ref[...].reshape(-1, BLOCK) for ref in values])
    for yr in (0, 1):
        result = mm(turned_ref[yr * HALF : (yr + 1) * HALF], value, 1, 0)
        for spot in range(8):
            part = result[spot * HEAD_DIM : (spot + 1) * HEAD_DIM]
            zlr, xr, cr = spot >> 2, spot >> 1 & 1, spot & 1
            if cr == 0:
                keep_ref[zlr, yr, xr] = part
            else:
                send_ref[zlr, yr, xr] = part.astype(BF)


def fold(fill, sources, values, name):
    depth = sum(v.size // CLIP for v in values)
    dims = (2, 2, 2, HEAD_DIM, CLIP)
    return pl.pallas_call(
        functools.partial(fold_kernel, fill, (len(sources), len(values))),
        grid=(STEPS,),
        in_specs=[fixed(a) for a in sources] + [tokens_spec(v.shape) for v in values],
        out_specs=[tokens_spec(dims)] * 2,
        out_shape=[shaped(dims, F32), shaped(dims)],
        scratch_shapes=[pltpu.VMEM((D, depth), BF)],
        cost_estimate=cost(2 * D * depth * CLIP, 6 * D * CLIP * 2),
        name=name,
    )(*sources, *values)


def fill_out(sources, yr):
    return x_last(sources, yr, OUT_ROWS)


def fill_up(sources, yr):
    return y_last(sources, yr)


def fill_down(sources, yr):
    return x_last(sources, yr)


def fill_project(sources, yr):
    return jnp.concatenate([y_last(sources[:2], yr), x_last(sources[2:], yr, HEAD_ROWS)])


def pair_y_kernel(left_ref, right_ref, keep_ref, send_ref):
    result = mm(left_ref[0], right_ref[...], 1, 1)
    keep_ref[0] = result[:, :HALF]
    send_ref[0] = result[:, HALF:].astype(BF)


def grad_y_first(left, right, name):
    rows = left.shape[1]
    dims = (4, rows, HALF)
    spec = pl.BlockSpec((1, rows, HALF), lambda i: (i, 0, 0))
    return pl.pallas_call(
        pair_y_kernel,
        grid=(4,),
        in_specs=[pl.BlockSpec((1, rows, CLIP), lambda i: (i, 0, 0)), fixed(right)],
        out_specs=[spec] * 2,
        out_shape=[shaped(dims, F32), shaped(dims)],
        cost_estimate=cost(2 * 4 * rows * D * CLIP, 4 * rows * D * 6),
        name=name,
    )(left, right)


def pair_x_kernel(count, *refs):
    keep_ref, send_ref = refs[2 * count :]
    start = 0
    for left_ref, right_ref in zip(refs[:count], refs[count : 2 * count]):
        rows = slice(start, start + left_ref.shape[2])
        start += left_ref.shape[2]
        for xr in (0, 1):
            result = mm(left_ref[xr, 0], right_ref[...], 1, 1)
            for yr in (0, 1):
                part = result[:, yr * HALF : (yr + 1) * HALF]
                if xr == 0:
                    keep_ref[yr, 0, rows] = part
                else:
                    send_ref[yr, 0, rows] = part.astype(BF)


def grad_x_first(lefts, rights, name):
    rows = sum(v.shape[2] for v in lefts)
    dims = (2, 2, rows, HALF)
    spec = pl.BlockSpec((2, 1, rows, HALF), lambda i: (0, i, 0, 0))
    return pl.pallas_call(
        functools.partial(pair_x_kernel, len(lefts)),
        grid=(2,),
        in_specs=[pl.BlockSpec((2, 1) + v.shape[2:], lambda i: (0, i, 0, 0)) for v in lefts]
        + [fixed(v) for v in rights],
        out_specs=[spec] * 2,
        out_shape=[shaped(dims, F32), shaped(dims)],
        cost_estimate=cost(2 * 4 * rows * D * CLIP, 4 * rows * D * 6),
        name=name,
    )(*lefts, *rights)


def token_stats(values):
    mean = jnp.mean(values, axis=0)
    off = values - mean
    return jnp.stack([mean, jnp.sum(off * off, axis=0)])


def swap_both(values):
    route = [(8 * r + q, 8 * (r ^ 1) + (q ^ 2)) for r in range(4) for q in range(8)]
    return lax.ppermute(values, ("row", "col"), route)


def group_round(values):
    return values, swap_core(values), swap_zl(values), swap_both(values)


def merge_stats(stats, count):
    stats = group_round(stats)
    mean = sum(s[0] for s in stats) * 0.25
    total = sum(s[1] + count * jnp.square(s[0] - mean) for s in stats)
    return mean, total / (4 * count)


def after(values, *others):
    return lax.optimization_barrier((values, others))[0]


def local_clip(
    hidden_in,
    lengths,
    ln1_gain,
    ln1_shift,
    qkv_weight,
    qv_bias,
    out_weight,
    out_bias,
    ln2_gain,
    ln2_shift,
    in_weight,
    in_bias,
    down_weight,
    down_bias,
    cotangent,
):
    row, col = lax.axis_index("row"), lax.axis_index("col")
    y, c = row // 2, row % 2
    zh, zl, x = col // 4, col // 2 % 2, col % 2
    same_zy = y == zh
    spots = jnp.stack([c, zl == c, zh == c, x, same_zy]).astype(jnp.int32)

    def flip(grid):
        grid = jnp.where(same_zy, grid, grid[::-1])
        return jnp.where(x == 0, grid, grid[:, ::-1])

    def fold_cores(parts):
        got = swap_core(parts[1])
        return parts[0][0] + got[0], (parts[0][1] + got[1]).astype(BF)

    kept, sent = prepare(
        spots,
        jnp.swapaxes(qkv_weight, 1, 2),
        out_weight,
        in_weight,
        jnp.swapaxes(down_weight, 0, 1),
    )
    weights_got = swap_core(sent)
    h_kept, h_sent, c_kept, c_sent = split(spots, hidden_in, cotangent)
    h_here, h_send = deal(spots, h_kept, swap_core(h_sent))
    s_qk, s_vo, s_up, s_down = join_lanes(spots, kept, weights_got)
    h_there = swap_x(h_send)
    c_here, c_send = deal(spots, c_kept, swap_core(after(c_sent, h_send)))
    c_there = swap_x(after(c_send, h_there))
    qk_zh, vo_zh = swap_zh(s_qk), swap_zh(s_vo)

    pack = jnp.stack(
        [ln1_gain, ln1_shift, ln2_gain, ln2_shift, out_bias, qv_bias[0], qv_bias[1]]
    )
    pack = jnp.where(c == 0, pack[:, :HEAD_DIM], pack[:, HEAD_DIM:])
    hidden_shift = jnp.where(c == 0, in_bias[:OWN], in_bias[OWN:])
    pack = jnp.concatenate([pack, hidden_shift.reshape(4, HEAD_DIM)])
    pack = jnp.stack([pack, swap_x(pack)])
    pack = jnp.stack([pack, swap_zh(pack)])

    h_message = jnp.stack([h_here[1], h_there[1]])
    h_far = swap_zh(after(h_message, c_send))
    qk_one = jnp.stack([s_qk, qk_zh])
    vo_one = jnp.stack([s_vo, vo_zh])
    qk_two, vo_two = swap_x(qk_one), swap_y(vo_one)
    h_far = after(h_far, qk_one, vo_one)
    s_up, s_down = after((s_up, s_down), h_far)

    owned = flip(pack)
    gain_one, shift_one, gain_two, shift_two, out_shift = (
        owned[:, :, i, :, None] for i in range(5)
    )
    by_head = pack.transpose(1, 0, 2, 3)
    q_shift = by_head[:, :, 5].reshape(4, HEAD_DIM, 1)
    v_shift = by_head[:, :, 6].reshape(4, HEAD_DIM, 1)
    in_shift = by_head[:, :, 7:].reshape(UNITS, 1)

    hidden_own, stats = place(spots, h_here, h_there, h_far, True)
    mean, variance = merge_stats(stats, OWN)
    inv_one = lax.rsqrt(variance + EPS)
    inv_one, qk_two, vo_two, c_there = lax.optimization_barrier(
        (inv_one, qk_two, vo_two, c_there)
    )
    own_one = (hidden_own - mean) * inv_one
    w_qk = jnp.stack([qk_one, qk_two])
    w_vo = jnp.stack([vo_one, vo_two])
    w_qk = w_qk, swap_y(w_qk)
    w_vo = w_vo, swap_x(w_vo)
    up_zh = swap_zh(s_up)
    low_one = (own_one * gain_one + shift_one).astype(BF)
    low_one_z = swap_zl(low_one)
    low_one_z, up_zh = lax.optimization_barrier((low_one_z, up_zh))
    s_down = after(s_down, up_zh)
    down_zh = swap_zh(s_down)
    up_one = jnp.stack([s_up, up_zh])
    up_two = swap_x(after(up_one, w_vo[1]))
    wide_one = low_one, swap_core(low_one), low_one_z, swap_core(low_one_z)
    wide_one = after(wide_one, up_one, s_down)

    qk, values, ln_one = project(wide_one, w_qk, w_vo, q_shift, v_shift)
    clip_len = lax.dynamic_slice_in_dim(lengths, 4 * y + 2 * zh + x, 1)
    qk, down_zh = lax.optimization_barrier((qk, down_zh))
    down_one = jnp.stack([s_down, down_zh])
    c_message = after(jnp.stack([c_here[1], c_there[1]]), down_zh)
    down_two, c_far = swap_y(down_one), swap_zh(c_message)
    attended, log_sum = attend_clip(after(qk, down_one, c_message), values, clip_len, CLIP)
    delta = fold(fill_out, w_vo, (attended,), "fold_out")
    *delta, up_two, down_two, c_far = lax.optimization_barrier(
        (*delta, up_two, down_two, c_far)
    )
    w_up = jnp.stack([up_one, up_two])
    w_down = jnp.stack([down_one, down_two])
    w_up = w_up, swap_y(w_up)
    w_down = w_down, swap_x(w_down)
    delta_near, delta_send = fold_cores(delta)
    delta_mid = delta_near + swap_zl(delta_send) + out_shift

    hidden_mid = hidden_own + delta_mid
    mean, variance = merge_stats(token_stats(hidden_mid.reshape(OWN, CLIP)), OWN)
    inv_two = lax.rsqrt(variance + EPS)
    own_two = (hidden_mid - mean) * inv_two
    low_two = (own_two * gain_two + shift_two).astype(BF)
    low_two_z = swap_zl(low_two)
    (cot_own,) = place(spots, c_here, c_there, after(c_far, low_two), False)
    cot_own = after(cot_own, low_two_z)
    cot_z = swap_zl(cot_own)
    wide_two = low_two, swap_core(low_two), low_two_z, swap_core(low_two_z)
    act_low, slope, ln_two = up_project(after(wide_two, cot_own), w_up, in_shift)
    act_low, slope, cot_z = lax.optimization_barrier((act_low, slope, cot_z))
    wide_cot = cot_own, swap_core(cot_own), cot_z, swap_core(cot_z)
    out_near, out_send = fold_cores(fold(fill_down, w_down, (act_low,), "fold_down"))
    out_got = swap_zl(out_send)

    grad_pre, cot_all = grad_act(after(wide_cot, out_send), w_down, slope)
    grad_pre_fold, out_got = lax.optimization_barrier((grad_pre, out_got))
    two_near, two_send = fold_cores(fold(fill_up, w_up, (grad_pre_fold,), "fold_up"))
    two_got = swap_zl(two_send)
    by_unit = (2, 2, OWN, CLIP)
    act_low_after, cot_all_after = after((act_low, cot_all), two_send)
    part_down = grad_x_first((act_low_after.reshape(by_unit),), (cot_all_after,), "grad_down")
    down_first = swap_x(part_down[1])
    part_up = grad_y_first(
        after(grad_pre, part_down[1]).reshape(4, OWN, CLIP), ln_two, "grad_up"
    )
    up_first = swap_y(part_up[1])
    two_got = after(two_got, part_up[1])
    grad_two = two_near + two_got

    def norm_back(grad, normed, inv, gain, meanwhile=()):
        scaled = grad * gain
        sums = jnp.stack([jnp.sum(scaled, axis=(0, 1, 2)), jnp.sum(scaled * normed, axis=(0, 1, 2))])
        sums, meanwhile = lax.optimization_barrier((sum(group_round(sums)) / D, meanwhile))
        return inv * (scaled - sums[0] - normed * sums[1]), meanwhile

    norm_two_grad, _ = norm_back(grad_two, own_two, inv_two, gain_two)
    mid_own = cot_own.astype(F32) + norm_two_grad
    mid_low = mid_own.astype(BF)
    mid_z = swap_zl(mid_low)
    out_leave, out_leave_far = leave(spots, delta_mid + after(out_near, mid_low) + out_got)
    out_leave_far, mid_z = lax.optimization_barrier((out_leave_far, mid_z))
    out_far = swap_zh(out_leave_far)
    wide_mid = mid_low, swap_core(mid_low), mid_z, swap_core(mid_z)
    wide_mid = after(wide_mid, out_leave_far)

    def second_step(keep, got):
        keep = keep.reshape(2, 2, -1, HALF) + got.reshape(2, 2, -1, HALF)
        return keep[0], keep[1].astype(BF)

    def third_step(keep, got):
        keep = keep + got
        return keep[0], keep[1].astype(BF)

    grad_attended, mid_all = grad_attended_of(wide_mid, w_vo)
    early = attend_clip_back(qk, values, log_sum, grad_attended, clip_len, 0)
    *early, down_first, up_first = lax.optimization_barrier((*early, down_first, up_first))
    down_keep, down_send = second_step(part_down[0], down_first)
    up_keep, up_send = second_step(part_up[0], up_first)
    down_second, up_second = swap_y(down_send), swap_x(up_send)
    grad_attended = after(grad_attended, down_send, up_send)
    grad_qk, grad_v = attend_clip_back(
        qk, values, log_sum, grad_attended, clip_len, 2, tuple(early)
    )
    grad_qk, grad_v, out_far = lax.optimization_barrier((grad_qk, grad_v, out_far))
    out_message = jnp.stack([out_leave[1], out_far[1]])
    out_there = swap_x(out_message)
    folded = fold(
        fill_project, (*w_qk, *w_vo), after((grad_qk, grad_v), out_message), "fold_project"
    )
    *folded, down_second, up_second = lax.optimization_barrier(
        (*folded, down_second, up_second)
    )
    down_keep, down_send = third_step(down_keep, down_second)
    up_keep, up_send = third_step(up_keep, up_second)
    down_third, up_third = swap_zh(down_send), swap_zh(up_send)
    one_near, one_send = fold_cores(folded)
    one_got = swap_zl(one_send)
    by_head_dims = (2, 2, HEAD_DIM, CLIP)
    grad_v, grad_qk = after((grad_v, grad_qk), one_send, down_send, up_send)
    part_vo = grad_x_first(
        (grad_v.reshape(by_head_dims), attended.reshape(by_head_dims)),
        (ln_one, mid_all),
        "grad_vo",
    )
    *part_vo, one_got = lax.optimization_barrier((*part_vo, one_got))
    vo_first = swap_x(part_vo[1])
    part_qk = grad_y_first(
        after(grad_qk, part_vo[1]).reshape(4, 2 * HEAD_DIM, CLIP), ln_one, "grad_qk"
    )
    *part_qk, down_third = lax.optimization_barrier((*part_qk, down_third))
    qk_first = swap_y(part_qk[1])
    out_kept, out_sent = undeal(spots, out_leave, out_far, after(out_there, part_qk[1]))
    hidden_out = finish(spots, out_kept, swap_core(out_sent), hidden_in, down_bias[:, None])

    grad_one = one_near + one_got
    norm_one_grad, (vo_first, qk_first) = norm_back(
        grad_one, own_one, inv_one, gain_one, (vo_first, qk_first)
    )
    vo_keep, vo_send = second_step(part_vo[0], vo_first)
    vo_second = swap_y(vo_send)
    qk_keep, qk_send = second_step(part_qk[0], qk_first)
    qk_second = swap_x(qk_send)
    norm_one_grad = after(norm_one_grad, qk_send, vo_send)
    in_leave, in_leave_far = leave(spots, norm_two_grad + norm_one_grad)
    in_far = swap_zh(in_leave_far)

    up_third, vo_second = after((up_third, vo_second), in_leave_far)
    vo_keep, vo_send = third_step(vo_keep, vo_second)
    vo_third = swap_zh(vo_send)
    up_third = after(up_third, vo_send)
    ff_kept, ff_sent = store_ff(spots, up_keep + up_third, down_keep + down_third)
    ff_got = swap_core(ff_sent)
    in_far, qk_second = lax.optimization_barrier(after((in_far, qk_second), ff_sent))
    in_message = jnp.stack([in_leave[1], in_far[1]])
    in_there = swap_x(in_message)
    qk_keep, qk_send = third_step(qk_keep, qk_second)
    qk_third = swap_zh(qk_send)
    g_up, g_down = join_ff(spots, ff_kept, after(ff_got, qk_send, in_message))

    def over_tokens(values):
        return jnp.sum(values, axis=-1, dtype=F32)

    owned = jnp.stack(
        [
            over_tokens(v)
            for v in (
                grad_one * own_one,
                grad_one,
                grad_two * own_two,
                grad_two,
                mid_own,
                cot_own.astype(F32),
            )
        ],
        axis=2,
    ).reshape(2, 2, -1)
    heads = jnp.concatenate(
        [
            over_tokens(grad_qk[:, 0].astype(F32)),
            over_tokens(grad_v.astype(F32)),
            over_tokens(grad_pre.astype(F32)).reshape(4, OWN),
        ],
        axis=1,
    )
    vectors = jnp.concatenate([flip(owned), heads.reshape(2, 2, -1).transpose(1, 0, 2)], axis=2)
    total = vectors[0] + swap_zh(vectors[1])
    total = total[0] + swap_x(total[1])
    total = total + swap_y(total)
    other = swap_core(total)
    both = jnp.where(c == 0, jnp.stack([total, other]), jnp.stack([other, total]))
    singles = both[:, : 8 * HEAD_DIM].reshape(2, 8, HEAD_DIM).transpose(1, 0, 2).reshape(8, -1)

    in_kept, in_sent = undeal(spots, in_leave, in_far, in_there)
    no_shift = jnp.zeros((2 * HEAD_DIM, 1), F32)
    hidden_grad = finish(spots, in_kept, swap_core(in_sent), cotangent, no_shift)
    qk_third, vo_third = after((qk_third, vo_third), other, g_up, g_down, hidden_out)
    at_kept, at_sent = store_qkvo(spots, qk_keep + qk_third, vo_keep + vo_third)
    g_qkv, g_out = join_qkvo(spots, at_kept, swap_core(at_sent))

    return (
        hidden_out,
        hidden_grad,
        singles[0],
        singles[1],
        jnp.swapaxes(g_qkv, 1, 2),
        singles[6:8],
        g_out,
        singles[4],
        singles[2],
        singles[3],
        g_up,
        both[:, 8 * HEAD_DIM :].reshape(-1),
        jnp.swapaxes(g_down, 0, 1),
        singles[5],
    )


def solution(mesh):
    sizes = dict(mesh.shape)

    def program(*arrays):
        small = sizes == {"row": 4, "col": 8} and arrays[0].shape == (D, 2 * sizes["row"] * CLIP)
        return mapped(local_clip if small else local, mesh)(*arrays)

    return program


def mapped(body, mesh):
    return jax.shard_map(
        body,
        mesh=mesh,
        in_specs=(
            P("col", "row"),
            P(),
            P("col"),
            P("col"),
            P(None, "row", "col"),
            P(None, "col"),
            P("col", "row"),
            P("col"),
            P("col"),
            P("col"),
            P("row", "col"),
            P("col"),
            P("col", "row"),
            P("col"),
            P("col", "row"),
        ),
        out_specs=(
            P("col", "row"),
            P("col", "row"),
            P("col"),
            P("col"),
            P(None, "row", "col"),
            P(None, "col"),
            P("col", "row"),
            P("col"),
            P("col"),
            P("col"),
            P("row", "col"),
            P("col"),
            P("col", "row"),
            P("col"),
        ),
        check_vma=False,
    )
```

```python
import functools

import jax
import jax.numpy as jnp
from jax import lax
from jax.experimental import pallas as pl
from jax.experimental.pallas import tpu as pltpu
from jax.sharding import PartitionSpec as P

HEADS = 16
HEAD_DIM = 80
D = 1280
MICRO = 2
GROUP = 8


EPS = 1e-05


def partner(block, axis, distance):
    count = lax.axis_size(axis)
    route = []
    for low in range(count):
        high = low | 1 << distance
        if high != low and high < count:
            route += [(low, high), (high, low)]
    return lax.ppermute(block, axis, route)


def row_totals(first_sum, second_sum):
    return lax.psum((first_sum, second_sum), "col")


def widen(values):
    return lax.all_gather(values, "col", axis=1, tiled=True)


def narrow(values):
    return lax.psum_scatter(values, "col", scatter_dimension=1, tiled=True)


def to_clips(stacked):
    return lax.all_to_all(stacked, "col", split_axis=1, concat_axis=2, tiled=True)


def to_columns(stacked):
    return lax.all_to_all(stacked, "col", split_axis=2, concat_axis=1, tiled=True)


def contract_rows(left, right):
    return lax.dot_general(
        left, right, (((0,), (0,)), ((), ())), preferred_element_type=jnp.float32
    )


def contract_cols(left, right):
    return lax.dot_general(
        left, right, (((1,), (1,)), ((), ())), preferred_element_type=jnp.float32
    )


def exact_gelu(values):
    return jax.nn.gelu(values, approximate=False)


def norm_forward(values, norm_gain, norm_shift):
    first_sum, second_sum = row_totals(jnp.sum(values, axis=1), jnp.sum(values * values, axis=1))
    mean_rows = first_sum / D
    inv_std = lax.rsqrt(second_sum / D - mean_rows * mean_rows + EPS)
    normed = (values - mean_rows[:, None]) * inv_std[:, None]
    return (normed, inv_std, normed * norm_gain + norm_shift)


def norm_backward(grad_out, normed, inv_std, norm_gain):
    scaled = grad_out * norm_gain
    first_sum, second_sum = row_totals(jnp.sum(scaled, axis=1), jnp.sum(scaled * normed, axis=1))
    grad_input = inv_std[:, None] * (
        scaled - first_sum[:, None] / D - normed * (second_sum[:, None] / D)
    )
    return (grad_input, jnp.sum(grad_out * normed, axis=0), jnp.sum(grad_out, axis=0))


def split_heads(values):
    return values.reshape(values.shape[0], HEADS, HEAD_DIM)


def gather_clip(key_rows, value_rows):
    position = lax.axis_index("col")
    for bit_index in range(GROUP.bit_length() - 1):
        other_keys, other_values = partner((key_rows, value_rows), "col", bit_index)
        upper_half = position >> bit_index & 1 == 1
        key_rows = jnp.where(
            upper_half,
            jnp.concatenate([other_keys, key_rows]),
            jnp.concatenate([key_rows, other_keys]),
        )
        value_rows = jnp.where(
            upper_half,
            jnp.concatenate([other_values, value_rows]),
            jnp.concatenate([value_rows, other_values]),
        )
    return (key_rows, value_rows)


def scatter_clip(grad_keys, grad_values):
    position = lax.axis_index("col")
    for bit_index in reversed(range(GROUP.bit_length() - 1)):
        half_rows = grad_keys.shape[0] // 2
        upper_half = position >> bit_index & 1 == 1
        keep_keys = jnp.where(upper_half, grad_keys[half_rows:], grad_keys[:half_rows])
        send_keys = jnp.where(upper_half, grad_keys[:half_rows], grad_keys[half_rows:])
        keep_values = jnp.where(upper_half, grad_values[half_rows:], grad_values[:half_rows])
        send_values = jnp.where(upper_half, grad_values[:half_rows], grad_values[half_rows:])
        got_keys, got_values = partner((send_keys, send_values), "col", bit_index)
        grad_keys = keep_keys + got_keys
        grad_values = keep_values + got_values
    return (grad_keys, grad_values)


def clip_scores(queries, key_rows, valid_len):
    scale_factor = HEAD_DIM ** (-0.5)
    scores = (
        jnp.einsum(
            "qhe,khe->hqk",
            split_heads(queries),
            split_heads(key_rows),
            preferred_element_type=jnp.float32,
        )
        * scale_factor
    )
    live_keys = lax.broadcasted_iota(jnp.int32, (1, 1, key_rows.shape[0]), 2) < valid_len
    return jnp.where(live_keys, scores, -1e30)


def attend(queries, key_rows, value_rows, valid_len):
    scores = clip_scores(queries, key_rows, valid_len)
    top_score = jnp.max(scores, axis=2, keepdims=True)
    weights = jnp.exp(scores - top_score)
    weight_sum = jnp.sum(weights, axis=2, keepdims=True)
    prob_low = (weights / weight_sum).astype(jnp.bfloat16)
    attended = jnp.einsum(
        "hqk,khe->qhe", prob_low, split_heads(value_rows), preferred_element_type=jnp.float32
    )
    return (attended.reshape(queries.shape[0], -1), top_score + jnp.log(weight_sum))


def attend_back(queries, key_rows, value_rows, valid_len, log_sum, grad_low):
    scale_factor = HEAD_DIM ** (-0.5)
    scores = clip_scores(queries, key_rows, valid_len)
    probs_full = jnp.exp(scores - log_sum)
    grad_heads = split_heads(grad_low)
    grad_value = jnp.einsum(
        "hqk,qhe->khe",
        probs_full.astype(jnp.bfloat16),
        grad_heads,
        preferred_element_type=jnp.float32,
    )
    grad_probs = jnp.einsum(
        "qhe,khe->hqk", grad_heads, split_heads(value_rows), preferred_element_type=jnp.float32
    )
    row_dot = jnp.sum(probs_full * grad_probs, axis=2, keepdims=True)
    grad_scores = (probs_full * (grad_probs - row_dot)).astype(jnp.bfloat16)
    grad_query = (
        jnp.einsum(
            "hqk,khe->qhe", grad_scores, split_heads(key_rows), preferred_element_type=jnp.float32
        )
        * scale_factor
    )
    grad_key = (
        jnp.einsum(
            "hqk,qhe->khe", grad_scores, split_heads(queries), preferred_element_type=jnp.float32
        )
        * scale_factor
    )
    return (
        grad_query.reshape(queries.shape[0], -1),
        grad_key.reshape(key_rows.shape[0], -1),
        grad_value.reshape(key_rows.shape[0], -1),
    )


def layer_pass(input_rows, grad_rows, weights, vectors, valid_len):
    qkv_full, out_full, in_full, down_full = weights
    gain_one, shift_one, qv_full, out_shift, gain_two, shift_two, in_shift, down_shift = vectors
    bias_three = jnp.stack([qv_full[0], jnp.zeros_like(qv_full[0]), qv_full[1]])[:, None, :]
    normed_one, inv_one, ln_one = norm_forward(input_rows, gain_one, shift_one)
    wide_one = widen(ln_one.astype(jnp.bfloat16))
    projected = (
        jnp.einsum("td,sdc->stc", wide_one, qkv_full, preferred_element_type=jnp.float32)
        + bias_three
    )
    projected = to_clips(projected.astype(jnp.bfloat16))
    key_rows, value_rows = gather_clip(projected[1], projected[2])
    attended, log_sum = attend(projected[0], key_rows, value_rows, valid_len)
    attended_low = to_columns(attended.astype(jnp.bfloat16)[None])[0]
    hidden_mid = (
        input_rows
        + narrow(jnp.dot(attended_low, out_full, preferred_element_type=jnp.float32))
        + out_shift
    )
    normed_two, inv_two, ln_two = norm_forward(hidden_mid, gain_two, shift_two)
    wide_two = widen(ln_two.astype(jnp.bfloat16))
    pre_act = jnp.dot(wide_two, in_full, preferred_element_type=jnp.float32) + in_shift
    act_value, gelu_back = jax.vjp(exact_gelu, pre_act)
    act_low = act_value.astype(jnp.bfloat16)
    hidden_out = (
        hidden_mid
        + narrow(jnp.dot(act_low, down_full, preferred_element_type=jnp.float32))
        + down_shift
    )
    grad_wide = widen(grad_rows.astype(jnp.bfloat16))
    grad_down = contract_rows(act_low, grad_wide)
    grad_pre = gelu_back(contract_cols(grad_wide, down_full))[0].astype(jnp.bfloat16)
    grad_in = contract_rows(wide_two, grad_pre)
    grad_ln_two = narrow(contract_cols(grad_pre, in_full))
    grad_norm_two, grad_gain_two, grad_shift_two = norm_backward(
        grad_ln_two, normed_two, inv_two, gain_two
    )
    grad_mid = grad_rows + grad_norm_two
    grad_mid_wide = widen(grad_mid.astype(jnp.bfloat16))
    grad_out = contract_rows(attended_low, grad_mid_wide)
    grad_attended = to_clips(contract_cols(grad_mid_wide, out_full).astype(jnp.bfloat16)[None])[0]
    grad_query, grad_key, grad_value = attend_back(
        projected[0], key_rows, value_rows, valid_len, log_sum, grad_attended
    )
    grad_key, grad_value = scatter_clip(grad_key, grad_value)
    grad_proj = to_columns(jnp.stack([grad_query, grad_key, grad_value]).astype(jnp.bfloat16))
    grad_qkv = jnp.einsum("td,stc->sdc", wide_one, grad_proj, preferred_element_type=jnp.float32)
    grad_ln_one = narrow(
        jnp.einsum("stc,sdc->td", grad_proj, qkv_full, preferred_element_type=jnp.float32)
    )
    grad_norm_one, grad_gain_one, grad_shift_one = norm_backward(
        grad_ln_one, normed_one, inv_one, gain_one
    )
    grad_input = grad_mid + grad_norm_one
    proj_sums = jnp.sum(grad_proj, axis=1, dtype=jnp.float32)
    vector_parts = (
        grad_gain_one,
        grad_shift_one,
        jnp.stack([proj_sums[0], proj_sums[2]]),
        jnp.sum(grad_mid, axis=0),
        grad_gain_two,
        grad_shift_two,
        jnp.sum(grad_pre, axis=0, dtype=jnp.float32),
        jnp.sum(grad_rows, axis=0),
    )
    return (hidden_out, grad_input, (grad_qkv, grad_out, grad_in, grad_down), vector_parts)


def tile_grid(vector, row_count):
    return jnp.broadcast_to(vector[None], (row_count,) + vector.shape)


def grid_reduce(partials, vector_parts):
    row_count = lax.axis_size("row")
    qkv_part, out_part, in_part, down_part = partials
    qkv_blocks = qkv_part.reshape(3, row_count, -1, qkv_part.shape[2]).transpose(1, 0, 2, 3)
    out_blocks = out_part.reshape(out_part.shape[0], row_count, -1).transpose(1, 0, 2)
    in_blocks = in_part.reshape(row_count, -1, in_part.shape[1])
    down_blocks = down_part.reshape(down_part.shape[0], row_count, -1).transpose(1, 0, 2)
    tiled = [tile_grid(vector, row_count) for vector in vector_parts]
    reduced = (
        lax.psum_scatter(qkv_blocks, "row", scatter_dimension=0, tiled=True),
        lax.psum_scatter(out_blocks, "row", scatter_dimension=0, tiled=True),
        lax.psum_scatter(in_blocks, "row", scatter_dimension=0, tiled=True),
        lax.psum_scatter(down_blocks, "row", scatter_dimension=0, tiled=True),
        lax.psum_scatter(tiled[0], "row", scatter_dimension=0, tiled=True),
        lax.psum_scatter(tiled[1], "row", scatter_dimension=0, tiled=True),
        lax.psum_scatter(tiled[2], "row", scatter_dimension=0, tiled=True),
        lax.psum_scatter(tiled[3], "row", scatter_dimension=0, tiled=True),
        lax.psum_scatter(tiled[4], "row", scatter_dimension=0, tiled=True),
        lax.psum_scatter(tiled[5], "row", scatter_dimension=0, tiled=True),
        lax.psum_scatter(tiled[6], "row", scatter_dimension=0, tiled=True),
        lax.psum_scatter(tiled[7], "row", scatter_dimension=0, tiled=True),
    )
    return tuple((piece[0] for piece in reduced))


def local(
    hidden_in,
    lengths,
    ln1_gain,
    ln1_shift,
    qkv_weight,
    qv_bias,
    out_weight,
    out_bias,
    ln2_gain,
    ln2_shift,
    in_weight,
    in_bias,
    down_weight,
    down_bias,
    cotangent,
):
    col_count = lax.axis_size("col")
    token_rows = jnp.transpose(hidden_in)
    cot_rows = jnp.transpose(cotangent)
    rows_block = token_rows.shape[0] // MICRO
    weights = (
        lax.all_gather(qkv_weight, "row", axis=1, tiled=True),
        lax.all_gather(out_weight, "row", axis=1, tiled=True),
        lax.all_gather(in_weight, "row", axis=0, tiled=True),
        lax.all_gather(down_weight, "row", axis=1, tiled=True),
    )
    vectors = (ln1_gain, ln1_shift, qv_bias, out_bias, ln2_gain, ln2_shift, in_bias, down_bias)
    clip_slot = lax.axis_index("col") // GROUP
    outputs = []
    input_grads = []
    totals = None
    running = None
    for micro_index in range(MICRO):
        input_rows = token_rows[micro_index * rows_block : (micro_index + 1) * rows_block]
        grad_rows = cot_rows[micro_index * rows_block : (micro_index + 1) * rows_block]
        clip_id = (lax.axis_index("row") * MICRO + micro_index) * (col_count // GROUP) + clip_slot
        valid_len = lax.dynamic_index_in_dim(lengths, clip_id, keepdims=False)
        out_rows, back_rows, partials, vector_parts = layer_pass(
            input_rows, grad_rows, weights, vectors, valid_len
        )
        outputs.append(out_rows)
        input_grads.append(back_rows)
        current = (partials, vector_parts)
        running = current if running is None else jax.tree.map(jnp.add, running, current)
    totals = grid_reduce(running[0], running[1])
    (
        grad_qkv,
        grad_out,
        grad_in,
        grad_down,
        grad_gain_one,
        grad_shift_one,
        grad_qv,
        grad_out_shift,
        grad_gain_two,
        grad_shift_two,
        grad_in_shift,
        grad_down_shift,
    ) = totals
    hidden_out = jnp.transpose(jnp.concatenate(outputs, axis=0))
    hidden_grad = jnp.transpose(jnp.concatenate(input_grads, axis=0))
    return (
        hidden_out,
        hidden_grad,
        grad_gain_one,
        grad_shift_one,
        grad_qkv,
        grad_qv,
        grad_out,
        grad_out_shift,
        grad_gain_two,
        grad_shift_two,
        grad_in,
        grad_in_shift,
        grad_down,
        grad_down_shift,
    )


CLIP = 1024
FF = 5120
OWN = D // 4
UNITS = FF // 4
HALF = D // 2
BLOCK = 256
STEPS = CLIP // BLOCK
BF = jnp.bfloat16
F32 = jnp.float32


def swap_core(values):
    return lax.ppermute(values, "row", [(i, i ^ 1) for i in range(4)])


def swap_y(values):
    return lax.ppermute(values, "row", [(i, i ^ 2) for i in range(4)])


def swap_x(values):
    return lax.ppermute(values, "col", [(i, i ^ 1) for i in range(8)])


def swap_zl(values):
    return lax.ppermute(values, "col", [(i, i ^ 2) for i in range(8)])


def swap_zh(values):
    return lax.ppermute(values, "col", [(i, i ^ 4) for i in range(8)])


def pick(values, index, axis=0):
    return lax.dynamic_index_in_dim(values, index, axis, keepdims=False)


def mm(left, right, left_dim, right_dim):
    return lax.dot_general(
        left, right, (((left_dim,), (right_dim,)), ((), ())), preferred_element_type=F32
    )


def shaped(dims, kind=BF):
    return jax.ShapeDtypeStruct(dims, kind)


def spots_spec():
    return pl.BlockSpec(memory_space=pltpu.SMEM)


def fixed(array):
    rank = len(array.shape)
    return pl.BlockSpec(array.shape, lambda i: (0,) * rank)


def tokens_spec(dims):
    lead = tuple(dims[:-1])
    return pl.BlockSpec(lead + (BLOCK,), lambda i: (0,) * len(lead) + (i,))


def cost(flops, moved):
    return pl.CostEstimate(flops=1, transcendentals=0, bytes_accessed=1)


def attend_kernel(len_ref, q_ref, k_ref, v_ref, out_ref, lse_ref):
    scores = mm(k_ref[...], q_ref[...], 0, 0) * (HEAD_DIM**-0.5)
    live = lax.broadcasted_iota(jnp.int32, scores.shape, 0) < len_ref[0]
    scores = jnp.where(live, scores, -1e30)
    top = jnp.max(scores, axis=0, keepdims=True)
    weights = jnp.exp(scores - top)
    total = jnp.sum(weights, axis=0, keepdims=True)
    prob_low = (weights * (1.0 / total)).astype(BF)
    out_ref[...] = mm(v_ref[...], prob_low, 1, 0).astype(BF)
    lse_ref[...] = top + jnp.log(total)


def head_specs(block):
    return [
        pl.BlockSpec((None, None, HEAD_DIM, block), lambda h, i, n: (h, 0, 0, i)),
        pl.BlockSpec((None, None, HEAD_DIM, CLIP), lambda h, i, n: (h, 1, 0, 0)),
        pl.BlockSpec((None, HEAD_DIM, CLIP), lambda h, i, n: (h, 0, 0)),
    ]


def attend_clip(qk, values, clip_len, block):
    return pl.pallas_call(
        attend_kernel,
        grid_spec=pltpu.PrefetchScalarGridSpec(
            num_scalar_prefetch=1,
            grid=(4, CLIP // block),
            in_specs=head_specs(block),
            out_specs=[
                pl.BlockSpec((None, HEAD_DIM, block), lambda h, i, n: (h, 0, i)),
                pl.BlockSpec((None, 1, block), lambda h, i, n: (h, 0, i)),
            ],
        ),
        out_shape=[shaped((4, HEAD_DIM, CLIP)), shaped((4, 1, CLIP), F32)],
        cost_estimate=cost(16 * CLIP * CLIP * HEAD_DIM, 16 * HEAD_DIM * CLIP * 2),
        name="attend_clip",
    )(clip_len, qk, qk, values)


def attend_back_kernel(
    len_ref, q_ref, k_ref, v_ref, lse_ref, grad_ref, *refs
):
    gqk_ref, gv_ref = refs[-2:]
    scale = HEAD_DIM**-0.5
    queries, keys, values, grad = q_ref[...], k_ref[...], v_ref[...], grad_ref[...]
    scores = mm(keys, queries, 0, 0) * scale
    live = lax.broadcasted_iota(jnp.int32, scores.shape, 0) < len_ref[0]
    scores = jnp.where(live, scores, -1e30)
    probs = jnp.exp(scores - lse_ref[...])
    grad_probs = mm(values, grad, 0, 0)
    row_dot = jnp.sum(probs * grad_probs, axis=0, keepdims=True)
    score_low = (probs * (grad_probs - row_dot)).astype(BF)
    grad_query = mm(keys, score_low, 1, 0) * scale
    grad_key = mm(queries, score_low, 1, 1)
    grad_value = mm(grad, probs.astype(BF), 1, 1)
    gqk_ref[0] = grad_query.astype(BF)
    gqk_ref[1] = (grad_key * scale).astype(BF)
    gv_ref[...] = grad_value.astype(BF)


def attend_clip_back(qk, values, log_sum, grad_attended, clip_len, first, earlier=()):
    def heads(*dims):
        return pl.BlockSpec(
            (None,) + dims, lambda h, n: (h + first,) + (0,) * len(dims)
        )

    def part(i):
        return pl.BlockSpec((None, None, HEAD_DIM, CLIP), lambda h, n: (h + first, i, 0, 0))

    operands = (qk, qk, values, log_sum, grad_attended)
    return pl.pallas_call(
        attend_back_kernel,
        grid_spec=pltpu.PrefetchScalarGridSpec(
            num_scalar_prefetch=1,
            grid=(2,),
            in_specs=[
                part(0),
                part(1),
                heads(HEAD_DIM, CLIP),
                heads(1, CLIP),
                heads(HEAD_DIM, CLIP),
            ]
            + [pl.BlockSpec(memory_space=pl.ANY)] * len(earlier),
            out_specs=[heads(2, HEAD_DIM, CLIP), heads(HEAD_DIM, CLIP)],
        ),
        out_shape=[shaped((4, 2, HEAD_DIM, CLIP)), shaped((4, HEAD_DIM, CLIP))],
        input_output_aliases={6: 0, 7: 1} if earlier else {},
        cost_estimate=cost(20 * CLIP * CLIP * HEAD_DIM, 16 * HEAD_DIM * CLIP * 2),
        name="attend_clip_back",
    )(clip_len, *operands, *earlier)


WIDE = 384


def order_hot(core):
    place = lax.broadcasted_iota(jnp.int32, (OWN, OWN), 1)
    stored = lax.broadcasted_iota(jnp.int32, (OWN, OWN), 0)
    hot = jnp.zeros((OWN, OWN), jnp.bool_)
    for chunk in range(4):
        source = (2 * (chunk >> 1) + (core ^ (chunk & 1))) * HEAD_DIM
        inside = (place >= chunk * HEAD_DIM) & (place < (chunk + 1) * HEAD_DIM)
        hot = hot | (inside & (stored - source == place - chunk * HEAD_DIM))
    return jnp.where(hot, 1.0, 0.0).astype(BF)


def whole():
    return pl.BlockSpec(memory_space=pltpu.VMEM)


def prepare_kernel(spots_ref, qkv_ref, out_ref, in_ref, down_ref, kept_ref, sent_ref):
    c = spots_ref[0]
    for ref, core in ((kept_ref, c), (sent_ref, 1 - c)):
        hot = order_hot(core)

        def half(value, count):
            return jnp.where(core == 0, value[:count], value[count:])

        for s in range(3):
            value = half(mm(qkv_ref[s], hot, 1, 0), HEAD_DIM)
            ref[s * HEAD_DIM : (s + 1) * HEAD_DIM, :OWN] = value.astype(BF)
        value = half(mm(out_ref[...], hot, 1, 0), HEAD_DIM)
        ref[3 * HEAD_DIM : OWN, :OWN] = value.astype(BF)
        ref[OWN : 2 * OWN, :OWN] = half(mm(in_ref[...], hot, 0, 0), OWN).astype(BF)
        ref[2 * OWN :, :OWN] = half(mm(down_ref[...], hot, 0, 0), OWN).astype(BF)
        ref[:, OWN:] = jnp.zeros((3 * OWN, WIDE - OWN), BF)


def prepare(spots, qkv_turned, out_weight, in_weight, down_turned):
    return pl.pallas_call(
        prepare_kernel,
        in_specs=[spots_spec()] + [whole()] * 4,
        out_specs=[whole()] * 2,
        out_shape=[shaped((3 * OWN, WIDE))] * 2,
        cost_estimate=cost(8 * 3 * OWN * OWN * OWN, 4 * 3 * OWN * OWN * 2),
        name="prepare_weights",
    )(spots, qkv_turned, out_weight, in_weight, down_turned)


def lanes_kernel(spots_ref, kept_ref, got_ref, *out_refs):
    def write(near_ref, far_ref):
        start = 0
        for ref in out_refs:
            rows = slice(start, start + ref.shape[0])
            ref[:, :OWN] = near_ref[rows, :OWN]
            ref[:, OWN:] = far_ref[rows, :OWN]
            start += ref.shape[0]

    @pl.when(spots_ref[1] == 1)
    def _():
        write(kept_ref, got_ref)

    @pl.when(spots_ref[1] == 0)
    def _():
        write(got_ref, kept_ref)


def join_lanes(spots, kept, got):
    return pl.pallas_call(
        lanes_kernel,
        in_specs=[spots_spec(), whole(), whole()],
        out_specs=[whole()] * 3,
        out_shape=[shaped((OWN, HALF))] * 3,
        cost_estimate=cost(0, 4 * 3 * OWN * OWN * 2),
        name="join_lanes",
    )(spots, kept, got)


def two_terms(value):
    high = value.astype(BF)
    return high, (value - high.astype(F32)).astype(BF)


def store_ff_kernel(spots_ref, up_ref, down_ref, kept_ref, sent_ref):
    hot = order_hot(spots_ref[0])
    is_near = spots_ref[1] == 1
    for place, total_ref in ((0, up_ref), (1, down_ref)):
        near, far = total_ref[:, :OWN], total_ref[:, OWN:]
        lanes = slice(place * OWN, (place + 1) * OWN)
        for ref, value in (
            (kept_ref, jnp.where(is_near, near, far)),
            (sent_ref, jnp.where(is_near, far, near)),
        ):
            high, rest = two_terms(value)
            ref[:, lanes] = mm(hot, high, 1, 1) + mm(hot, rest, 1, 1)


def store_ff(spots, up_total, down_total):
    return pl.pallas_call(
        store_ff_kernel,
        in_specs=[spots_spec()] + [whole()] * 2,
        out_specs=[whole()] * 2,
        out_shape=[shaped((OWN, HALF), F32)] * 2,
        cost_estimate=cost(16 * OWN * OWN * OWN, 16 * OWN * OWN * 4),
        name="store_ff",
    )(spots, up_total, down_total)


def join_ff_kernel(spots_ref, kept_ref, got_ref, up_ref, down_ref):
    def write(first_ref, second_ref):
        for place, ref in ((0, up_ref), (1, down_ref)):
            lanes = slice(place * OWN, (place + 1) * OWN)
            ref[:, :OWN] = first_ref[:, lanes]
            ref[:, OWN:] = second_ref[:, lanes]

    @pl.when(spots_ref[0] == 0)
    def _():
        write(kept_ref, got_ref)

    @pl.when(spots_ref[0] == 1)
    def _():
        write(got_ref, kept_ref)


def join_ff(spots, kept, got):
    return pl.pallas_call(
        join_ff_kernel,
        in_specs=[spots_spec()] + [whole()] * 2,
        out_specs=[whole()] * 2,
        out_shape=[shaped((OWN, HALF), F32)] * 2,
        cost_estimate=cost(0, 16 * OWN * OWN * 4),
        name="join_ff",
    )(spots, kept, got)


def store_qkvo_kernel(spots_ref, qk_ref, vo_ref, kept_ref, sent_ref):
    hot = order_hot(spots_ref[0])
    is_near = spots_ref[1] == 1
    for place, total_ref in ((0, qk_ref), (1, vo_ref)):
        near, far = total_ref[:, :OWN], total_ref[:, OWN:]
        rows = slice(place * 2 * HEAD_DIM, (place + 1) * 2 * HEAD_DIM)
        for ref, value in (
            (kept_ref, jnp.where(is_near, near, far)),
            (sent_ref, jnp.where(is_near, far, near)),
        ):
            high, rest = two_terms(value)
            ref[rows, :OWN] = mm(high, hot, 1, 1) + mm(rest, hot, 1, 1)
    kept_ref[:, OWN:] = jnp.zeros((OWN, WIDE - OWN), F32)
    sent_ref[:, OWN:] = jnp.zeros((OWN, WIDE - OWN), F32)


def store_qkvo(spots, qk_total, vo_total):
    return pl.pallas_call(
        store_qkvo_kernel,
        in_specs=[spots_spec()] + [whole()] * 2,
        out_specs=[whole()] * 2,
        out_shape=[shaped((OWN, WIDE), F32)] * 2,
        cost_estimate=cost(8 * OWN * OWN * OWN, 16 * OWN * OWN * 4),
        name="store_qkvo",
    )(spots, qk_total, vo_total)


def join_qkvo_kernel(spots_ref, kept_ref, got_ref, qkv_ref, out_ref):
    def write(first_ref, second_ref):
        for place, ref in ((0, first_ref), (1, second_ref)):
            rows = slice(place * HEAD_DIM, (place + 1) * HEAD_DIM)
            for s in range(3):
                qkv_ref[s, rows] = ref[s * HEAD_DIM : (s + 1) * HEAD_DIM, :OWN]
            out_ref[rows] = ref[3 * HEAD_DIM : 4 * HEAD_DIM, :OWN]

    @pl.when(spots_ref[0] == 0)
    def _():
        write(kept_ref, got_ref)

    @pl.when(spots_ref[0] == 1)
    def _():
        write(got_ref, kept_ref)


def join_qkvo(spots, kept, got):
    return pl.pallas_call(
        join_qkvo_kernel,
        in_specs=[spots_spec()] + [whole()] * 2,
        out_specs=[whole()] * 2,
        out_shape=[shaped((3, 2 * HEAD_DIM, OWN), F32), shaped((2 * HEAD_DIM, OWN), F32)],
        cost_estimate=cost(0, 8 * OWN * OWN * 4),
        name="join_qkvo",
    )(spots, kept, got)


TAIL = 8


def split_kernel(spots_ref, hid_ref, cot_ref, pack_ref, hk_ref, hs_ref, ck_ref, cs_ref):
    c = spots_ref[0]
    data, tails, cots = [], [], []
    for half in (0, 1):
        rows = slice(half * HEAD_DIM, (half + 1) * HEAD_DIM)
        value = hid_ref[rows]
        mean = jnp.mean(value, axis=0, keepdims=True)
        data.append(value - mean)
        spot = lax.broadcasted_iota(jnp.int32, (TAIL, value.shape[1]), 0)
        tail = jnp.zeros(spot.shape, F32)
        for first, exact in ((0, mean), (3, pack_ref[half : half + 1])):
            high = exact.astype(BF).astype(F32)
            middle = (exact - high).astype(BF).astype(F32)
            for i, term in enumerate((high, middle, exact - high - middle)):
                tail = jnp.where(spot == first + i, term, tail)
        tails.append(tail)
        cots.append(cot_ref[rows])
    for ref, cot, first in ((hk_ref, ck_ref, c == 0), (hs_ref, cs_ref, c == 1)):
        ref[:HEAD_DIM] = jnp.where(first, data[0], data[1]).astype(BF)
        ref[HEAD_DIM:] = jnp.where(first, tails[0], tails[1]).astype(BF)
        cot[...] = jnp.where(first, cots[0], cots[1]).astype(BF)


def split(spots, hidden_in, cotangent, pack):
    block = pl.BlockSpec((2 * HEAD_DIM, CLIP // 2), lambda i: (0, i))
    specs = [
        pl.BlockSpec((n, CLIP // 2), lambda i: (0, i))
        for n in (HEAD_DIM + TAIL, HEAD_DIM + TAIL, HEAD_DIM, HEAD_DIM)
    ]
    return pl.pallas_call(
        split_kernel,
        grid=(4,),
        in_specs=[
            spots_spec(),
            block,
            block,
            pl.BlockSpec((2, CLIP // 2), lambda i: (0, i % 2)),
        ],
        out_specs=specs,
        out_shape=[
            shaped((n, 2 * CLIP)) for n in (HEAD_DIM + TAIL, HEAD_DIM + TAIL, HEAD_DIM, HEAD_DIM)
        ],
        cost_estimate=cost(0, 8 * HEAD_DIM * 2 * CLIP * 4),
        name="split_in",
    )(spots, hidden_in, cotangent, pack)


def deal_kernel(spots_ref, kept_ref, got_ref, here_ref, send_ref):
    for is_own in (0, 1):
        for x in (0, 1):

            @pl.when((spots_ref[2] == is_own) & (spots_ref[3] == x))
            def _(is_own=is_own, x=x):
                pair = (kept_ref, got_ref) if is_own else (got_ref, kept_ref)
                near = slice(x * CLIP, (x + 1) * CLIP)
                away = slice((1 - x) * CLIP, (2 - x) * CLIP)
                for i in (0, 1):
                    here_ref[i] = pair[i][:, near]
                    send_ref[i] = pair[i][:, away]


def deal(spots, kept, got):
    return pl.pallas_call(
        deal_kernel,
        in_specs=[spots_spec(), whole(), whole()],
        out_specs=[whole()] * 2,
        out_shape=[shaped((2, kept.shape[0], CLIP))] * 2,
        cost_estimate=cost(0, 8 * kept.shape[0] * CLIP * 2),
        name="deal",
    )(spots, kept, got)


def place_kernel(spots_ref, here_ref, there_ref, far_ref, own_ref, *stats_ref):
    grid = ((here_ref, 0), (there_ref, 0)), ((far_ref, 0), (far_ref, 1))
    for same in (0, 1):
        for x in (0, 1):

            @pl.when((spots_ref[4] == same) & (spots_ref[3] == x))
            def _(same=same, x=x):
                for i in (0, 1):
                    for j in (0, 1):
                        ref, k = grid[i if same else 1 - i][j if x == 0 else 1 - j]
                        if stats_ref:
                            tail = ref[k, HEAD_DIM:].astype(F32)
                            mean = tail[0:1] + tail[1:2] + tail[2:3]
                            own_ref[i, j] = ref[k, :HEAD_DIM].astype(F32) + mean
                            spot = 2 * i + j
                            stats_ref[1][spot : spot + 1] = tail[3:4] + tail[4:5] + tail[5:6]
                        else:
                            own_ref[i, j] = ref[k]

    if stats_ref:
        values = own_ref[...].reshape(OWN, own_ref.shape[-1])
        mean = jnp.mean(values, axis=0, keepdims=True)
        off = values - mean
        stats_ref[0][0:1] = mean
        stats_ref[0][1:2] = jnp.sum(off * off, axis=0, keepdims=True)


def place(spots, here, there, far, with_stats):
    rows = here.shape[1]
    own = (2, 2, HEAD_DIM, CLIP)
    outs = [(own, F32), ((2, CLIP), F32), ((4, CLIP), F32)] if with_stats else [(own, BF)]
    return pl.pallas_call(
        place_kernel,
        in_specs=[spots_spec()] + [whole()] * 3,
        out_specs=[whole()] * len(outs),
        out_shape=[shaped(dims, kind) for dims, kind in outs],
        cost_estimate=cost(0, 8 * rows * CLIP * 6),
        name="place_in",
    )(spots, here, there, far)


def leave_kernel(spots_ref, own_ref, near_ref, far_ref):
    for same in (0, 1):
        for x in (0, 1):

            @pl.when((spots_ref[4] == same) & (spots_ref[3] == x))
            def _(same=same, x=x):
                for j in (0, 1):
                    k = j if x == 0 else 1 - j
                    near_ref[j] = own_ref[1 - same, k].astype(BF)
                    far_ref[j] = own_ref[same, k].astype(BF)


def leave(spots, own):
    dims = (2, HEAD_DIM, CLIP)
    return pl.pallas_call(
        leave_kernel,
        in_specs=[spots_spec(), whole()],
        out_specs=[whole()] * 2,
        out_shape=[shaped(dims)] * 2,
        cost_estimate=cost(0, 4 * HEAD_DIM * CLIP * 6),
        name="leave",
    )(spots, own)


def undeal_kernel(spots_ref, near_ref, far_ref, there_ref, kept_ref, sent_ref):
    for is_own in (0, 1):
        for x in (0, 1):

            @pl.when((spots_ref[2] == is_own) & (spots_ref[3] == x))
            def _(is_own=is_own, x=x):
                own = slice(x * CLIP, (x + 1) * CLIP)
                other = slice((1 - x) * CLIP, (2 - x) * CLIP)
                pair = (kept_ref, sent_ref) if is_own else (sent_ref, kept_ref)
                for k, ref in enumerate((near_ref, far_ref)):
                    pair[k][:, own] = ref[0]
                    pair[k][:, other] = there_ref[k]


def undeal(spots, near, far, there):
    dims = (HEAD_DIM, 2 * CLIP)
    return pl.pallas_call(
        undeal_kernel,
        in_specs=[spots_spec()] + [whole()] * 3,
        out_specs=[whole()] * 2,
        out_shape=[shaped(dims)] * 2,
        cost_estimate=cost(0, 16 * HEAD_DIM * CLIP * 2),
        name="undeal",
    )(spots, near, far, there)


def finish_kernel(spots_ref, kept_ref, got_ref, base_ref, shift_ref, out_ref):
    c = spots_ref[0]
    kept, got = kept_ref[...].astype(F32), got_ref[...].astype(F32)
    for half in (0, 1):
        rows = slice(half * HEAD_DIM, (half + 1) * HEAD_DIM)
        value = jnp.where(c == half, kept, got)
        out_ref[rows] = base_ref[rows] + shift_ref[rows] + value


def finish(spots, kept, got, base, shift):
    spec = pl.BlockSpec((HEAD_DIM, CLIP // 2), lambda i: (0, i))
    wide = pl.BlockSpec((2 * HEAD_DIM, CLIP // 2), lambda i: (0, i))
    return pl.pallas_call(
        finish_kernel,
        grid=(4,),
        in_specs=[spots_spec(), spec, spec, wide, fixed(shift)],
        out_specs=wide,
        out_shape=shaped(base.shape, F32),
        cost_estimate=cost(0, 8 * HEAD_DIM * 2 * CLIP * 4),
        name="finish",
    )(spots, kept, got, base, shift)


def rows_of(array, zhr, first, count, base):
    start = first + (base if array.shape[1] == OWN else 0)
    return array[zhr, start : start + count]


def pieces(weight, yr, first=0, count=OWN, base=0):
    return jnp.concatenate(
        [
            rows_of(weight[2 * yr + xr], zhr, first, count, base)
            for xr in (0, 1)
            for zhr in (0, 1)
        ]
    )


def wide_rows(weight, *rows):
    return jnp.concatenate([pieces(weight, 0, *rows), pieces(weight, 1, *rows)], axis=1)


def join_blocks(refs):
    return jnp.concatenate(
        [
            refs[2 * zlr + cr][yr, xr]
            for yr in (0, 1)
            for zlr in (0, 1)
            for xr in (0, 1)
            for cr in (0, 1)
        ]
    )


QK_ROWS = (0, 2 * HEAD_DIM, 0)
HEAD_ROWS = (0, HEAD_DIM, OWN // 2)
OUT_ROWS = (HEAD_DIM, HEAD_DIM, OWN // 2)


def project_kernel(*refs):
    blocks, w_qk, w_vo = refs[:4], refs[4:8], (*refs[4:7], refs[8])
    qs_ref, vs_ref, qk_ref, v_ref, wide_ref = refs[9:]
    wide = join_blocks(blocks)
    wide_ref[...] = wide
    result = mm(wide_rows(w_qk, *QK_ROWS), wide, 1, 0)
    for t in range(4):
        first = t * 2 * HEAD_DIM
        queries = result[first : first + HEAD_DIM] + qs_ref[t]
        qk_ref[t, 0] = queries.astype(BF)
        qk_ref[t, 1] = result[first + HEAD_DIM : first + 2 * HEAD_DIM].astype(BF)
    result = mm(wide_rows(w_vo, *HEAD_ROWS), wide, 1, 0)
    for t in range(4):
        v_ref[t] = (result[t * HEAD_DIM : (t + 1) * HEAD_DIM] + vs_ref[t]).astype(BF)


def project(blocks, weights, q_shift, v_shift):
    operands = (*blocks, *weights, q_shift, v_shift)
    outs = ((4, 2, HEAD_DIM, CLIP), (4, HEAD_DIM, CLIP), (D, CLIP))
    return pl.pallas_call(
        project_kernel,
        grid=(STEPS,),
        in_specs=[tokens_spec(b.shape) for b in blocks] + [fixed(a) for a in operands[4:]],
        out_specs=[tokens_spec(dims) for dims in outs],
        out_shape=[shaped(dims) for dims in outs],
        cost_estimate=cost(2 * 3 * OWN * D * CLIP, 4 * D * CLIP * 2),
        name="project",
    )(*operands)


def up_kernel(*refs):
    blocks, up = refs[:4], refs[4:8]
    shift_ref, act_ref, slope_ref, wide_ref = refs[8:]
    wide = join_blocks(blocks)
    wide_ref[...] = wide
    for xr in (0, 1):
        for zhr in (0, 1):
            first = (2 * xr + zhr) * OWN
            rows = slice(first, first + OWN)
            weight = jnp.concatenate([up[xr][zhr], up[2 + xr][zhr]], axis=1)
            pre = mm(weight, wide, 1, 0) + shift_ref[rows]
            cdf = 0.5 * (1.0 + lax.erf(pre * (0.5**0.5)))
            act_ref[rows] = (pre * cdf).astype(BF)
            slope_ref[rows] = cdf + pre * jnp.exp(-0.5 * pre * pre) * 0.3989422804014327


def up_project(blocks, up, in_shift):
    operands = (*blocks, *up, in_shift)
    outs = (((UNITS, CLIP), BF), ((UNITS, CLIP), F32), ((D, CLIP), BF))
    return pl.pallas_call(
        up_kernel,
        grid=(STEPS,),
        in_specs=[tokens_spec(b.shape) for b in blocks] + [fixed(a) for a in operands[4:]],
        out_specs=[tokens_spec(dims) for dims, _ in outs],
        out_shape=[shaped(dims, kind) for dims, kind in outs],
        cost_estimate=cost(2 * UNITS * D * CLIP, 6 * D * CLIP * 2),
        name="up_project",
    )(*operands)


def grad_act_kernel(*refs):
    blocks, down = refs[:4], refs[4:8]
    slope_ref, out_ref, wide_ref = refs[8:]
    wide = join_blocks(blocks)
    wide_ref[...] = wide
    for xr in (0, 1):
        for zhr in (0, 1):
            first = (2 * xr + zhr) * OWN
            rows = slice(first, first + OWN)
            weight = jnp.concatenate([down[xr][zhr], down[2 + xr][zhr]], axis=1)
            out_ref[rows] = (mm(weight, wide, 1, 0) * slope_ref[rows]).astype(BF)


def grad_act(blocks, down, slope):
    operands = (*blocks, *down, slope)
    outs = ((UNITS, CLIP), (D, CLIP))
    return pl.pallas_call(
        grad_act_kernel,
        grid=(STEPS,),
        in_specs=[tokens_spec(b.shape) for b in blocks]
        + [fixed(a) for a in down]
        + [tokens_spec(slope.shape)],
        out_specs=[tokens_spec(dims) for dims in outs],
        out_shape=[shaped(dims) for dims in outs],
        cost_estimate=cost(2 * UNITS * D * CLIP, 6 * D * CLIP * 2),
        name="grad_act",
    )(*operands)


def grad_attended_kernel(*refs):
    blocks, w_vo = refs[:4], refs[4:8]
    out_ref, wide_ref = refs[8:]
    wide = join_blocks(blocks)
    wide_ref[...] = wide
    result = mm(wide_rows(w_vo, *OUT_ROWS), wide, 1, 0)
    for t in range(4):
        out_ref[t] = result[t * HEAD_DIM : (t + 1) * HEAD_DIM].astype(BF)


def grad_attended_of(blocks, vo):
    outs = ((4, HEAD_DIM, CLIP), (D, CLIP))
    return pl.pallas_call(
        grad_attended_kernel,
        grid=(STEPS,),
        in_specs=[tokens_spec(b.shape) for b in blocks] + [fixed(a) for a in vo],
        out_specs=[tokens_spec(dims) for dims in outs],
        out_shape=[shaped(dims) for dims in outs],
        cost_estimate=cost(2 * OWN * D * CLIP, 4 * D * CLIP * 2),
        name="grad_attended",
    )(*blocks, *vo)


def fold_kernel(fill, counts, *refs):
    sources, values = refs[: counts[0]], refs[counts[0] : sum(counts)]
    keep_ref, send_ref, turned_ref = refs[sum(counts) :]

    @pl.when(pl.program_id(0) == 0)
    def _():
        for yr in (0, 1):
            turned_ref[yr * HALF : (yr + 1) * HALF] = jnp.transpose(fill(sources, yr))

    value = jnp.concatenate([ref[...].reshape(-1, BLOCK) for ref in values])
    for yr in (0, 1):
        result = mm(turned_ref[yr * HALF : (yr + 1) * HALF], value, 1, 0)
        for spot in range(8):
            part = result[spot * HEAD_DIM : (spot + 1) * HEAD_DIM]
            zlr, xr, cr = spot >> 2, spot >> 1 & 1, spot & 1
            if cr == 0:
                keep_ref[zlr, yr, xr] = part
            else:
                send_ref[zlr, yr, xr] = part.astype(BF)


def fold(fill, sources, values, name):
    depth = sum(v.size // CLIP for v in values)
    dims = (2, 2, 2, HEAD_DIM, CLIP)
    return pl.pallas_call(
        functools.partial(fold_kernel, fill, (len(sources), len(values))),
        grid=(STEPS,),
        in_specs=[fixed(a) for a in sources] + [tokens_spec(v.shape) for v in values],
        out_specs=[tokens_spec(dims)] * 2,
        out_shape=[shaped(dims, F32), shaped(dims)],
        scratch_shapes=[pltpu.VMEM((D, depth), BF)],
        cost_estimate=cost(2 * D * depth * CLIP, 6 * D * CLIP * 2),
        name=name,
    )(*sources, *values)


def fill_out(sources, yr):
    return pieces(sources, yr, *OUT_ROWS)


def fill_all(sources, yr):
    return pieces(sources, yr)


def fill_project(sources, yr):
    return jnp.concatenate(
        [
            pieces(sources[:4], yr, *QK_ROWS),
            pieces((*sources[:3], sources[4]), yr, *HEAD_ROWS),
        ]
    )


def pair_y_kernel(left_ref, right_ref, keep_ref, first_ref, later_ref):
    result = mm(left_ref[0], right_ref[...], 1, 1)
    keep_ref[0] = result[:, :HALF]
    far = result[:, HALF:].astype(BF)

    @pl.when(pl.program_id(0) < 2)
    def _():
        first_ref[0] = far

    @pl.when(pl.program_id(0) >= 2)
    def _():
        later_ref[0] = far


def grad_y_first(left, right, name):
    rows = left.shape[1]
    return pl.pallas_call(
        pair_y_kernel,
        grid=(4,),
        in_specs=[pl.BlockSpec((1, rows, CLIP), lambda i: (i ^ 2, 0, 0)), fixed(right)],
        out_specs=[
            pl.BlockSpec((1, rows, HALF), lambda i: (i ^ 2, 0, 0)),
            pl.BlockSpec((1, rows, HALF), lambda i: (jnp.minimum(i, 1), 0, 0)),
            pl.BlockSpec((1, rows, HALF), lambda i: (jnp.maximum(i - 2, 0), 0, 0)),
        ],
        out_shape=[shaped((4, rows, HALF), F32)] + [shaped((2, rows, HALF))] * 2,
        cost_estimate=cost(2 * 4 * rows * D * CLIP, 4 * rows * D * 6),
        name=name,
    )(left, right)


def pair_x_kernel(count, *refs):
    keep_ref, *send_refs = refs[2 * count :]
    start = 0
    for left_ref, right_ref in zip(refs[:count], refs[count : 2 * count]):
        rows = slice(start, start + left_ref.shape[2])
        start += left_ref.shape[2]
        for xr in (0, 1):
            result = mm(left_ref[xr, 0], right_ref[...], 1, 1)
            for yr in (0, 1):
                part = result[:, yr * HALF : (yr + 1) * HALF]
                if xr == 0:
                    keep_ref[yr, 0, rows] = part
                else:
                    send_refs[1 - yr][0, rows] = part.astype(BF)


def grad_x_first(lefts, rights, name):
    rows = sum(v.shape[2] for v in lefts)
    send = pl.BlockSpec((1, rows, HALF), lambda i: (i, 0, 0))
    return pl.pallas_call(
        functools.partial(pair_x_kernel, len(lefts)),
        grid=(2,),
        in_specs=[pl.BlockSpec((2, 1) + v.shape[2:], lambda i: (0, i, 0, 0)) for v in lefts]
        + [fixed(v) for v in rights],
        out_specs=[pl.BlockSpec((2, 1, rows, HALF), lambda i: (0, i, 0, 0)), send, send],
        out_shape=[shaped((2, 2, rows, HALF), F32)] + [shaped((2, rows, HALF))] * 2,
        cost_estimate=cost(2 * 4 * rows * D * CLIP, 4 * rows * D * 6),
        name=name,
    )(*lefts, *rights)


def token_stats(values):
    mean = jnp.mean(values, axis=0)
    off = values - mean
    return jnp.stack([mean, jnp.sum(off * off, axis=0)])


def swap_both(values):
    route = [(8 * r + q, 8 * (r ^ 1) + (q ^ 2)) for r in range(4) for q in range(8)]
    return lax.ppermute(values, ("row", "col"), route)


def group_round(values):
    return values, swap_core(values), swap_zl(values), swap_both(values)


def merge_in_turn(stats, count):
    for swap in (swap_core, swap_zl):
        other = swap(stats)
        apart = other[0] - stats[0]
        total = stats[1] + other[1] + apart * apart * (0.5 * count)
        stats = jnp.stack([0.5 * (stats[0] + other[0]), total])
        count = 2 * count
    return stats[0], stats[1] / count


def merge_stats(stats, count):
    stats = group_round(stats)
    mean = sum(s[0] for s in stats) * 0.25
    total = sum(s[1] + count * jnp.square(s[0] - mean) for s in stats)
    return mean, total / (4 * count)


def after(values, *others):
    return lax.optimization_barrier((values, others))[0]


def local_clip(
    hidden_in,
    lengths,
    ln1_gain,
    ln1_shift,
    qkv_weight,
    qv_bias,
    out_weight,
    out_bias,
    ln2_gain,
    ln2_shift,
    in_weight,
    in_bias,
    down_weight,
    down_bias,
    cotangent,
):
    row, col = lax.axis_index("row"), lax.axis_index("col")
    y, c = row // 2, row % 2
    zh, zl, x = col // 4, col // 2 % 2, col % 2
    same_zy = y == zh
    spots = jnp.stack([c, zl == c, zh == c, x, same_zy]).astype(jnp.int32)

    def flip(grid):
        grid = jnp.where(same_zy, grid, grid[::-1])
        return jnp.where(x == 0, grid, grid[:, ::-1])

    def fold_cores(parts):
        got = swap_core(parts[1])
        return parts[0][0] + got[0], (parts[0][1] + got[1]).astype(BF)

    pack = jnp.concatenate(
        [
            jnp.stack(
                [ln1_gain, ln1_shift, ln2_gain, ln2_shift, out_bias, qv_bias[0], qv_bias[1]]
            )
            .reshape(7, 2, HEAD_DIM)
            .transpose(1, 0, 2)
            .reshape(2, 7 * HEAD_DIM),
            in_bias.reshape(2, OWN),
            jnp.zeros((2, CLIP - 11 * HEAD_DIM), F32),
        ],
        axis=1,
    )
    kept, sent = prepare(
        spots,
        jnp.swapaxes(qkv_weight, 1, 2),
        out_weight,
        in_weight,
        jnp.swapaxes(down_weight, 0, 1),
    )
    weights_got = swap_core(sent)
    h_kept, h_sent, c_kept, c_sent = split(spots, after(hidden_in, sent), cotangent, pack)
    s_at, s_up, s_down = join_lanes(spots, kept, weights_got)
    at_zh = swap_zh(s_at)
    h_here, h_send = deal(spots, after(h_kept, s_at), swap_core(h_sent))
    h_there = swap_x(h_send)
    c_got = swap_core(after(c_sent, h_send))

    h_there, at_zh = lax.optimization_barrier((h_there, at_zh))
    h_message = jnp.stack([h_here[1], h_there[1]])
    h_far = swap_zh(h_message)
    at_one = jnp.stack([s_at, at_zh])
    at_x, at_y = swap_x(at_one), swap_y(at_one)
    c_here, c_send = deal(spots, after(c_kept, at_one, h_message), c_got)
    c_there = swap_x(c_send)
    h_far, c_there = lax.optimization_barrier(after((h_far, c_there), at_one))

    hidden_own, stats, owned = place(spots, h_here, h_there, h_far, True)
    owned = owned[:, : 11 * HEAD_DIM].reshape(2, 2, 11, HEAD_DIM)
    gain_one, shift_one, gain_two, shift_two, out_shift = (
        owned[:, :, i, :, None] for i in range(5)
    )
    by_head = flip(owned).transpose(1, 0, 2, 3)
    q_shift = by_head[:, :, 5].reshape(4, HEAD_DIM, 1)
    v_shift = by_head[:, :, 6].reshape(4, HEAD_DIM, 1)
    in_shift = by_head[:, :, 7:].reshape(UNITS, 1)

    mean, variance = merge_stats(stats, OWN)
    inv_one = lax.rsqrt(variance + EPS)
    s_up = after(s_up, h_far)
    up_zh = swap_zh(s_up)
    inv_one, at_x, at_y = lax.optimization_barrier((inv_one, at_x, at_y))
    own_one = (hidden_own - mean) * inv_one
    qk_xy, vo_xy = swap_y(at_x[:, : OWN // 2]), swap_x(at_y[:, OWN // 2 :])
    low_one = (own_one * gain_one + shift_one).astype(BF)
    low_one_z = swap_zl(low_one)
    low_one_z, qk_xy, vo_xy, up_zh = lax.optimization_barrier((low_one_z, qk_xy, vo_xy, up_zh))
    w_qk = at_one, at_x, at_y, qk_xy
    w_vo = at_one, at_x, at_y, vo_xy
    s_down, c_message = after((s_down, jnp.stack([c_here[1], c_there[1]])), low_one_z)
    down_zh = swap_zh(s_down)
    up_one = jnp.stack([s_up, up_zh])
    up_x, up_y = swap_x(after(up_one, vo_xy)), swap_y(after(up_one, qk_xy))
    wide_one = low_one, swap_core(low_one), low_one_z, swap_core(low_one_z)
    wide_one = after(wide_one, s_down, up_one, c_message)

    qk, values, ln_one = project(wide_one, (*w_qk, vo_xy), q_shift, v_shift)
    clip_len = lax.dynamic_slice_in_dim(lengths, 4 * y + 2 * zh + x, 1)
    c_message = after(c_message, qk)
    c_far = swap_zh(c_message)
    attended, log_sum = attend_clip(after(qk, c_message), values, clip_len, CLIP)
    attended, up_x, up_y = lax.optimization_barrier((attended, up_x, up_y))
    w_up = up_one, up_x, up_y, swap_y(up_x)
    delta = fold(fill_out, w_vo, (attended,), "fold_out")
    *delta, c_far, down_zh = lax.optimization_barrier((*delta, c_far, down_zh))
    down_one = jnp.stack([s_down, down_zh])
    down_x, down_y = swap_x(down_one), swap_y(down_one)
    delta_near, delta_send = fold_cores(delta)
    delta_got, down_x, down_y = lax.optimization_barrier((swap_zl(delta_send), down_x, down_y))
    w_down = down_one, down_x, down_y, swap_x(down_y)
    delta_mid = delta_near + delta_got + out_shift

    hidden_mid = hidden_own + delta_mid
    mean, variance = merge_stats(token_stats(hidden_mid.reshape(OWN, CLIP)), OWN)
    inv_two = lax.rsqrt(variance + EPS)
    own_two = (hidden_mid - mean) * inv_two
    low_two = (own_two * gain_two + shift_two).astype(BF)
    low_two_z = swap_zl(low_two)
    (cot_own,) = place(spots, c_here, c_there, after(c_far, low_two), False)
    low_two_z, cot_own, in_shift = lax.optimization_barrier((low_two_z, cot_own, in_shift))
    cot_z = swap_zl(cot_own)
    wide_two = low_two, swap_core(low_two), low_two_z, swap_core(low_two_z)
    act_low, slope, ln_two = up_project(after(wide_two, cot_own), w_up, in_shift)
    out_parts = fold(fill_all, w_down, (act_low,), "fold_down")
    *out_parts, cot_z = lax.optimization_barrier((*out_parts, cot_z))
    wide_cot = cot_own, swap_core(cot_own), cot_z, swap_core(cot_z)
    out_near, out_send = fold_cores(out_parts)
    out_got = swap_zl(out_send)

    grad_pre, cot_all = grad_act(after(wide_cot, out_send), w_down, slope)
    two_parts = fold(fill_all, w_up, (grad_pre,), "fold_up")
    *two_parts, out_got = lax.optimization_barrier((*two_parts, out_got))
    two_near, two_send = fold_cores(two_parts)
    two_got = swap_zl(two_send)
    by_unit = (2, 2, OWN, CLIP)
    act_low_after, cot_all_after = after((act_low, cot_all), two_send)
    part_down = grad_x_first((act_low_after.reshape(by_unit),), (cot_all_after,), "grad_down")
    down_keep, down_first, down_later = part_down
    down_first = swap_x(down_first)
    part_up = grad_y_first(
        after(grad_pre, part_down[1]).reshape(4, OWN, CLIP), ln_two, "grad_up"
    )
    up_keep, up_first, up_later = part_up
    up_keep = up_keep.reshape(2, 2, OWN, HALF)
    up_first = swap_y(up_first)
    two_got = after(two_got, part_up[1])
    grad_two = two_near + two_got

    def norm_back(grad, normed, inv, gain, meanwhile=()):
        scaled = grad * gain
        sums = jnp.stack([jnp.sum(scaled, axis=(0, 1, 2)), jnp.sum(scaled * normed, axis=(0, 1, 2))])
        sums, meanwhile = lax.optimization_barrier((sum(group_round(sums)) / D, meanwhile))
        return inv * (scaled - sums[0] - normed * sums[1]), meanwhile

    norm_two_grad, down_first = norm_back(grad_two, own_two, inv_two, gain_two, down_first)
    mid_own = cot_own.astype(F32) + norm_two_grad
    mid_low = mid_own.astype(BF)
    mid_z = swap_zl(mid_low)
    out_leave, out_leave_far = leave(spots, delta_mid + after(out_near, mid_low) + out_got)
    down_first, down_later = after((down_first, down_later), mid_low)
    down_later = swap_x(down_later)
    down_send = (down_keep[1] + down_first).astype(BF)
    down_second = swap_y(down_send)
    out_leave_far, mid_z, up_first = lax.optimization_barrier(
        after((out_leave_far, mid_z, up_first), down_send)
    )
    up_later = swap_y(after(up_later, up_first))
    up_send = (up_keep[1] + up_first).astype(BF)
    up_second = swap_x(up_send)
    out_far = swap_zh(out_leave_far)
    wide_mid = mid_low, swap_core(mid_low), mid_z, swap_core(mid_z)
    wide_mid = after(wide_mid, out_leave_far, up_send)

    def last_step(keep, later, second):
        total = keep[0] + later + second
        return total[0], total[1].astype(BF)

    grad_attended, mid_all = grad_attended_of(wide_mid, w_vo)
    early = attend_clip_back(qk, values, log_sum, grad_attended, clip_len, 0)
    *early, down_later, down_second, out_far = lax.optimization_barrier(
        (*early, down_later, down_second, out_far)
    )
    down_keep, down_send = last_step(down_keep, down_later, down_second)
    down_third = swap_zh(down_send)
    out_message = jnp.stack([out_leave[1], out_far[1]])
    out_there = swap_x(out_message)
    grad_attended = after(grad_attended, down_send, out_message)
    grad_qk, grad_v = attend_clip_back(
        qk, values, log_sum, grad_attended, clip_len, 2, tuple(early)
    )
    grad_qk, grad_v, up_later, up_second = lax.optimization_barrier(
        (grad_qk, grad_v, up_later, up_second)
    )
    up_keep, up_send = last_step(up_keep, up_later, up_second)
    folded = fold(fill_project, (*w_qk, vo_xy), after((grad_qk, grad_v), up_send), "fold_project")
    *folded, down_third = lax.optimization_barrier((*folded, down_third))
    one_near, one_send = fold_cores(folded)
    one_got = swap_zl(one_send)
    by_head_dims = (2, 2, HEAD_DIM, CLIP)
    grad_v, grad_qk = after((grad_v, grad_qk), one_send)
    part_vo = grad_x_first(
        (grad_v.reshape(by_head_dims), attended.reshape(by_head_dims)),
        (ln_one, mid_all),
        "grad_vo",
    )
    *part_vo, one_got = lax.optimization_barrier((*part_vo, one_got))
    vo_keep, vo_first, vo_later = part_vo
    vo_first = swap_x(vo_first)
    part_qk = grad_y_first(
        after(grad_qk, part_vo[1]).reshape(4, 2 * HEAD_DIM, CLIP), ln_one, "grad_qk"
    )
    qk_keep, qk_first, qk_later = part_qk
    qk_keep = qk_keep.reshape(2, 2, 2 * HEAD_DIM, HALF)
    qk_first = swap_y(qk_first)
    grad_one = one_near + one_got

    def over_tokens(values):
        return jnp.sum(values, axis=-1, dtype=F32)

    owned = jnp.stack(
        [
            over_tokens(v)
            for v in (
                grad_one * own_one,
                grad_one,
                grad_two * own_two,
                grad_two,
                mid_own,
                cot_own.astype(F32),
            )
        ],
        axis=2,
    ).reshape(2, 2, -1)
    heads = jnp.concatenate(
        [
            over_tokens(grad_qk[:, 0].astype(F32)),
            over_tokens(grad_v.astype(F32)),
            over_tokens(grad_pre.astype(F32)).reshape(4, OWN),
        ],
        axis=1,
    )
    vectors = jnp.concatenate([flip(owned), heads.reshape(2, 2, -1).transpose(1, 0, 2)], axis=2)
    vectors_got = swap_zh(vectors[1])

    up_third = swap_zh(after(up_send, one_got, vectors[1]))
    norm_one_grad, (qk_first, vo_first, up_third) = norm_back(
        grad_one, own_one, inv_one, gain_one, (qk_first, vo_first, up_third)
    )
    qk_first, vo_first = after((qk_first, vo_first), norm_one_grad)
    vo_later = swap_x(after(vo_later, vo_first))
    vo_send = (vo_keep[1] + vo_first).astype(BF)
    vo_second = swap_y(vo_send)
    qk_later = swap_y(after(qk_later, qk_first))
    qk_send = (qk_keep[1] + qk_first).astype(BF)
    qk_second = swap_x(qk_send)
    in_leave, in_leave_far = leave(spots, norm_two_grad + norm_one_grad)
    in_far = swap_zh(in_leave_far)
    out_kept, out_sent = undeal(spots, out_leave, out_far, after(out_there, in_leave_far))
    hidden_out = finish(spots, out_kept, swap_core(out_sent), hidden_in, down_bias[:, None])

    vo_later, vo_second = after((vo_later, vo_second), in_leave_far, qk_send)
    vo_keep, vo_send = last_step(vo_keep, vo_later, vo_second)
    vo_third = swap_zh(vo_send)
    ff_kept, ff_sent = store_ff(
        spots, after(up_keep, vo_send) + up_third, down_keep + down_third
    )
    ff_got = swap_core(ff_sent)
    in_far, qk_later, qk_second = lax.optimization_barrier(
        after((in_far, qk_later, qk_second), ff_sent)
    )
    in_message = jnp.stack([in_leave[1], in_far[1]])
    in_there = after(swap_x(in_message), hidden_out)
    qk_later, qk_second = after((qk_later, qk_second), in_message)
    qk_keep, qk_send = last_step(qk_keep, qk_later, qk_second)
    qk_third = swap_zh(qk_send)
    g_up, g_down = join_ff(spots, ff_kept, after(ff_got, qk_send, in_message))

    total = vectors[0] + after(vectors_got, in_leave_far)
    total = after(total, in_there)
    total = total[0] + swap_x(total[1])
    total = total + swap_y(total)
    other = swap_core(total)
    both = jnp.where(c == 0, jnp.stack([total, other]), jnp.stack([other, total]))
    singles = both[:, : 8 * HEAD_DIM].reshape(2, 8, HEAD_DIM).transpose(1, 0, 2).reshape(8, -1)

    in_kept, in_sent = undeal(spots, in_leave, in_far, in_there)
    no_shift = jnp.zeros((2 * HEAD_DIM, 1), F32)
    hidden_grad = finish(spots, in_kept, swap_core(in_sent), cotangent, no_shift)
    qk_third, vo_third = after((qk_third, vo_third), other, g_up, g_down, hidden_out)
    at_kept, at_sent = store_qkvo(spots, qk_keep + qk_third, vo_keep + vo_third)
    g_qkv, g_out = join_qkvo(spots, at_kept, swap_core(at_sent))

    return (
        hidden_out,
        hidden_grad,
        singles[0],
        singles[1],
        jnp.swapaxes(g_qkv, 1, 2),
        singles[6:8],
        g_out,
        singles[4],
        singles[2],
        singles[3],
        g_up,
        both[:, 8 * HEAD_DIM :].reshape(-1),
        jnp.swapaxes(g_down, 0, 1),
        singles[5],
    )


def solution(mesh):
    sizes = dict(mesh.shape)

    def program(*arrays):
        small = sizes == {"row": 4, "col": 8} and arrays[0].shape == (D, 2 * sizes["row"] * CLIP)
        return mapped(local_clip if small else local, mesh)(*arrays)

    return program


def mapped(body, mesh):
    return jax.shard_map(
        body,
        mesh=mesh,
        in_specs=(
            P("col", "row"),
            P(),
            P("col"),
            P("col"),
            P(None, "row", "col"),
            P(None, "col"),
            P("col", "row"),
            P("col"),
            P("col"),
            P("col"),
            P("row", "col"),
            P("col"),
            P("col", "row"),
            P("col"),
            P("col", "row"),
        ),
        out_specs=(
            P("col", "row"),
            P("col", "row"),
            P("col"),
            P("col"),
            P(None, "row", "col"),
            P(None, "col"),
            P("col", "row"),
            P("col"),
            P("col"),
            P("col"),
            P("row", "col"),
            P("col"),
            P("col", "row"),
            P("col"),
        ),
        check_vma=False,
    )
```

```python
import functools

import jax
import jax.numpy as jnp
from jax import lax
from jax.experimental import pallas as pl
from jax.experimental.pallas import tpu as pltpu
from jax.sharding import PartitionSpec as P

HEADS = 16
HEAD_DIM = 80
D = 1280
MICRO = 2
GROUP = 8


EPS = 1e-05


def partner(block, axis, distance):
    count = lax.axis_size(axis)
    route = []
    for low in range(count):
        high = low | 1 << distance
        if high != low and high < count:
            route += [(low, high), (high, low)]
    return lax.ppermute(block, axis, route)


def row_totals(first_sum, second_sum):
    return lax.psum((first_sum, second_sum), "col")


def widen(values):
    return lax.all_gather(values, "col", axis=1, tiled=True)


def narrow(values):
    return lax.psum_scatter(values, "col", scatter_dimension=1, tiled=True)


def to_clips(stacked):
    return lax.all_to_all(stacked, "col", split_axis=1, concat_axis=2, tiled=True)


def to_columns(stacked):
    return lax.all_to_all(stacked, "col", split_axis=2, concat_axis=1, tiled=True)


def contract_rows(left, right):
    return lax.dot_general(
        left, right, (((0,), (0,)), ((), ())), preferred_element_type=jnp.float32
    )


def contract_cols(left, right):
    return lax.dot_general(
        left, right, (((1,), (1,)), ((), ())), preferred_element_type=jnp.float32
    )


def exact_gelu(values):
    return jax.nn.gelu(values, approximate=False)


def norm_forward(values, norm_gain, norm_shift):
    first_sum, second_sum = row_totals(jnp.sum(values, axis=1), jnp.sum(values * values, axis=1))
    mean_rows = first_sum / D
    inv_std = lax.rsqrt(second_sum / D - mean_rows * mean_rows + EPS)
    normed = (values - mean_rows[:, None]) * inv_std[:, None]
    return (normed, inv_std, normed * norm_gain + norm_shift)


def norm_backward(grad_out, normed, inv_std, norm_gain):
    scaled = grad_out * norm_gain
    first_sum, second_sum = row_totals(jnp.sum(scaled, axis=1), jnp.sum(scaled * normed, axis=1))
    grad_input = inv_std[:, None] * (
        scaled - first_sum[:, None] / D - normed * (second_sum[:, None] / D)
    )
    return (grad_input, jnp.sum(grad_out * normed, axis=0), jnp.sum(grad_out, axis=0))


def split_heads(values):
    return values.reshape(values.shape[0], HEADS, HEAD_DIM)


def gather_clip(key_rows, value_rows):
    position = lax.axis_index("col")
    for bit_index in range(GROUP.bit_length() - 1):
        other_keys, other_values = partner((key_rows, value_rows), "col", bit_index)
        upper_half = position >> bit_index & 1 == 1
        key_rows = jnp.where(
            upper_half,
            jnp.concatenate([other_keys, key_rows]),
            jnp.concatenate([key_rows, other_keys]),
        )
        value_rows = jnp.where(
            upper_half,
            jnp.concatenate([other_values, value_rows]),
            jnp.concatenate([value_rows, other_values]),
        )
    return (key_rows, value_rows)


def scatter_clip(grad_keys, grad_values):
    position = lax.axis_index("col")
    for bit_index in reversed(range(GROUP.bit_length() - 1)):
        half_rows = grad_keys.shape[0] // 2
        upper_half = position >> bit_index & 1 == 1
        keep_keys = jnp.where(upper_half, grad_keys[half_rows:], grad_keys[:half_rows])
        send_keys = jnp.where(upper_half, grad_keys[:half_rows], grad_keys[half_rows:])
        keep_values = jnp.where(upper_half, grad_values[half_rows:], grad_values[:half_rows])
        send_values = jnp.where(upper_half, grad_values[:half_rows], grad_values[half_rows:])
        got_keys, got_values = partner((send_keys, send_values), "col", bit_index)
        grad_keys = keep_keys + got_keys
        grad_values = keep_values + got_values
    return (grad_keys, grad_values)


def clip_scores(queries, key_rows, valid_len):
    scale_factor = HEAD_DIM ** (-0.5)
    scores = (
        jnp.einsum(
            "qhe,khe->hqk",
            split_heads(queries),
            split_heads(key_rows),
            preferred_element_type=jnp.float32,
        )
        * scale_factor
    )
    live_keys = lax.broadcasted_iota(jnp.int32, (1, 1, key_rows.shape[0]), 2) < valid_len
    return jnp.where(live_keys, scores, -1e30)


def attend(queries, key_rows, value_rows, valid_len):
    scores = clip_scores(queries, key_rows, valid_len)
    top_score = jnp.max(scores, axis=2, keepdims=True)
    weights = jnp.exp(scores - top_score)
    weight_sum = jnp.sum(weights, axis=2, keepdims=True)
    prob_low = (weights / weight_sum).astype(jnp.bfloat16)
    attended = jnp.einsum(
        "hqk,khe->qhe", prob_low, split_heads(value_rows), preferred_element_type=jnp.float32
    )
    return (attended.reshape(queries.shape[0], -1), top_score + jnp.log(weight_sum))


def attend_back(queries, key_rows, value_rows, valid_len, log_sum, grad_low):
    scale_factor = HEAD_DIM ** (-0.5)
    scores = clip_scores(queries, key_rows, valid_len)
    probs_full = jnp.exp(scores - log_sum)
    grad_heads = split_heads(grad_low)
    grad_value = jnp.einsum(
        "hqk,qhe->khe",
        probs_full.astype(jnp.bfloat16),
        grad_heads,
        preferred_element_type=jnp.float32,
    )
    grad_probs = jnp.einsum(
        "qhe,khe->hqk", grad_heads, split_heads(value_rows), preferred_element_type=jnp.float32
    )
    row_dot = jnp.sum(probs_full * grad_probs, axis=2, keepdims=True)
    grad_scores = (probs_full * (grad_probs - row_dot)).astype(jnp.bfloat16)
    grad_query = (
        jnp.einsum(
            "hqk,khe->qhe", grad_scores, split_heads(key_rows), preferred_element_type=jnp.float32
        )
        * scale_factor
    )
    grad_key = (
        jnp.einsum(
            "hqk,qhe->khe", grad_scores, split_heads(queries), preferred_element_type=jnp.float32
        )
        * scale_factor
    )
    return (
        grad_query.reshape(queries.shape[0], -1),
        grad_key.reshape(key_rows.shape[0], -1),
        grad_value.reshape(key_rows.shape[0], -1),
    )


def layer_pass(input_rows, grad_rows, weights, vectors, valid_len):
    qkv_full, out_full, in_full, down_full = weights
    gain_one, shift_one, qv_full, out_shift, gain_two, shift_two, in_shift, down_shift = vectors
    bias_three = jnp.stack([qv_full[0], jnp.zeros_like(qv_full[0]), qv_full[1]])[:, None, :]
    normed_one, inv_one, ln_one = norm_forward(input_rows, gain_one, shift_one)
    wide_one = widen(ln_one.astype(jnp.bfloat16))
    projected = (
        jnp.einsum("td,sdc->stc", wide_one, qkv_full, preferred_element_type=jnp.float32)
        + bias_three
    )
    projected = to_clips(projected.astype(jnp.bfloat16))
    key_rows, value_rows = gather_clip(projected[1], projected[2])
    attended, log_sum = attend(projected[0], key_rows, value_rows, valid_len)
    attended_low = to_columns(attended.astype(jnp.bfloat16)[None])[0]
    hidden_mid = (
        input_rows
        + narrow(jnp.dot(attended_low, out_full, preferred_element_type=jnp.float32))
        + out_shift
    )
    normed_two, inv_two, ln_two = norm_forward(hidden_mid, gain_two, shift_two)
    wide_two = widen(ln_two.astype(jnp.bfloat16))
    pre_act = jnp.dot(wide_two, in_full, preferred_element_type=jnp.float32) + in_shift
    act_value, gelu_back = jax.vjp(exact_gelu, pre_act)
    act_low = act_value.astype(jnp.bfloat16)
    hidden_out = (
        hidden_mid
        + narrow(jnp.dot(act_low, down_full, preferred_element_type=jnp.float32))
        + down_shift
    )
    grad_wide = widen(grad_rows.astype(jnp.bfloat16))
    grad_down = contract_rows(act_low, grad_wide)
    grad_pre = gelu_back(contract_cols(grad_wide, down_full))[0].astype(jnp.bfloat16)
    grad_in = contract_rows(wide_two, grad_pre)
    grad_ln_two = narrow(contract_cols(grad_pre, in_full))
    grad_norm_two, grad_gain_two, grad_shift_two = norm_backward(
        grad_ln_two, normed_two, inv_two, gain_two
    )
    grad_mid = grad_rows + grad_norm_two
    grad_mid_wide = widen(grad_mid.astype(jnp.bfloat16))
    grad_out = contract_rows(attended_low, grad_mid_wide)
    grad_attended = to_clips(contract_cols(grad_mid_wide, out_full).astype(jnp.bfloat16)[None])[0]
    grad_query, grad_key, grad_value = attend_back(
        projected[0], key_rows, value_rows, valid_len, log_sum, grad_attended
    )
    grad_key, grad_value = scatter_clip(grad_key, grad_value)
    grad_proj = to_columns(jnp.stack([grad_query, grad_key, grad_value]).astype(jnp.bfloat16))
    grad_qkv = jnp.einsum("td,stc->sdc", wide_one, grad_proj, preferred_element_type=jnp.float32)
    grad_ln_one = narrow(
        jnp.einsum("stc,sdc->td", grad_proj, qkv_full, preferred_element_type=jnp.float32)
    )
    grad_norm_one, grad_gain_one, grad_shift_one = norm_backward(
        grad_ln_one, normed_one, inv_one, gain_one
    )
    grad_input = grad_mid + grad_norm_one
    proj_sums = jnp.sum(grad_proj, axis=1, dtype=jnp.float32)
    vector_parts = (
        grad_gain_one,
        grad_shift_one,
        jnp.stack([proj_sums[0], proj_sums[2]]),
        jnp.sum(grad_mid, axis=0),
        grad_gain_two,
        grad_shift_two,
        jnp.sum(grad_pre, axis=0, dtype=jnp.float32),
        jnp.sum(grad_rows, axis=0),
    )
    return (hidden_out, grad_input, (grad_qkv, grad_out, grad_in, grad_down), vector_parts)


def tile_grid(vector, row_count):
    return jnp.broadcast_to(vector[None], (row_count,) + vector.shape)


def grid_reduce(partials, vector_parts):
    row_count = lax.axis_size("row")
    qkv_part, out_part, in_part, down_part = partials
    qkv_blocks = qkv_part.reshape(3, row_count, -1, qkv_part.shape[2]).transpose(1, 0, 2, 3)
    out_blocks = out_part.reshape(out_part.shape[0], row_count, -1).transpose(1, 0, 2)
    in_blocks = in_part.reshape(row_count, -1, in_part.shape[1])
    down_blocks = down_part.reshape(down_part.shape[0], row_count, -1).transpose(1, 0, 2)
    tiled = [tile_grid(vector, row_count) for vector in vector_parts]
    reduced = (
        lax.psum_scatter(qkv_blocks, "row", scatter_dimension=0, tiled=True),
        lax.psum_scatter(out_blocks, "row", scatter_dimension=0, tiled=True),
        lax.psum_scatter(in_blocks, "row", scatter_dimension=0, tiled=True),
        lax.psum_scatter(down_blocks, "row", scatter_dimension=0, tiled=True),
        lax.psum_scatter(tiled[0], "row", scatter_dimension=0, tiled=True),
        lax.psum_scatter(tiled[1], "row", scatter_dimension=0, tiled=True),
        lax.psum_scatter(tiled[2], "row", scatter_dimension=0, tiled=True),
        lax.psum_scatter(tiled[3], "row", scatter_dimension=0, tiled=True),
        lax.psum_scatter(tiled[4], "row", scatter_dimension=0, tiled=True),
        lax.psum_scatter(tiled[5], "row", scatter_dimension=0, tiled=True),
        lax.psum_scatter(tiled[6], "row", scatter_dimension=0, tiled=True),
        lax.psum_scatter(tiled[7], "row", scatter_dimension=0, tiled=True),
    )
    return tuple((piece[0] for piece in reduced))


def local(
    hidden_in,
    lengths,
    ln1_gain,
    ln1_shift,
    qkv_weight,
    qv_bias,
    out_weight,
    out_bias,
    ln2_gain,
    ln2_shift,
    in_weight,
    in_bias,
    down_weight,
    down_bias,
    cotangent,
):
    col_count = lax.axis_size("col")
    token_rows = jnp.transpose(hidden_in)
    cot_rows = jnp.transpose(cotangent)
    rows_block = token_rows.shape[0] // MICRO
    weights = (
        lax.all_gather(qkv_weight, "row", axis=1, tiled=True),
        lax.all_gather(out_weight, "row", axis=1, tiled=True),
        lax.all_gather(in_weight, "row", axis=0, tiled=True),
        lax.all_gather(down_weight, "row", axis=1, tiled=True),
    )
    vectors = (ln1_gain, ln1_shift, qv_bias, out_bias, ln2_gain, ln2_shift, in_bias, down_bias)
    clip_slot = lax.axis_index("col") // GROUP
    outputs = []
    input_grads = []
    totals = None
    running = None
    for micro_index in range(MICRO):
        input_rows = token_rows[micro_index * rows_block : (micro_index + 1) * rows_block]
        grad_rows = cot_rows[micro_index * rows_block : (micro_index + 1) * rows_block]
        clip_id = (lax.axis_index("row") * MICRO + micro_index) * (col_count // GROUP) + clip_slot
        valid_len = lax.dynamic_index_in_dim(lengths, clip_id, keepdims=False)
        out_rows, back_rows, partials, vector_parts = layer_pass(
            input_rows, grad_rows, weights, vectors, valid_len
        )
        outputs.append(out_rows)
        input_grads.append(back_rows)
        current = (partials, vector_parts)
        running = current if running is None else jax.tree.map(jnp.add, running, current)
    totals = grid_reduce(running[0], running[1])
    (
        grad_qkv,
        grad_out,
        grad_in,
        grad_down,
        grad_gain_one,
        grad_shift_one,
        grad_qv,
        grad_out_shift,
        grad_gain_two,
        grad_shift_two,
        grad_in_shift,
        grad_down_shift,
    ) = totals
    hidden_out = jnp.transpose(jnp.concatenate(outputs, axis=0))
    hidden_grad = jnp.transpose(jnp.concatenate(input_grads, axis=0))
    return (
        hidden_out,
        hidden_grad,
        grad_gain_one,
        grad_shift_one,
        grad_qkv,
        grad_qv,
        grad_out,
        grad_out_shift,
        grad_gain_two,
        grad_shift_two,
        grad_in,
        grad_in_shift,
        grad_down,
        grad_down_shift,
    )


CLIP = 1024
FF = 5120
OWN = D // 4
UNITS = FF // 4
HALF = D // 2
BLOCK = 256
STEPS = CLIP // BLOCK
BF = jnp.bfloat16
F32 = jnp.float32


def swap_core(values):
    return lax.ppermute(values, "row", [(i, i ^ 1) for i in range(4)])


def swap_y(values):
    return lax.ppermute(values, "row", [(i, i ^ 2) for i in range(4)])


def swap_x(values):
    return lax.ppermute(values, "col", [(i, i ^ 1) for i in range(8)])


def swap_zl(values):
    return lax.ppermute(values, "col", [(i, i ^ 2) for i in range(8)])


def swap_zh(values):
    return lax.ppermute(values, "col", [(i, i ^ 4) for i in range(8)])


def pick(values, index, axis=0):
    return lax.dynamic_index_in_dim(values, index, axis, keepdims=False)


def mm(left, right, left_dim, right_dim):
    return lax.dot_general(
        left, right, (((left_dim,), (right_dim,)), ((), ())), preferred_element_type=F32
    )


def shaped(dims, kind=BF):
    return jax.ShapeDtypeStruct(dims, kind)


def spots_spec():
    return pl.BlockSpec(memory_space=pltpu.SMEM)


def fixed(array):
    rank = len(array.shape)
    return pl.BlockSpec(array.shape, lambda i: (0,) * rank)


def tokens_spec(dims):
    lead = tuple(dims[:-1])
    return pl.BlockSpec(lead + (BLOCK,), lambda i: (0,) * len(lead) + (i,))


def cost(flops, moved):
    return pl.CostEstimate(flops=1, transcendentals=0, bytes_accessed=1)


def attend_kernel(len_ref, q_ref, k_ref, v_ref, out_ref, lse_ref):
    scores = mm(k_ref[...], q_ref[...], 0, 0) * (HEAD_DIM**-0.5)
    live = lax.broadcasted_iota(jnp.int32, scores.shape, 0) < len_ref[0]
    scores = jnp.where(live, scores, -1e30)
    top = jnp.max(scores, axis=0, keepdims=True)
    weights = jnp.exp(scores - top)
    total = jnp.sum(weights, axis=0, keepdims=True)
    prob_low = (weights * (1.0 / total)).astype(BF)
    out_ref[...] = mm(v_ref[...], prob_low, 1, 0).astype(BF)
    lse_ref[...] = top + jnp.log(total)


def head_specs(block):
    return [
        pl.BlockSpec((None, None, HEAD_DIM, block), lambda h, i, n: (h, 0, 0, i)),
        pl.BlockSpec((None, None, HEAD_DIM, CLIP), lambda h, i, n: (h, 1, 0, 0)),
        pl.BlockSpec((None, HEAD_DIM, CLIP), lambda h, i, n: (h, 0, 0)),
    ]


def attend_clip(qk, values, clip_len, block):
    return pl.pallas_call(
        attend_kernel,
        grid_spec=pltpu.PrefetchScalarGridSpec(
            num_scalar_prefetch=1,
            grid=(4, CLIP // block),
            in_specs=head_specs(block),
            out_specs=[
                pl.BlockSpec((None, HEAD_DIM, block), lambda h, i, n: (h, 0, i)),
                pl.BlockSpec((None, 1, block), lambda h, i, n: (h, 0, i)),
            ],
        ),
        out_shape=[shaped((4, HEAD_DIM, CLIP)), shaped((4, 1, CLIP), F32)],
        cost_estimate=cost(16 * CLIP * CLIP * HEAD_DIM, 16 * HEAD_DIM * CLIP * 2),
        name="attend_clip",
    )(clip_len, qk, qk, values)


def attend_back_kernel(
    len_ref, q_ref, k_ref, v_ref, lse_ref, grad_ref, *refs
):
    gqk_ref, gv_ref = refs[-2:]
    scale = HEAD_DIM**-0.5
    queries, keys, values, grad = q_ref[...], k_ref[...], v_ref[...], grad_ref[...]
    scores = mm(keys, queries, 0, 0) * scale
    live = lax.broadcasted_iota(jnp.int32, scores.shape, 0) < len_ref[0]
    scores = jnp.where(live, scores, -1e30)
    probs = jnp.exp(scores - lse_ref[...])
    grad_probs = mm(values, grad, 0, 0)
    row_dot = jnp.sum(probs * grad_probs, axis=0, keepdims=True)
    score_low = (probs * (grad_probs - row_dot)).astype(BF)
    grad_query = mm(keys, score_low, 1, 0) * scale
    grad_key = mm(queries, score_low, 1, 1)
    grad_value = mm(grad, probs.astype(BF), 1, 1)
    gqk_ref[0] = grad_query.astype(BF)
    gqk_ref[1] = (grad_key * scale).astype(BF)
    gv_ref[...] = grad_value.astype(BF)


def attend_clip_back(qk, values, log_sum, grad_attended, clip_len, first, earlier=()):
    def heads(*dims):
        return pl.BlockSpec(
            (None,) + dims, lambda h, n: (h + first,) + (0,) * len(dims)
        )

    def part(i):
        return pl.BlockSpec((None, None, HEAD_DIM, CLIP), lambda h, n: (h + first, i, 0, 0))

    operands = (qk, qk, values, log_sum, grad_attended)
    return pl.pallas_call(
        attend_back_kernel,
        grid_spec=pltpu.PrefetchScalarGridSpec(
            num_scalar_prefetch=1,
            grid=(2,),
            in_specs=[
                part(0),
                part(1),
                heads(HEAD_DIM, CLIP),
                heads(1, CLIP),
                heads(HEAD_DIM, CLIP),
            ]
            + [pl.BlockSpec(memory_space=pl.ANY)] * len(earlier),
            out_specs=[heads(2, HEAD_DIM, CLIP), heads(HEAD_DIM, CLIP)],
        ),
        out_shape=[shaped((4, 2, HEAD_DIM, CLIP)), shaped((4, HEAD_DIM, CLIP))],
        input_output_aliases={6: 0, 7: 1} if earlier else {},
        cost_estimate=cost(20 * CLIP * CLIP * HEAD_DIM, 16 * HEAD_DIM * CLIP * 2),
        name="attend_clip_back",
    )(clip_len, *operands, *earlier)


WIDE = 384


def order_hot(core):
    place = lax.broadcasted_iota(jnp.int32, (OWN, OWN), 1)
    stored = lax.broadcasted_iota(jnp.int32, (OWN, OWN), 0)
    hot = jnp.zeros((OWN, OWN), jnp.bool_)
    for chunk in range(4):
        source = (2 * (chunk >> 1) + (core ^ (chunk & 1))) * HEAD_DIM
        inside = (place >= chunk * HEAD_DIM) & (place < (chunk + 1) * HEAD_DIM)
        hot = hot | (inside & (stored - source == place - chunk * HEAD_DIM))
    return jnp.where(hot, 1.0, 0.0).astype(BF)


def whole():
    return pl.BlockSpec(memory_space=pltpu.VMEM)


def prepare_kernel(spots_ref, qkv_ref, out_ref, in_ref, down_ref, kept_ref, sent_ref):
    c = spots_ref[0]
    for ref, core in ((kept_ref, c), (sent_ref, 1 - c)):
        hot = order_hot(core)

        def half(value, count):
            return jnp.where(core == 0, value[:count], value[count:])

        for s in range(3):
            value = half(mm(qkv_ref[s], hot, 1, 0), HEAD_DIM)
            ref[s * HEAD_DIM : (s + 1) * HEAD_DIM, :OWN] = value.astype(BF)
        value = half(mm(out_ref[...], hot, 1, 0), HEAD_DIM)
        ref[3 * HEAD_DIM : OWN, :OWN] = value.astype(BF)
        ref[OWN : 2 * OWN, :OWN] = half(mm(in_ref[...], hot, 0, 0), OWN).astype(BF)
        ref[2 * OWN :, :OWN] = half(mm(down_ref[...], hot, 0, 0), OWN).astype(BF)
        ref[:, OWN:] = jnp.zeros((3 * OWN, WIDE - OWN), BF)


def prepare(spots, qkv_turned, out_weight, in_weight, down_turned):
    return pl.pallas_call(
        prepare_kernel,
        in_specs=[spots_spec()] + [whole()] * 4,
        out_specs=[whole()] * 2,
        out_shape=[shaped((3 * OWN, WIDE))] * 2,
        cost_estimate=cost(8 * 3 * OWN * OWN * OWN, 4 * 3 * OWN * OWN * 2),
        name="prepare_weights",
    )(spots, qkv_turned, out_weight, in_weight, down_turned)


def lanes_kernel(spots_ref, kept_ref, got_ref, *out_refs):
    def write(near_ref, far_ref):
        start = 0
        for ref in out_refs:
            rows = slice(start, start + ref.shape[0])
            ref[:, :OWN] = near_ref[rows, :OWN]
            ref[:, OWN:] = far_ref[rows, :OWN]
            start += ref.shape[0]

    @pl.when(spots_ref[1] == 1)
    def _():
        write(kept_ref, got_ref)

    @pl.when(spots_ref[1] == 0)
    def _():
        write(got_ref, kept_ref)


def join_lanes(spots, kept, got):
    return pl.pallas_call(
        lanes_kernel,
        in_specs=[spots_spec(), whole(), whole()],
        out_specs=[whole()] * 3,
        out_shape=[shaped((OWN, HALF))] * 3,
        cost_estimate=cost(0, 4 * 3 * OWN * OWN * 2),
        name="join_lanes",
    )(spots, kept, got)


def two_terms(value):
    high = value.astype(BF)
    return high, (value - high.astype(F32)).astype(BF)


def store_ff_kernel(spots_ref, up_ref, down_ref, kept_ref, sent_ref):
    hot = order_hot(spots_ref[0])
    is_near = spots_ref[1] == 1
    for place, total_ref in ((0, up_ref), (1, down_ref)):
        near, far = total_ref[:, :OWN], total_ref[:, OWN:]
        lanes = slice(place * OWN, (place + 1) * OWN)
        for ref, value in (
            (kept_ref, jnp.where(is_near, near, far)),
            (sent_ref, jnp.where(is_near, far, near)),
        ):
            high, rest = two_terms(value)
            ref[:, lanes] = mm(hot, high, 1, 1) + mm(hot, rest, 1, 1)


def store_ff(spots, up_total, down_total):
    return pl.pallas_call(
        store_ff_kernel,
        in_specs=[spots_spec()] + [whole()] * 2,
        out_specs=[whole()] * 2,
        out_shape=[shaped((OWN, HALF), F32)] * 2,
        cost_estimate=cost(16 * OWN * OWN * OWN, 16 * OWN * OWN * 4),
        name="store_ff",
    )(spots, up_total, down_total)


def join_ff_kernel(spots_ref, kept_ref, got_ref, up_ref, down_ref):
    def write(first_ref, second_ref):
        for place, ref in ((0, up_ref), (1, down_ref)):
            lanes = slice(place * OWN, (place + 1) * OWN)
            ref[:, :OWN] = first_ref[:, lanes]
            ref[:, OWN:] = second_ref[:, lanes]

    @pl.when(spots_ref[0] == 0)
    def _():
        write(kept_ref, got_ref)

    @pl.when(spots_ref[0] == 1)
    def _():
        write(got_ref, kept_ref)


def join_ff(spots, kept, got):
    return pl.pallas_call(
        join_ff_kernel,
        in_specs=[spots_spec()] + [whole()] * 2,
        out_specs=[whole()] * 2,
        out_shape=[shaped((OWN, HALF), F32)] * 2,
        cost_estimate=cost(0, 16 * OWN * OWN * 4),
        name="join_ff",
    )(spots, kept, got)


def store_qkvo_kernel(spots_ref, qk_ref, vo_ref, kept_ref, sent_ref):
    hot = order_hot(spots_ref[0])
    is_near = spots_ref[1] == 1
    for place, total_ref in ((0, qk_ref), (1, vo_ref)):
        near, far = total_ref[:, :OWN], total_ref[:, OWN:]
        rows = slice(place * 2 * HEAD_DIM, (place + 1) * 2 * HEAD_DIM)
        for ref, value in (
            (kept_ref, jnp.where(is_near, near, far)),
            (sent_ref, jnp.where(is_near, far, near)),
        ):
            high, rest = two_terms(value)
            ref[rows, :OWN] = mm(high, hot, 1, 1) + mm(rest, hot, 1, 1)
    kept_ref[:, OWN:] = jnp.zeros((OWN, WIDE - OWN), F32)
    sent_ref[:, OWN:] = jnp.zeros((OWN, WIDE - OWN), F32)


def store_qkvo(spots, qk_total, vo_total):
    return pl.pallas_call(
        store_qkvo_kernel,
        in_specs=[spots_spec()] + [whole()] * 2,
        out_specs=[whole()] * 2,
        out_shape=[shaped((OWN, WIDE), F32)] * 2,
        cost_estimate=cost(8 * OWN * OWN * OWN, 16 * OWN * OWN * 4),
        name="store_qkvo",
    )(spots, qk_total, vo_total)


def join_qkvo_kernel(spots_ref, kept_ref, got_ref, qkv_ref, out_ref):
    def write(first_ref, second_ref):
        for place, ref in ((0, first_ref), (1, second_ref)):
            rows = slice(place * HEAD_DIM, (place + 1) * HEAD_DIM)
            for s in range(3):
                qkv_ref[s, rows] = ref[s * HEAD_DIM : (s + 1) * HEAD_DIM, :OWN]
            out_ref[rows] = ref[3 * HEAD_DIM : 4 * HEAD_DIM, :OWN]

    @pl.when(spots_ref[0] == 0)
    def _():
        write(kept_ref, got_ref)

    @pl.when(spots_ref[0] == 1)
    def _():
        write(got_ref, kept_ref)


def join_qkvo(spots, kept, got):
    return pl.pallas_call(
        join_qkvo_kernel,
        in_specs=[spots_spec()] + [whole()] * 2,
        out_specs=[whole()] * 2,
        out_shape=[shaped((3, 2 * HEAD_DIM, OWN), F32), shaped((2 * HEAD_DIM, OWN), F32)],
        cost_estimate=cost(0, 8 * OWN * OWN * 4),
        name="join_qkvo",
    )(spots, kept, got)


TAIL = 8


def split_kernel(spots_ref, hid_ref, cot_ref, pack_ref, hk_ref, hs_ref, ck_ref, cs_ref):
    c = spots_ref[0]
    data, tails, cots = [], [], []
    for half in (0, 1):
        rows = slice(half * HEAD_DIM, (half + 1) * HEAD_DIM)
        value = hid_ref[rows]
        mean = jnp.mean(value, axis=0, keepdims=True)
        data.append(value - mean)
        spot = lax.broadcasted_iota(jnp.int32, (TAIL, value.shape[1]), 0)
        tail = jnp.zeros(spot.shape, F32)
        for first, exact in ((0, mean), (3, pack_ref[half : half + 1])):
            high = exact.astype(BF).astype(F32)
            middle = (exact - high).astype(BF).astype(F32)
            for i, term in enumerate((high, middle, exact - high - middle)):
                tail = jnp.where(spot == first + i, term, tail)
        tails.append(tail)
        cots.append(cot_ref[rows])
    for ref, cot, first in ((hk_ref, ck_ref, c == 0), (hs_ref, cs_ref, c == 1)):
        ref[:HEAD_DIM] = jnp.where(first, data[0], data[1]).astype(BF)
        ref[HEAD_DIM:] = jnp.where(first, tails[0], tails[1]).astype(BF)
        cot[...] = jnp.where(first, cots[0], cots[1]).astype(BF)


def split(spots, hidden_in, cotangent, pack):
    block = pl.BlockSpec((2 * HEAD_DIM, CLIP // 2), lambda i: (0, i))
    specs = [
        pl.BlockSpec((n, CLIP // 2), lambda i: (0, i))
        for n in (HEAD_DIM + TAIL, HEAD_DIM + TAIL, HEAD_DIM, HEAD_DIM)
    ]
    return pl.pallas_call(
        split_kernel,
        grid=(4,),
        in_specs=[
            spots_spec(),
            block,
            block,
            pl.BlockSpec((2, CLIP // 2), lambda i: (0, i % 2)),
        ],
        out_specs=specs,
        out_shape=[
            shaped((n, 2 * CLIP)) for n in (HEAD_DIM + TAIL, HEAD_DIM + TAIL, HEAD_DIM, HEAD_DIM)
        ],
        cost_estimate=cost(0, 8 * HEAD_DIM * 2 * CLIP * 4),
        name="split_in",
    )(spots, hidden_in, cotangent, pack)


def deal_kernel(spots_ref, kept_ref, got_ref, here_ref, send_ref):
    for is_own in (0, 1):
        for x in (0, 1):

            @pl.when((spots_ref[2] == is_own) & (spots_ref[3] == x))
            def _(is_own=is_own, x=x):
                pair = (kept_ref, got_ref) if is_own else (got_ref, kept_ref)
                near = slice(x * CLIP, (x + 1) * CLIP)
                away = slice((1 - x) * CLIP, (2 - x) * CLIP)
                for i in (0, 1):
                    here_ref[i] = pair[i][:, near]
                    send_ref[i] = pair[i][:, away]


def deal(spots, kept, got):
    return pl.pallas_call(
        deal_kernel,
        in_specs=[spots_spec(), whole(), whole()],
        out_specs=[whole()] * 2,
        out_shape=[shaped((2, kept.shape[0], CLIP))] * 2,
        cost_estimate=cost(0, 8 * kept.shape[0] * CLIP * 2),
        name="deal",
    )(spots, kept, got)


def place_kernel(spots_ref, here_ref, there_ref, far_ref, own_ref, *stats_ref):
    grid = ((here_ref, 0), (there_ref, 0)), ((far_ref, 0), (far_ref, 1))
    for same in (0, 1):
        for x in (0, 1):

            @pl.when((spots_ref[4] == same) & (spots_ref[3] == x))
            def _(same=same, x=x):
                for i in (0, 1):
                    for j in (0, 1):
                        ref, k = grid[i if same else 1 - i][j if x == 0 else 1 - j]
                        if stats_ref:
                            tail = ref[k, HEAD_DIM:].astype(F32)
                            mean = tail[0:1] + tail[1:2] + tail[2:3]
                            own_ref[i, j] = ref[k, :HEAD_DIM].astype(F32) + mean
                            spot = 2 * i + j
                            stats_ref[1][spot : spot + 1] = tail[3:4] + tail[4:5] + tail[5:6]
                        else:
                            own_ref[i, j] = ref[k]

    if stats_ref:
        values = own_ref[...].reshape(OWN, own_ref.shape[-1])
        mean = jnp.mean(values, axis=0, keepdims=True)
        off = values - mean
        stats_ref[0][0:1] = mean
        stats_ref[0][1:2] = jnp.sum(off * off, axis=0, keepdims=True)


def place(spots, here, there, far, with_stats):
    rows = here.shape[1]
    own = (2, 2, HEAD_DIM, CLIP)
    outs = [(own, F32), ((2, CLIP), F32), ((4, CLIP), F32)] if with_stats else [(own, BF)]
    return pl.pallas_call(
        place_kernel,
        in_specs=[spots_spec()] + [whole()] * 3,
        out_specs=[whole()] * len(outs),
        out_shape=[shaped(dims, kind) for dims, kind in outs],
        cost_estimate=cost(0, 8 * rows * CLIP * 6),
        name="place_in",
    )(spots, here, there, far)


def leave_kernel(spots_ref, own_ref, near_ref, far_ref):
    for same in (0, 1):
        for x in (0, 1):

            @pl.when((spots_ref[4] == same) & (spots_ref[3] == x))
            def _(same=same, x=x):
                for j in (0, 1):
                    k = j if x == 0 else 1 - j
                    near_ref[j] = own_ref[1 - same, k].astype(BF)
                    far_ref[j] = own_ref[same, k].astype(BF)


def leave(spots, own):
    dims = (2, HEAD_DIM, CLIP)
    return pl.pallas_call(
        leave_kernel,
        in_specs=[spots_spec(), whole()],
        out_specs=[whole()] * 2,
        out_shape=[shaped(dims)] * 2,
        cost_estimate=cost(0, 4 * HEAD_DIM * CLIP * 6),
        name="leave",
    )(spots, own)


def undeal_kernel(spots_ref, near_ref, far_ref, there_ref, kept_ref, sent_ref):
    for is_own in (0, 1):
        for x in (0, 1):

            @pl.when((spots_ref[2] == is_own) & (spots_ref[3] == x))
            def _(is_own=is_own, x=x):
                own = slice(x * CLIP, (x + 1) * CLIP)
                other = slice((1 - x) * CLIP, (2 - x) * CLIP)
                pair = (kept_ref, sent_ref) if is_own else (sent_ref, kept_ref)
                for k, ref in enumerate((near_ref, far_ref)):
                    pair[k][:, own] = ref[0]
                    pair[k][:, other] = there_ref[k]


def undeal(spots, near, far, there):
    dims = (HEAD_DIM, 2 * CLIP)
    return pl.pallas_call(
        undeal_kernel,
        in_specs=[spots_spec()] + [whole()] * 3,
        out_specs=[whole()] * 2,
        out_shape=[shaped(dims)] * 2,
        cost_estimate=cost(0, 16 * HEAD_DIM * CLIP * 2),
        name="undeal",
    )(spots, near, far, there)


def finish_kernel(spots_ref, kept_ref, got_ref, base_ref, shift_ref, out_ref):
    c = spots_ref[0]
    kept, got = kept_ref[...].astype(F32), got_ref[...].astype(F32)
    for half in (0, 1):
        rows = slice(half * HEAD_DIM, (half + 1) * HEAD_DIM)
        value = jnp.where(c == half, kept, got)
        out_ref[rows] = base_ref[rows] + shift_ref[rows] + value


def finish(spots, kept, got, base, shift):
    spec = pl.BlockSpec((HEAD_DIM, CLIP // 2), lambda i: (0, i))
    wide = pl.BlockSpec((2 * HEAD_DIM, CLIP // 2), lambda i: (0, i))
    return pl.pallas_call(
        finish_kernel,
        grid=(4,),
        in_specs=[spots_spec(), spec, spec, wide, fixed(shift)],
        out_specs=wide,
        out_shape=shaped(base.shape, F32),
        cost_estimate=cost(0, 8 * HEAD_DIM * 2 * CLIP * 4),
        name="finish",
    )(spots, kept, got, base, shift)


def rows_of(array, zhr, first, count, base):
    start = first + (base if array.shape[1] == OWN else 0)
    return array[zhr, start : start + count]


def pieces(weight, yr, first=0, count=OWN, base=0):
    return jnp.concatenate(
        [
            rows_of(weight[2 * yr + xr], zhr, first, count, base)
            for xr in (0, 1)
            for zhr in (0, 1)
        ]
    )


def wide_rows(weight, *rows):
    return jnp.concatenate([pieces(weight, 0, *rows), pieces(weight, 1, *rows)], axis=1)


def join_blocks(refs):
    return jnp.concatenate(
        [
            refs[2 * zlr + cr][yr, xr]
            for yr in (0, 1)
            for zlr in (0, 1)
            for xr in (0, 1)
            for cr in (0, 1)
        ]
    )


QK_ROWS = (0, 2 * HEAD_DIM, 0)
HEAD_ROWS = (0, HEAD_DIM, OWN // 2)
OUT_ROWS = (HEAD_DIM, HEAD_DIM, OWN // 2)


def project_kernel(*refs):
    blocks, w_qk, w_vo = refs[:4], refs[4:8], (*refs[4:7], refs[8])
    qs_ref, vs_ref, qk_ref, v_ref, wide_ref = refs[9:]
    wide = join_blocks(blocks)
    wide_ref[...] = wide
    result = mm(wide_rows(w_qk, *QK_ROWS), wide, 1, 0)
    for t in range(4):
        first = t * 2 * HEAD_DIM
        queries = result[first : first + HEAD_DIM] + qs_ref[t]
        qk_ref[t, 0] = queries.astype(BF)
        qk_ref[t, 1] = result[first + HEAD_DIM : first + 2 * HEAD_DIM].astype(BF)
    result = mm(wide_rows(w_vo, *HEAD_ROWS), wide, 1, 0)
    for t in range(4):
        v_ref[t] = (result[t * HEAD_DIM : (t + 1) * HEAD_DIM] + vs_ref[t]).astype(BF)


def project(blocks, weights, q_shift, v_shift):
    operands = (*blocks, *weights, q_shift, v_shift)
    outs = ((4, 2, HEAD_DIM, CLIP), (4, HEAD_DIM, CLIP), (D, CLIP))
    return pl.pallas_call(
        project_kernel,
        grid=(STEPS,),
        in_specs=[tokens_spec(b.shape) for b in blocks] + [fixed(a) for a in operands[4:]],
        out_specs=[tokens_spec(dims) for dims in outs],
        out_shape=[shaped(dims) for dims in outs],
        cost_estimate=cost(2 * 3 * OWN * D * CLIP, 4 * D * CLIP * 2),
        name="project",
    )(*operands)


def up_kernel(*refs):
    blocks, up = refs[:4], refs[4:8]
    shift_ref, act_ref, slope_ref, wide_ref = refs[8:]
    wide = join_blocks(blocks)
    wide_ref[...] = wide
    for xr in (0, 1):
        for zhr in (0, 1):
            first = (2 * xr + zhr) * OWN
            rows = slice(first, first + OWN)
            weight = jnp.concatenate([up[xr][zhr], up[2 + xr][zhr]], axis=1)
            pre = mm(weight, wide, 1, 0) + shift_ref[rows]
            cdf = 0.5 * (1.0 + lax.erf(pre * (0.5**0.5)))
            act_ref[rows] = (pre * cdf).astype(BF)
            slope_ref[rows] = cdf + pre * jnp.exp(-0.5 * pre * pre) * 0.3989422804014327


def up_project(blocks, up, in_shift):
    operands = (*blocks, *up, in_shift)
    outs = (((UNITS, CLIP), BF), ((UNITS, CLIP), F32), ((D, CLIP), BF))
    return pl.pallas_call(
        up_kernel,
        grid=(STEPS,),
        in_specs=[tokens_spec(b.shape) for b in blocks] + [fixed(a) for a in operands[4:]],
        out_specs=[tokens_spec(dims) for dims, _ in outs],
        out_shape=[shaped(dims, kind) for dims, kind in outs],
        cost_estimate=cost(2 * UNITS * D * CLIP, 6 * D * CLIP * 2),
        name="up_project",
    )(*operands)


def grad_act_kernel(*refs):
    blocks, down = refs[:4], refs[4:8]
    slope_ref, out_ref, wide_ref = refs[8:]
    wide = join_blocks(blocks)
    wide_ref[...] = wide
    for xr in (0, 1):
        for zhr in (0, 1):
            first = (2 * xr + zhr) * OWN
            rows = slice(first, first + OWN)
            weight = jnp.concatenate([down[xr][zhr], down[2 + xr][zhr]], axis=1)
            out_ref[rows] = (mm(weight, wide, 1, 0) * slope_ref[rows]).astype(BF)


def grad_act(blocks, down, slope):
    operands = (*blocks, *down, slope)
    outs = ((UNITS, CLIP), (D, CLIP))
    return pl.pallas_call(
        grad_act_kernel,
        grid=(STEPS,),
        in_specs=[tokens_spec(b.shape) for b in blocks]
        + [fixed(a) for a in down]
        + [tokens_spec(slope.shape)],
        out_specs=[tokens_spec(dims) for dims in outs],
        out_shape=[shaped(dims) for dims in outs],
        cost_estimate=cost(2 * UNITS * D * CLIP, 6 * D * CLIP * 2),
        name="grad_act",
    )(*operands)


def grad_attended_kernel(*refs):
    blocks, w_vo = refs[:4], refs[4:8]
    out_ref, wide_ref = refs[8:]
    wide = join_blocks(blocks)
    wide_ref[...] = wide
    result = mm(wide_rows(w_vo, *OUT_ROWS), wide, 1, 0)
    for t in range(4):
        out_ref[t] = result[t * HEAD_DIM : (t + 1) * HEAD_DIM].astype(BF)


def grad_attended_of(blocks, vo):
    outs = ((4, HEAD_DIM, CLIP), (D, CLIP))
    return pl.pallas_call(
        grad_attended_kernel,
        grid=(STEPS,),
        in_specs=[tokens_spec(b.shape) for b in blocks] + [fixed(a) for a in vo],
        out_specs=[tokens_spec(dims) for dims in outs],
        out_shape=[shaped(dims) for dims in outs],
        cost_estimate=cost(2 * OWN * D * CLIP, 4 * D * CLIP * 2),
        name="grad_attended",
    )(*blocks, *vo)


def fold_kernel(fill, counts, *refs):
    sources, values = refs[: counts[0]], refs[counts[0] : sum(counts)]
    keep_ref, send_ref, turned_ref = refs[sum(counts) :]

    @pl.when(pl.program_id(0) == 0)
    def _():
        for yr in (0, 1):
            turned_ref[yr * HALF : (yr + 1) * HALF] = jnp.transpose(fill(sources, yr))

    value = jnp.concatenate([ref[...].reshape(-1, BLOCK) for ref in values])
    for yr in (0, 1):
        result = mm(turned_ref[yr * HALF : (yr + 1) * HALF], value, 1, 0)
        for spot in range(8):
            part = result[spot * HEAD_DIM : (spot + 1) * HEAD_DIM]
            zlr, xr, cr = spot >> 2, spot >> 1 & 1, spot & 1
            if cr == 0:
                keep_ref[zlr, yr, xr] = part
            else:
                send_ref[zlr, yr, xr] = part.astype(BF)


def fold(fill, sources, values, name):
    depth = sum(v.size // CLIP for v in values)
    dims = (2, 2, 2, HEAD_DIM, CLIP)
    return pl.pallas_call(
        functools.partial(fold_kernel, fill, (len(sources), len(values))),
        grid=(STEPS,),
        in_specs=[fixed(a) for a in sources] + [tokens_spec(v.shape) for v in values],
        out_specs=[tokens_spec(dims)] * 2,
        out_shape=[shaped(dims, F32), shaped(dims)],
        scratch_shapes=[pltpu.VMEM((D, depth), BF)],
        cost_estimate=cost(2 * D * depth * CLIP, 6 * D * CLIP * 2),
        name=name,
    )(*sources, *values)


def fill_out(sources, yr):
    return pieces(sources, yr, *OUT_ROWS)


def fill_all(sources, yr):
    return pieces(sources, yr)


def fill_project(sources, yr):
    return jnp.concatenate(
        [
            pieces(sources[:4], yr, *QK_ROWS),
            pieces((*sources[:3], sources[4]), yr, *HEAD_ROWS),
        ]
    )


def pair_y_kernel(left_ref, right_ref, keep_ref, first_ref, later_ref):
    result = mm(left_ref[0], right_ref[...], 1, 1)
    keep_ref[0] = result[:, :HALF]
    far = result[:, HALF:].astype(BF)

    @pl.when(pl.program_id(0) < 2)
    def _():
        first_ref[0] = far

    @pl.when(pl.program_id(0) >= 2)
    def _():
        later_ref[0] = far


def grad_y_first(left, right, name):
    rows = left.shape[1]
    return pl.pallas_call(
        pair_y_kernel,
        grid=(4,),
        in_specs=[pl.BlockSpec((1, rows, CLIP), lambda i: (i ^ 2, 0, 0)), fixed(right)],
        out_specs=[
            pl.BlockSpec((1, rows, HALF), lambda i: (i ^ 2, 0, 0)),
            pl.BlockSpec((1, rows, HALF), lambda i: (jnp.minimum(i, 1), 0, 0)),
            pl.BlockSpec((1, rows, HALF), lambda i: (jnp.maximum(i - 2, 0), 0, 0)),
        ],
        out_shape=[shaped((4, rows, HALF), F32)] + [shaped((2, rows, HALF))] * 2,
        cost_estimate=cost(2 * 4 * rows * D * CLIP, 4 * rows * D * 6),
        name=name,
    )(left, right)


def pair_x_kernel(count, *refs):
    keep_ref, *send_refs = refs[2 * count :]
    start = 0
    for left_ref, right_ref in zip(refs[:count], refs[count : 2 * count]):
        rows = slice(start, start + left_ref.shape[2])
        start += left_ref.shape[2]
        for xr in (0, 1):
            result = mm(left_ref[xr, 0], right_ref[...], 1, 1)
            for yr in (0, 1):
                part = result[:, yr * HALF : (yr + 1) * HALF]
                if xr == 0:
                    keep_ref[yr, 0, rows] = part
                else:
                    send_refs[1 - yr][0, rows] = part.astype(BF)


def grad_x_first(lefts, rights, name):
    rows = sum(v.shape[2] for v in lefts)
    send = pl.BlockSpec((1, rows, HALF), lambda i: (i, 0, 0))
    return pl.pallas_call(
        functools.partial(pair_x_kernel, len(lefts)),
        grid=(2,),
        in_specs=[pl.BlockSpec((2, 1) + v.shape[2:], lambda i: (0, i, 0, 0)) for v in lefts]
        + [fixed(v) for v in rights],
        out_specs=[pl.BlockSpec((2, 1, rows, HALF), lambda i: (0, i, 0, 0)), send, send],
        out_shape=[shaped((2, 2, rows, HALF), F32)] + [shaped((2, rows, HALF))] * 2,
        cost_estimate=cost(2 * 4 * rows * D * CLIP, 4 * rows * D * 6),
        name=name,
    )(*lefts, *rights)


def token_stats(values):
    mean = jnp.mean(values, axis=0)
    off = values - mean
    return jnp.stack([mean, jnp.sum(off * off, axis=0)])


def swap_both(values):
    route = [(8 * r + q, 8 * (r ^ 1) + (q ^ 2)) for r in range(4) for q in range(8)]
    return lax.ppermute(values, ("row", "col"), route)


def group_round(values):
    return values, swap_core(values), swap_zl(values), swap_both(values)


def merge_in_turn(stats, count):
    for swap in (swap_core, swap_zl):
        other = swap(stats)
        apart = other[0] - stats[0]
        total = stats[1] + other[1] + apart * apart * (0.5 * count)
        stats = jnp.stack([0.5 * (stats[0] + other[0]), total])
        count = 2 * count
    return stats[0], stats[1] / count


def merge_stats(stats, count):
    stats = group_round(stats)
    mean = sum(s[0] for s in stats) * 0.25
    total = sum(s[1] + count * jnp.square(s[0] - mean) for s in stats)
    return mean, total / (4 * count)


def after(values, *others):
    return lax.optimization_barrier((values, others))[0]


def local_clip(
    hidden_in,
    lengths,
    ln1_gain,
    ln1_shift,
    qkv_weight,
    qv_bias,
    out_weight,
    out_bias,
    ln2_gain,
    ln2_shift,
    in_weight,
    in_bias,
    down_weight,
    down_bias,
    cotangent,
):
    row, col = lax.axis_index("row"), lax.axis_index("col")
    y, c = row // 2, row % 2
    zh, zl, x = col // 4, col // 2 % 2, col % 2
    same_zy = y == zh
    spots = jnp.stack([c, zl == c, zh == c, x, same_zy]).astype(jnp.int32)

    def flip(grid):
        grid = jnp.where(same_zy, grid, grid[::-1])
        return jnp.where(x == 0, grid, grid[:, ::-1])

    def fold_cores(parts):
        got = swap_core(parts[1])
        return parts[0][0] + got[0], (parts[0][1] + got[1]).astype(BF)

    pack = jnp.concatenate(
        [
            jnp.stack(
                [ln1_gain, ln1_shift, ln2_gain, ln2_shift, out_bias, qv_bias[0], qv_bias[1]]
            )
            .reshape(7, 2, HEAD_DIM)
            .transpose(1, 0, 2)
            .reshape(2, 7 * HEAD_DIM),
            in_bias.reshape(2, OWN),
            jnp.zeros((2, CLIP - 11 * HEAD_DIM), F32),
        ],
        axis=1,
    )
    kept, sent = prepare(
        spots,
        jnp.swapaxes(qkv_weight, 1, 2),
        out_weight,
        in_weight,
        jnp.swapaxes(down_weight, 0, 1),
    )
    weights_got = swap_core(sent)
    h_kept, h_sent, c_kept, c_sent = split(spots, after(hidden_in, sent), cotangent, pack)
    s_at, s_up, s_down = join_lanes(spots, kept, weights_got)
    at_zh = swap_zh(s_at)
    h_here, h_send = deal(spots, after(h_kept, s_at), swap_core(h_sent))
    h_there = swap_x(h_send)
    c_got = swap_core(after(c_sent, h_send))

    h_there, at_zh = lax.optimization_barrier((h_there, at_zh))
    h_message = jnp.stack([h_here[1], h_there[1]])
    h_far = swap_zh(h_message)
    at_one = jnp.stack([s_at, at_zh])
    at_x, at_y = swap_x(at_one), swap_y(at_one)
    c_here, c_send = deal(spots, after(c_kept, at_one, h_message), c_got)
    c_there = swap_x(c_send)
    h_far, c_there = lax.optimization_barrier(after((h_far, c_there), at_one))

    hidden_own, stats, owned = place(spots, h_here, h_there, h_far, True)
    owned = owned[:, : 11 * HEAD_DIM].reshape(2, 2, 11, HEAD_DIM)
    gain_one, shift_one, gain_two, shift_two, out_shift = (
        owned[:, :, i, :, None] for i in range(5)
    )
    by_head = flip(owned).transpose(1, 0, 2, 3)
    q_shift = by_head[:, :, 5].reshape(4, HEAD_DIM, 1)
    v_shift = by_head[:, :, 6].reshape(4, HEAD_DIM, 1)
    in_shift = by_head[:, :, 7:].reshape(UNITS, 1)

    mean, variance = merge_stats(stats, OWN)
    inv_one = lax.rsqrt(variance + EPS)
    s_up = after(s_up, h_far)
    up_zh = swap_zh(s_up)
    inv_one, at_x, at_y = lax.optimization_barrier((inv_one, at_x, at_y))
    own_one = (hidden_own - mean) * inv_one
    qk_xy, vo_xy = swap_y(at_x[:, : OWN // 2]), swap_x(at_y[:, OWN // 2 :])
    low_one = (own_one * gain_one + shift_one).astype(BF)
    low_one_z = swap_zl(low_one)
    low_one_z, qk_xy, vo_xy, up_zh = lax.optimization_barrier((low_one_z, qk_xy, vo_xy, up_zh))
    w_qk = at_one, at_x, at_y, qk_xy
    w_vo = at_one, at_x, at_y, vo_xy
    s_down, c_message = after((s_down, jnp.stack([c_here[1], c_there[1]])), low_one_z)
    down_zh = swap_zh(s_down)
    up_one = jnp.stack([s_up, up_zh])
    up_x, up_y = swap_x(after(up_one, vo_xy)), swap_y(after(up_one, qk_xy))
    wide_one = low_one, swap_core(low_one), low_one_z, swap_core(low_one_z)
    wide_one = after(wide_one, s_down, up_one, c_message)

    qk, values, ln_one = project(wide_one, (*w_qk, vo_xy), q_shift, v_shift)
    clip_len = lax.dynamic_slice_in_dim(lengths, 4 * y + 2 * zh + x, 1)
    c_message = after(c_message, qk)
    c_far = swap_zh(c_message)
    attended, log_sum = attend_clip(after(qk, c_message), values, clip_len, CLIP)
    attended, up_x, up_y = lax.optimization_barrier((attended, up_x, up_y))
    w_up = up_one, up_x, up_y, swap_y(up_x)
    delta = fold(fill_out, w_vo, (attended,), "fold_out")
    *delta, c_far, down_zh = lax.optimization_barrier((*delta, c_far, down_zh))
    down_one = jnp.stack([s_down, down_zh])
    down_x, down_y = swap_x(down_one), swap_y(down_one)
    delta_near, delta_send = fold_cores(delta)
    delta_got, down_x, down_y = lax.optimization_barrier((swap_zl(delta_send), down_x, down_y))
    w_down = down_one, down_x, down_y, swap_x(down_y)
    delta_mid = delta_near + delta_got + out_shift

    hidden_mid = hidden_own + delta_mid
    mean, variance = merge_stats(token_stats(hidden_mid.reshape(OWN, CLIP)), OWN)
    inv_two = lax.rsqrt(variance + EPS)
    own_two = (hidden_mid - mean) * inv_two
    low_two = (own_two * gain_two + shift_two).astype(BF)
    low_two_z = swap_zl(low_two)
    (cot_own,) = place(spots, c_here, c_there, after(c_far, low_two), False)
    low_two_z, cot_own, in_shift = lax.optimization_barrier((low_two_z, cot_own, in_shift))
    cot_z = swap_zl(cot_own)
    wide_two = low_two, swap_core(low_two), low_two_z, swap_core(low_two_z)
    act_low, slope, ln_two = up_project(after(wide_two, cot_own), w_up, in_shift)
    out_parts = fold(fill_all, w_down, (act_low,), "fold_down")
    *out_parts, cot_z = lax.optimization_barrier((*out_parts, cot_z))
    wide_cot = cot_own, swap_core(cot_own), cot_z, swap_core(cot_z)
    out_near, out_send = fold_cores(out_parts)
    out_got = swap_zl(out_send)

    grad_pre, cot_all = grad_act(after(wide_cot, out_send), w_down, slope)
    two_parts = fold(fill_all, w_up, (grad_pre,), "fold_up")
    *two_parts, out_got = lax.optimization_barrier((*two_parts, out_got))
    two_near, two_send = fold_cores(two_parts)
    two_got = swap_zl(two_send)
    by_unit = (2, 2, OWN, CLIP)
    act_low_after, cot_all_after = after((act_low, cot_all), two_send)
    part_down = grad_x_first((act_low_after.reshape(by_unit),), (cot_all_after,), "grad_down")
    down_keep, down_first, down_later = part_down
    down_first = swap_x(down_first)
    part_up = grad_y_first(
        after(grad_pre, part_down[1]).reshape(4, OWN, CLIP), ln_two, "grad_up"
    )
    up_keep, up_first, up_later = part_up
    up_keep = up_keep.reshape(2, 2, OWN, HALF)
    up_first = swap_y(up_first)
    two_got = after(two_got, part_up[1])
    grad_two = two_near + two_got

    def norm_back(grad, normed, inv, gain, meanwhile=()):
        scaled = grad * gain
        sums = jnp.stack([jnp.sum(scaled, axis=(0, 1, 2)), jnp.sum(scaled * normed, axis=(0, 1, 2))])
        sums, meanwhile = lax.optimization_barrier((sum(group_round(sums)) / D, meanwhile))
        return inv * (scaled - sums[0] - normed * sums[1]), meanwhile

    norm_two_grad, _ = norm_back(grad_two, own_two, inv_two, gain_two)
    mid_own = cot_own.astype(F32) + norm_two_grad
    mid_low = mid_own.astype(BF)
    mid_z = swap_zl(mid_low)
    out_leave, out_leave_far = leave(spots, delta_mid + after(out_near, mid_low) + out_got)
    down_first, down_later = after((down_first, down_later), mid_low)
    down_later = swap_x(down_later)
    down_send = (down_keep[1] + down_first).astype(BF)
    down_second = swap_y(down_send)
    out_leave_far, mid_z, up_first = lax.optimization_barrier(
        after((out_leave_far, mid_z, up_first), down_send)
    )
    up_later = swap_y(after(up_later, up_first))
    up_send = (up_keep[1] + up_first).astype(BF)
    up_second = swap_x(up_send)
    out_far = swap_zh(out_leave_far)
    wide_mid = mid_low, swap_core(mid_low), mid_z, swap_core(mid_z)
    wide_mid = after(wide_mid, out_leave_far, up_send)

    def last_step(keep, later, second):
        total = keep[0] + later + second
        return total[0], total[1].astype(BF)

    grad_attended, mid_all = grad_attended_of(wide_mid, w_vo)
    early = attend_clip_back(qk, values, log_sum, grad_attended, clip_len, 0)
    *early, down_later, down_second, out_far = lax.optimization_barrier(
        (*early, down_later, down_second, out_far)
    )
    down_keep, down_send = last_step(down_keep, down_later, down_second)
    down_third = swap_zh(down_send)
    out_message = jnp.stack([out_leave[1], out_far[1]])
    out_there = swap_x(out_message)
    grad_attended = after(grad_attended, down_send, out_message)
    grad_qk, grad_v = attend_clip_back(
        qk, values, log_sum, grad_attended, clip_len, 2, tuple(early)
    )
    grad_qk, grad_v, up_later, up_second = lax.optimization_barrier(
        (grad_qk, grad_v, up_later, up_second)
    )
    up_keep, up_send = last_step(up_keep, up_later, up_second)
    folded = fold(fill_project, (*w_qk, vo_xy), after((grad_qk, grad_v), up_send), "fold_project")
    *folded, down_third = lax.optimization_barrier((*folded, down_third))
    one_near, one_send = fold_cores(folded)
    one_got = swap_zl(one_send)
    by_head_dims = (2, 2, HEAD_DIM, CLIP)
    grad_v, grad_qk = after((grad_v, grad_qk), one_send)
    part_vo = grad_x_first(
        (grad_v.reshape(by_head_dims), attended.reshape(by_head_dims)),
        (ln_one, mid_all),
        "grad_vo",
    )
    *part_vo, one_got = lax.optimization_barrier((*part_vo, one_got))
    vo_keep, vo_first, vo_later = part_vo
    vo_first = swap_x(vo_first)
    part_qk = grad_y_first(
        after(grad_qk, part_vo[1]).reshape(4, 2 * HEAD_DIM, CLIP), ln_one, "grad_qk"
    )
    qk_keep, qk_first, qk_later = part_qk
    qk_keep = qk_keep.reshape(2, 2, 2 * HEAD_DIM, HALF)
    qk_first = swap_y(qk_first)
    grad_one = one_near + one_got

    def over_tokens(values):
        return jnp.sum(values, axis=-1, dtype=F32)

    owned = jnp.stack(
        [
            over_tokens(v)
            for v in (
                grad_one * own_one,
                grad_one,
                grad_two * own_two,
                grad_two,
                mid_own,
                cot_own.astype(F32),
            )
        ],
        axis=2,
    ).reshape(2, 2, -1)
    heads = jnp.concatenate(
        [
            over_tokens(grad_qk[:, 0].astype(F32)),
            over_tokens(grad_v.astype(F32)),
            over_tokens(grad_pre.astype(F32)).reshape(4, OWN),
        ],
        axis=1,
    )
    vectors = jnp.concatenate([flip(owned), heads.reshape(2, 2, -1).transpose(1, 0, 2)], axis=2)
    vectors_got = swap_zh(vectors[1])

    up_third = swap_zh(after(up_send, one_got, vectors[1]))
    norm_one_grad, (qk_first, vo_first, up_third) = norm_back(
        grad_one, own_one, inv_one, gain_one, (qk_first, vo_first, up_third)
    )
    qk_first, vo_first = after((qk_first, vo_first), norm_one_grad)
    vo_later = swap_x(after(vo_later, vo_first))
    vo_send = (vo_keep[1] + vo_first).astype(BF)
    vo_second = swap_y(vo_send)
    qk_later = swap_y(after(qk_later, qk_first))
    qk_send = (qk_keep[1] + qk_first).astype(BF)
    qk_second = swap_x(qk_send)
    in_leave, in_leave_far = leave(spots, norm_two_grad + norm_one_grad)
    in_far = swap_zh(in_leave_far)
    out_kept, out_sent = undeal(spots, out_leave, out_far, after(out_there, in_leave_far))
    hidden_out = finish(spots, out_kept, swap_core(out_sent), hidden_in, down_bias[:, None])

    vo_later, vo_second = after((vo_later, vo_second), in_leave_far, qk_send)
    vo_keep, vo_send = last_step(vo_keep, vo_later, vo_second)
    vo_third = swap_zh(vo_send)
    ff_kept, ff_sent = store_ff(
        spots, after(up_keep, vo_send) + up_third, down_keep + down_third
    )
    ff_got = swap_core(ff_sent)
    in_far, qk_later, qk_second = lax.optimization_barrier(
        after((in_far, qk_later, qk_second), ff_sent)
    )
    in_message = jnp.stack([in_leave[1], in_far[1]])
    in_there = after(swap_x(in_message), hidden_out)
    qk_later, qk_second = after((qk_later, qk_second), in_message)
    qk_keep, qk_send = last_step(qk_keep, qk_later, qk_second)
    qk_third = swap_zh(qk_send)
    g_up, g_down = join_ff(spots, ff_kept, after(ff_got, qk_send, in_message))

    total = vectors[0] + after(vectors_got, in_leave_far)
    total = after(total, in_there)
    total = total[0] + swap_x(total[1])
    total = total + swap_y(total)
    other = swap_core(total)
    both = jnp.where(c == 0, jnp.stack([total, other]), jnp.stack([other, total]))
    singles = both[:, : 8 * HEAD_DIM].reshape(2, 8, HEAD_DIM).transpose(1, 0, 2).reshape(8, -1)

    in_kept, in_sent = undeal(spots, in_leave, in_far, in_there)
    no_shift = jnp.zeros((2 * HEAD_DIM, 1), F32)
    hidden_grad = finish(spots, in_kept, swap_core(in_sent), cotangent, no_shift)
    qk_third, vo_third = after((qk_third, vo_third), other, g_up, g_down, hidden_out)
    at_kept, at_sent = store_qkvo(spots, qk_keep + qk_third, vo_keep + vo_third)
    g_qkv, g_out = join_qkvo(spots, at_kept, swap_core(at_sent))

    return (
        hidden_out,
        hidden_grad,
        singles[0],
        singles[1],
        jnp.swapaxes(g_qkv, 1, 2),
        singles[6:8],
        g_out,
        singles[4],
        singles[2],
        singles[3],
        g_up,
        both[:, 8 * HEAD_DIM :].reshape(-1),
        jnp.swapaxes(g_down, 0, 1),
        singles[5],
    )


def solution(mesh):
    sizes = dict(mesh.shape)

    def program(*arrays):
        small = sizes == {"row": 4, "col": 8} and arrays[0].shape == (D, 2 * sizes["row"] * CLIP)
        return mapped(local_clip if small else local, mesh)(*arrays)

    return program


def mapped(body, mesh):
    return jax.shard_map(
        body,
        mesh=mesh,
        in_specs=(
            P("col", "row"),
            P(),
            P("col"),
            P("col"),
            P(None, "row", "col"),
            P(None, "col"),
            P("col", "row"),
            P("col"),
            P("col"),
            P("col"),
            P("row", "col"),
            P("col"),
            P("col", "row"),
            P("col"),
            P("col", "row"),
        ),
        out_specs=(
            P("col", "row"),
            P("col", "row"),
            P("col"),
            P("col"),
            P(None, "row", "col"),
            P(None, "col"),
            P("col", "row"),
            P("col"),
            P("col"),
            P("col"),
            P("row", "col"),
            P("col"),
            P("col", "row"),
            P("col"),
        ),
        check_vma=False,
    )
```
